512 devices in a mesh: tile: 16 (over y, z_lo), sub: 32 (over z_hi, x, core).
Axes of the slice: x: 4, y: 4, z: 16 (z_hi: 4, z_lo: 4; z = z_hi * 4 + z_lo), core: 2. Of those that a mesh axis runs over, the one named last changes fastest.
Arguments:
- seeds: float32 [16, 6, 64, 256, 128], P('tile', None, 'sub'), may hold values from -6 to 6
- material: int32 [16, 64, 256, 128], P('tile', 'sub'), may hold values from 0 to 3
- decay: float32 [4], replicated, may hold values from 0.5 to 1
- coupling: float32 [4], replicated, may hold values from 0.1 to 0.6
Outputs:
- gradient: float32 [16, 6, 64, 256, 128], P('tile', None, 'sub')
The draws below stay inside these ranges and needn't reach their ends.
All inputs are finite; a program needn't handle non-finite values.
Results may differ from the reference program's by a relative error of at most 0.0003.
Values sent between devices are 32-bit elements; how exact they have to be, the bound alone decides.
A program may use at most 64 MiB of HBM per device.

```python
import math
import jax
import jax.numpy as jnp
from jax import lax

TX = 256
TY = 128
BAND = 32
STEPS = 2
MATERIALS = 4
TILES = 16
Z = 64
N_TILE = 16


def touch_ends(values, rng, least, largest):
    longest = values.shape.index(max(values.shape))
    spots = []
    for shift in (0, 1):
        where = [jax.random.randint(jax.random.fold_in(rng, axis), (), 0, length) for axis, length in enumerate(values.shape)]
        where[longest] = (where[longest] + shift) % values.shape[longest]
        spots.append(tuple(where))
    return values.at[spots[0]].set(least).at[spots[1]].set(largest)


def shard_levels(key, dims, cuts, least, largest):
    level, own = 1.0, jax.random.fold_in(key, 6)
    for dim, shards_of in cuts:
        heights = jnp.exp(jax.random.uniform(jax.random.fold_in(own, dim), (shards_of,), jnp.float32, least / len(cuts), largest / len(cuts)))
        level = level * jnp.repeat(heights, dims[dim] // shards_of).reshape([-1 if axis == dim else 1 for axis in range(len(dims))])
    return level


def bell_draw(key, shape, scale, reach, split=(), kind=jnp.bfloat16):
    array = scale * jax.random.normal(key, shape, jnp.float32)
    if split:
        array = array * shard_levels(key, shape, split, -0.22, 0.18)
    return jnp.clip(array, -reach, reach).astype(kind)


def setup_inputs(seed: int = 0) -> dict:
    arg_keys = jax.random.split(jax.random.key(seed), 5)
    seeds = bell_draw(arg_keys[0], (TILES, 6, Z, TX, TY), 1.0, 6.0, ((0, 16), (2, 32)), jnp.float32)
    material = touch_ends(jax.random.randint(arg_keys[1], (TILES, Z, TX, TY), 0, MATERIALS), jax.random.fold_in(arg_keys[1], 1), 0, MATERIALS - 1).astype(jnp.int32)
    decay = jnp.clip(jax.random.uniform(arg_keys[2], (MATERIALS,), jnp.float32, 0.5, 1.0), 0.5, 1.0)
    coupling = jnp.clip(jnp.exp(jax.random.uniform(arg_keys[3], (MATERIALS,), jnp.float32, math.log(0.1), math.log(0.6))), 0.1, 0.6)
    return {"seeds": seeds, "material": material, "decay": decay, "coupling": coupling}


magnetic_coeff = 0.5

def lookup_table(material, table):
    labels = jnp.arange(table.shape[0], dtype=jnp.int32)[:, None, None, None]
    return lax.optimization_barrier(jnp.sum(jnp.where(material[None] == labels, table[:, None, None, None], 0.0), axis=0))

def plus_diff(values, axis_pos):
    width = values.shape[axis_pos]
    later = lax.slice_in_dim(values, 1, width, axis=axis_pos)
    padding = [(0, 0)] * values.ndim
    padding[axis_pos] = (0, 1)
    return jnp.pad(later, padding) - values

def minus_diff(values, axis_pos):
    width = values.shape[axis_pos]
    earlier = lax.slice_in_dim(values, 0, width - 1, axis=axis_pos)
    padding = [(0, 0)] * values.ndim
    padding[axis_pos] = (1, 0)
    return values - jnp.pad(earlier, padding)

def plus_depth(values, after_plane):
    return jnp.concatenate([values[1:], after_plane[None]], axis=0) - values

def minus_depth(values, before_plane):
    return values - jnp.concatenate([before_plane[None], values[:-1]], axis=0)

def curl_forward(fields, after):
    curl_x = plus_diff(fields[2], 2) - plus_depth(fields[1], after[1])
    curl_y = plus_depth(fields[0], after[0]) - plus_diff(fields[2], 1)
    curl_z = plus_diff(fields[1], 1) - plus_diff(fields[0], 2)
    return jnp.stack([curl_x, curl_y, curl_z])

def curl_backward(fields, before):
    curl_x = minus_diff(fields[2], 2) - minus_depth(fields[1], before[1])
    curl_y = minus_depth(fields[0], before[0]) - minus_diff(fields[2], 1)
    curl_z = minus_diff(fields[1], 1) - minus_diff(fields[0], 2)
    return jnp.stack([curl_x, curl_y, curl_z])

def ramp(count):
    position = jnp.arange(count).astype(jnp.float32) + 0.5
    low_part = position / BAND
    high_part = (count - position) / BAND
    return jnp.where(position < BAND, low_part, jnp.where(position > count - BAND, high_part, 1.0))

def reference(seeds, material, decay, coupling):
    side = math.isqrt(N_TILE)

    def run_tile(inputs):
        seed_tile, material_tile = inputs
        decay_map = lookup_table(material_tile, decay)
        coupling_map = lookup_table(material_tile, coupling)
        field_e = seed_tile[:3]
        field_h = seed_tile[3:]
        zero_planes = jnp.zeros((2, TX, TY), seed_tile.dtype)
        for turn_index in range(STEPS):
            scaled = coupling_map * field_e
            field_h = field_h + curl_forward(scaled, zero_planes)
            field_e = decay_map * field_e - magnetic_coeff * curl_backward(field_h, zero_planes)
        return jnp.concatenate([field_e, field_h], axis=0)
    adjoint = lax.map(run_tile, (seeds, material))
    weight = ramp(TX)[:, None] * ramp(TY)[None, :]
    weighted = adjoint * weight
    high_bands = weighted[:, :, :, TX - BAND:, :]
    low_bands = weighted[:, :, :, :BAND, :]
    from_prev = jnp.roll(high_bands, 1, axis=0)
    from_next = jnp.roll(low_bands, -1, axis=0)
    combined = weighted.at[:, :, :, :BAND, :].add(from_prev)
    combined = combined.at[:, :, :, TX - BAND:, :].add(from_next)
    top_slab = combined[..., TY - BAND:]
    bottom_slab = combined[..., :BAND]
    from_below = jnp.roll(top_slab, side, axis=0)
    from_above = jnp.roll(bottom_slab, -side, axis=0)
    result = combined.at[..., :BAND].add(from_below)
    result = result.at[..., TY - BAND:].add(from_above)
    return result
```

```python
import functools
import math

import jax
import jax.numpy as jnp
from jax import lax
from jax.experimental import pallas as pl
from jax.experimental.pallas import tpu as pltpu
from jax.sharding import PartitionSpec as P

BAND = 32
MESH = pl.DeviceIdType.MESH
MAGNETIC = 0.5
TX = 256
TY = 128
PAD = 8
ROWS = 32
EX, EY, EZ, HX, HY, HZ = range(6)

EARLY = ((HX, 0), (HY, 0), (HZ, 0), (HZ, 1), (EZ, 0))
LATE = ((HX, 1), (HY, 1), (EX, 0), (EY, 0), (EX, 1), (EY, 1), (EZ, 1))
ORDER = EARLY + LATE
GROUPS = ((0, len(EARLY)), (len(EARLY), len(LATE)))


def row_tiles(body):
    def step(index, carry):
        body(pl.multiple_of(index * ROWS, ROWS))
        return carry

    lax.fori_loop(0, TX // ROWS, step, 0)


def planes_of(group, body):
    first, count = GROUPS[group]

    def step(index, carry):
        body(index)
        return carry

    lax.fori_loop(first, first + count, step, 0)


def kernel(
    tiles, subs, decay, coupling, seeds, material, out,
    field, mat, ca, cb, s0, s1, h1, h2, e1, a1, a2, up_in, down_in, w,
    yc_out, yn_out, xn_out, xc_out, yc_in, yn_in, xn_in, xc_in,
    load_sem, store_sem, depth_send, depth_recv, band_send, band_recv,
):
    tile = lax.axis_index("tile")
    sub = lax.axis_index("sub")
    side = math.isqrt(tiles)
    has_below = sub > 0
    has_above = sub < subs - 1
    below = jnp.maximum(sub - 1, 0)
    above = jnp.minimum(sub + 1, subs - 1)
    x_prev = lax.rem(tile + tiles - 1, tiles)
    x_next = lax.rem(tile + 1, tiles)
    y_prev = lax.rem(tile + tiles - side, tiles)
    y_next = lax.rem(tile + side, tiles)

    loads = [
        pltpu.make_async_copy(material.at[0], mat, load_sem.at[0]),
        pltpu.make_async_copy(seeds.at[0, 0:3], field.at[0:3, :, PAD : PAD + TX], load_sem.at[1]),
        pltpu.make_async_copy(seeds.at[0, 3:6], field.at[3:6, :, PAD : PAD + TX], load_sem.at[2]),
    ]
    for load in loads:
        load.start()

    barrier = pltpu.get_barrier_semaphore()

    def greet(other_tile, other_sub):
        pl.semaphore_signal(barrier, inc=1, device_id=(other_tile, other_sub), device_id_type=MESH)

    for other in (x_prev, x_next, y_prev, y_next):
        greet(other, sub)
    pl.when(has_below)(lambda: greet(tile, below))
    pl.when(has_above)(lambda: greet(tile, above))

    lane = lax.broadcasted_iota(jnp.int32, (ROWS, TY), 1)
    not_last = lane < TY - 1
    not_first = lane > 0
    zeros_pad = jnp.zeros((PAD, TY), jnp.float32)
    for comp in range(3):
        for plane in range(2):
            for buf in (s0, s1):
                buf[comp, plane, PAD + TX : PAD + TX + PAD, :] = zeros_pad
            for buf in (h1, h2):
                buf[comp, plane, 0:PAD, :] = zeros_pad

    def at(buf, comp, plane, row):
        return buf[comp, plane, pl.ds(PAD + row, ROWS), :]

    def put(buf, comp, plane, row, value):
        buf[comp, plane, pl.ds(PAD + row, ROWS), :] = value

    def plus_x(buf, comp, plane, row):
        return buf[comp, plane, pl.ds(PAD + row + 1, ROWS), :] - at(buf, comp, plane, row)

    def minus_x(buf, comp, plane, row):
        return at(buf, comp, plane, row) - buf[comp, plane, pl.ds(PAD + row - 1, ROWS), :]

    def plus_y(value):
        return jnp.where(not_last, pltpu.roll(value, TY - 1, 1), 0.0) - value

    def minus_y(value):
        return value - jnp.where(not_first, pltpu.roll(value, 1, 1), 0.0)

    def curl_z(buf, plane, row):
        return plus_x(buf, 1, plane, row) - plus_y(at(buf, 0, plane, row))

    ramp_lane = lane.astype(jnp.float32) + 0.5
    ramp_y = jnp.minimum(jnp.minimum(ramp_lane, TY - ramp_lane) * (1.0 / BAND), 1.0)
    row_iota = lax.broadcasted_iota(jnp.int32, (ROWS, TY), 0)

    def weight(row):
        position = (row_iota + row).astype(jnp.float32) + 0.5
        return jnp.minimum(jnp.minimum(position, TX - position) * (1.0 / BAND), 1.0) * ramp_y

    def rows_of(buf, index, row):
        return buf[index, pl.ds(row, ROWS), :]

    def depth_copy(turn, upward):
        source = (a1, a2)[turn] if upward else (s0, s1)[turn].at[0:2, 0, PAD : PAD + TX]
        target = (up_in if upward else down_in).at[turn]
        slot = turn * 2 + int(upward)
        return pltpu.make_async_remote_copy(
            source, target, depth_send.at[slot], depth_recv.at[slot],
            device_id=(tile, above if upward else below), device_id_type=MESH)

    def band_copy(kind, group, toward_next):
        first, count = GROUPS[group]
        source, target = ((yc_out, yc_in), (xn_out, xn_in), (yn_out, yn_in), (xc_out, xc_in))[kind]
        direction = int(toward_next)
        if kind in (0, 2):
            other = y_next if toward_next else y_prev
        else:
            other = x_next if toward_next else x_prev
        slot = (kind * 2 + group) * 2 + direction
        part = slice(first, first + count)
        return pltpu.make_async_remote_copy(
            source.at[direction, part], target.at[direction, part],
            band_send.at[slot], band_recv.at[slot],
            device_id=(other, sub), device_id_type=MESH)

    def send_band(kind, group):
        for toward_next in (False, True):
            band_copy(kind, group, toward_next).start()

    def wait_band(kind, group):
        for toward_next in (False, True):
            band_copy(kind, group, toward_next).wait_recv()

    loads[0].wait()
    loads[1].wait()
    d0, d1, d2, d3 = (decay[i] for i in range(4))
    c0, c1, c2, c3 = (coupling[i] for i in range(4))

    def scale(row):
        for plane in range(2):
            label = mat[plane, pl.ds(row, ROWS), :]
            is0, is1, is2 = label == 0, label == 1, label == 2
            couple = jnp.where(is0, c0, jnp.where(is1, c1, jnp.where(is2, c2, c3)))
            cb[plane, pl.ds(row, ROWS), :] = couple
            ca[plane, pl.ds(row, ROWS), :] = jnp.where(is0, d0, jnp.where(is1, d1, jnp.where(is2, d2, d3)))
            for comp in range(3):
                put(s0, comp, plane, row, couple * at(field, comp, plane, row))

    row_tiles(scale)
    pl.semaphore_wait(barrier, 4 + has_below.astype(jnp.int32) + has_above.astype(jnp.int32))
    pl.when(has_below)(lambda: depth_copy(0, False).start())
    loads[2].wait()

    def partial(hbuf, offset, sbuf, abuf):
        def body(row):
            s_x, s_y, s_z = (at(sbuf, comp, 1, row) for comp in range(3))
            abuf[0, pl.ds(row, ROWS), :] = at(hbuf, offset, 1, row) + plus_y(s_z) + s_y
            abuf[1, pl.ds(row, ROWS), :] = at(hbuf, offset + 1, 1, row) - s_x - plus_x(sbuf, 2, 1, row)

        row_tiles(body)

    partial(field, HX, s0, a1)
    pl.when(has_above)(lambda: depth_copy(0, True).start())

    def magnetic_local(hbuf, offset, sbuf, row):
        s_x0, s_y0, s_z0 = (at(sbuf, comp, 0, row) for comp in range(3))
        new_x = at(hbuf, offset, 0, row) + plus_y(s_z0) - (at(sbuf, 1, 1, row) - s_y0)
        new_y = at(hbuf, offset + 1, 0, row) + (at(sbuf, 0, 1, row) - s_x0) - plus_x(sbuf, 2, 0, row)
        new_z = at(hbuf, offset + 2, 0, row) + curl_z(sbuf, 0, row)
        new_z1 = at(hbuf, offset + 2, 1, row) + curl_z(sbuf, 1, row)
        return new_x, new_y, new_z, new_z1

    def first_local(row):
        new_x, new_y, new_z, new_z1 = magnetic_local(field, HX, s0, row)
        put(h1, 0, 0, row, new_x)
        put(h1, 1, 0, row, new_y)
        put(h1, 2, 0, row, new_z)
        put(h1, 2, 1, row, new_z1)

    row_tiles(first_local)

    def edge_planes(turn, sbuf):
        @pl.when(jnp.logical_not(has_above))
        def _():
            def body(row):
                for comp in range(2):
                    down_in[turn, comp, pl.ds(row, ROWS), :] = jnp.zeros((ROWS, TY), jnp.float32)

            row_tiles(body)

        @pl.when(jnp.logical_not(has_below))
        def _():
            def body(row):
                up_in[turn, 0, pl.ds(row, ROWS), :] = at(sbuf, 1, 0, row)
                up_in[turn, 1, pl.ds(row, ROWS), :] = -at(sbuf, 0, 0, row)

            row_tiles(body)

    def wait_depth(turn):
        pl.when(has_above)(lambda: depth_copy(turn, False).wait_recv())
        pl.when(has_below)(lambda: depth_copy(turn, True).wait_recv())

    def magnetic_rest(turn, abuf, sbuf, row):
        new_x = rows_of(abuf, 0, row) - down_in[turn, 1, pl.ds(row, ROWS), :]
        new_y = rows_of(abuf, 1, row) + down_in[turn, 0, pl.ds(row, ROWS), :]
        under_x = up_in[turn, 0, pl.ds(row, ROWS), :] - at(sbuf, 1, 0, row)
        under_y = up_in[turn, 1, pl.ds(row, ROWS), :] + at(sbuf, 0, 0, row)
        return new_x, new_y, under_x, under_y

    def electric_xy(ebuf, hbuf, plane, row, h_x, h_y, under_x, under_y):
        h_z = at(hbuf, 2, plane, row)
        decays = rows_of(ca, plane, row)
        new_x = decays * at(ebuf, 0, plane, row) - MAGNETIC * (minus_y(h_z) - (h_y - under_y))
        new_y = decays * at(ebuf, 1, plane, row) - MAGNETIC * ((h_x - under_x) - minus_x(hbuf, 2, plane, row))
        return new_x, new_y

    def electric_z(ebuf, hbuf, plane, row, h_x):
        decays = rows_of(ca, plane, row)
        return decays * at(ebuf, 2, plane, row) - MAGNETIC * (minus_x(hbuf, 1, plane, row) - minus_y(h_x))

    edge_planes(0, s0)
    wait_depth(0)

    def first_rest(row):
        x1, y1, under_x, under_y = magnetic_rest(0, a1, s0, row)
        put(h1, 0, 1, row, x1)
        put(h1, 1, 1, row, y1)
        x0, y0 = at(h1, 0, 0, row), at(h1, 1, 0, row)
        for plane, (h_x, h_y, b_x, b_y) in enumerate(((x0, y0, under_x, under_y), (x1, y1, x0, y0))):
            new = (*electric_xy(field, h1, plane, row, h_x, h_y, b_x, b_y), electric_z(field, h1, plane, row, h_x))
            couple = rows_of(cb, plane, row)
            for comp in range(3):
                put(e1, comp, plane, row, new[comp])
                put(s1, comp, plane, row, couple * new[comp])

    row_tiles(first_rest)
    pl.when(has_below)(lambda: depth_copy(1, False).start())
    partial(h1, 0, s1, a2)
    pl.when(has_above)(lambda: depth_copy(1, True).start())

    def keep(name, row, value, weights):
        w[ORDER.index(name), pl.ds(row, ROWS), :] = value * weights

    def second_local(row):
        new_x, new_y, new_z, new_z1 = magnetic_local(h1, 0, s1, row)
        put(h2, 0, 0, row, new_x)
        put(h2, 1, 0, row, new_y)
        put(h2, 2, 0, row, new_z)
        put(h2, 2, 1, row, new_z1)
        weights = weight(row)
        keep((HX, 0), row, new_x, weights)
        keep((HY, 0), row, new_y, weights)
        keep((HZ, 0), row, new_z, weights)
        keep((HZ, 1), row, new_z1, weights)
        keep((EZ, 0), row, electric_z(e1, h2, 0, row, new_x), weights)

    row_tiles(second_local)

    def slot_of(rows):
        return lax.broadcasted_iota(jnp.int32, (rows, TY), 1) // BAND

    def pack_lanes(values):
        slot = slot_of(values[0].shape[0])
        turned = [values[0]] + [pltpu.roll(values[k], BAND * k, 1) for k in (1, 2, 3)]
        low, high = turned[3], turned[0]
        for k in (2, 1, 0):
            low = jnp.where(slot == k, turned[k], low)
            high = jnp.where(slot == k, turned[k + 1], high)
        return low, high

    def unpack_lanes(low_side, high_side):
        slot = slot_of(low_side.shape[0])
        turned = []
        for k in range(4):
            mixed = jnp.where(slot == (k + 3) % 4, low_side, high_side)
            shift = (TY - BAND * (k - 1)) % TY
            turned.append(pltpu.roll(mixed, shift, 1) if shift else mixed)
        return [jnp.where(slot == 0, turned[k], jnp.where(slot == 3, turned[(k + 2) % 4], 0.0)) for k in range(4)]

    corner_rows = (0, 16, TX - 32, TX - 16)
    middle_rows = (32, 80, 128, 176)

    def middle_lanes():
        slot = slot_of(16)
        return jnp.logical_or(slot == 1, slot == 2)

    def pack_corners(index):
        values = [w[index, first : first + 16, :] for first in corner_rows]
        low, high = pack_lanes(values)
        yc_out[0, index], yc_out[1, index] = low, high
        middle = middle_lanes()
        for direction in range(2):
            xn_out[direction, index] = jnp.where(
                middle, values[2 * direction], pltpu.roll(values[2 * direction + 1], TY // 2, 1))

    def pack_middle(index):
        low, high = pack_lanes([w[index, first : first + 48, :] for first in middle_rows])
        yn_out[0, index], yn_out[1, index] = low, high

    def add_corners(index):
        added = unpack_lanes(yc_in[1, index], yc_in[0, index])
        values = []
        for first, more in zip(corner_rows, added):
            total = w[index, first : first + 16, :] + more
            w[index, first : first + 16, :] = total
            values.append(total)
        middle = middle_lanes()
        for direction in range(2):
            xc_out[direction, index] = jnp.where(
                middle, pltpu.roll(values[2 * direction + 1], TY // 2, 1), values[2 * direction])

    def add_middle(index):
        added = unpack_lanes(yn_in[1, index], yn_in[0, index])
        for first, more in zip(middle_rows, added):
            w[index, first : first + 48, :] += more

    def add_x_bands(index):
        middle = middle_lanes()
        for side_of, first in ((1, 0), (0, TX - 32)):
            plain, summed = xn_in[side_of, index], xc_in[side_of, index]
            w[index, first : first + 16, :] += jnp.where(middle, plain, summed)
            w[index, first + 16 : first + 32, :] += pltpu.roll(jnp.where(middle, summed, plain), TY // 2, 1)

    def send_group(group):
        planes_of(group, pack_corners)
        send_band(0, group)
        send_band(1, group)
        planes_of(group, pack_middle)
        send_band(2, group)

    send_group(0)
    edge_planes(1, s1)
    wait_depth(1)

    def second_rest(row):
        x1, y1, under_x, under_y = magnetic_rest(1, a2, s1, row)
        put(h2, 0, 1, row, x1)
        put(h2, 1, 1, row, y1)
        x0, y0 = at(h2, 0, 0, row), at(h2, 1, 0, row)
        weights = weight(row)
        keep((HX, 1), row, x1, weights)
        keep((HY, 1), row, y1, weights)
        for plane, (h_x, h_y, b_x, b_y) in enumerate(((x0, y0, under_x, under_y), (x1, y1, x0, y0))):
            new_x, new_y = electric_xy(e1, h2, plane, row, h_x, h_y, b_x, b_y)
            keep((EX, plane), row, new_x, weights)
            keep((EY, plane), row, new_y, weights)
        keep((EZ, 1), row, electric_z(e1, h2, 1, row, x1), weights)

    row_tiles(second_rest)
    send_group(1)

    for group in range(2):
        wait_band(0, group)
        planes_of(group, add_corners)
        send_band(3, group)

    stores = []
    for group in range(2):
        wait_band(2, group)
        planes_of(group, add_middle)
        wait_band(1, group)
        wait_band(3, group)
        planes_of(group, add_x_bands)
        first, count = GROUPS[group]
        for index in range(first, first + count):
            comp, plane = ORDER[index]
            store = pltpu.make_async_copy(w.at[index], out.at[0, comp, plane], store_sem.at[index])
            store.start()
            stores.append(store)

    for turn in range(2):
        pl.when(has_below)(lambda: depth_copy(turn, False).wait_send())
        pl.when(has_above)(lambda: depth_copy(turn, True).wait_send())
    for group in range(2):
        for kind in range(4):
            for toward_next in (False, True):
                band_copy(kind, group, toward_next).wait_send()
    for store in stores:
        store.wait()


def on_device(tiles, subs, seeds, material, decay, coupling):
    f32 = jnp.float32
    padded = (3, 2, PAD + TX + PAD, TY)
    planes = len(ORDER)
    narrow, wide = pltpu.VMEM((2, planes, 16, TY), f32), pltpu.VMEM((2, planes, 48, TY), f32)
    smem = pl.BlockSpec(memory_space=pltpu.SMEM)
    anywhere = pl.BlockSpec(memory_space=pl.ANY)
    return pl.pallas_call(
        functools.partial(kernel, tiles, subs),
        out_shape=jax.ShapeDtypeStruct(seeds.shape, f32),
        in_specs=[smem, smem, anywhere, anywhere],
        out_specs=anywhere,
        scratch_shapes=[
            pltpu.VMEM((6, *padded[1:]), f32),
            pltpu.VMEM((2, TX, TY), jnp.int32),
            pltpu.VMEM((2, TX, TY), f32),
            pltpu.VMEM((2, TX, TY), f32),
            *[pltpu.VMEM(padded, f32)] * 5,
            pltpu.VMEM((2, TX, TY), f32),
            pltpu.VMEM((2, TX, TY), f32),
            pltpu.VMEM((2, 2, TX, TY), f32),
            pltpu.VMEM((2, 2, TX, TY), f32),
            pltpu.VMEM((planes, TX, TY), f32),
            narrow, wide, narrow, narrow,
            narrow, wide, narrow, narrow,
            pltpu.SemaphoreType.DMA((3,)),
            pltpu.SemaphoreType.DMA((planes,)),
            pltpu.SemaphoreType.DMA((4,)),
            pltpu.SemaphoreType.DMA((4,)),
            pltpu.SemaphoreType.DMA((16,)),
            pltpu.SemaphoreType.DMA((16,)),
        ],
        compiler_params=pltpu.CompilerParams(collective_id=0, has_side_effects=True),
    )(decay, coupling, seeds, material)


def solution(mesh):
    placed = (P("tile", None, "sub", None, None), P("tile", "sub", None, None), P(), P())
    return jax.shard_map(
        functools.partial(on_device, mesh.shape["tile"], mesh.shape["sub"]),
        mesh=mesh,
        in_specs=placed,
        out_specs=P("tile", None, "sub", None, None),
        check_vma=False,
    )
```

```python
import functools
import math

import jax
import jax.numpy as jnp
from jax import lax
from jax.experimental import pallas as pl
from jax.experimental.pallas import tpu as pltpu
from jax.sharding import PartitionSpec as P

BAND = 32
MESH = pl.DeviceIdType.MESH
MAGNETIC = 0.5
TX = 256
TY = 128
PAD = 8
ROWS = 32
EX, EY, EZ, HX, HY, HZ = range(6)

EARLY = ((HX, 0), (HY, 0), (HZ, 0), (HZ, 1), (EZ, 0))
LATE = ((HX, 1), (HY, 1), (EX, 0), (EY, 0), (EX, 1), (EY, 1), (EZ, 1))
ORDER = EARLY + LATE
GROUPS = ((0, len(EARLY)), (len(EARLY), len(LATE)))

RUN = 8
PARTS = 3
PART_ROWS = 56
DIRECT = TX - PARTS * PART_ROWS


def row_tiles(body):
    def step(index, carry):
        body(pl.multiple_of(index * ROWS, ROWS))
        return carry

    lax.fori_loop(0, TX // ROWS, step, 0)


def planes_of(group, body):
    first, count = GROUPS[group]

    def step(index, carry):
        body(index)
        return carry

    lax.fori_loop(first, first + count, step, 0)


def kernel(
    tiles, subs, decay_in, coupling_in, seeds, material, w,
    decay, coupling, field, mat, ca, cb, s0, s1, h1, h2, e1, a1, a2, up_in, down_in, relay_in,
    yc_out, yn_out, xn_out, xc_out, yc_in, yn_in, xn_in, xc_in,
    load_sem, depth_send, depth_recv, part_send, part_recv, relay_recv, relay_send, band_send, band_recv,
):
    tile = lax.axis_index("tile")
    sub = lax.axis_index("sub")
    side = math.isqrt(tiles)
    has_below = sub > 0
    has_above = sub < subs - 1
    below = jnp.maximum(sub - 1, 0)
    above = jnp.minimum(sub + 1, subs - 1)
    x_prev = lax.rem(tile + tiles - 1, tiles)
    x_next = lax.rem(tile + 1, tiles)
    y_prev = lax.rem(tile + tiles - side, tiles)
    y_next = lax.rem(tile + side, tiles)

    loads = [
        pltpu.make_async_copy(material.at[0], mat, load_sem.at[0]),
        pltpu.make_async_copy(seeds.at[0, 0:3], field.at[0:3, :, PAD : PAD + TX], load_sem.at[1]),
        pltpu.make_async_copy(seeds.at[0, 3:6], field.at[3:6, :, PAD : PAD + TX], load_sem.at[2]),
        pltpu.make_async_copy(decay_in, decay, load_sem.at[3]),
        pltpu.make_async_copy(coupling_in, coupling, load_sem.at[4]),
    ]
    for load in loads:
        load.start()

    barrier = pltpu.get_barrier_semaphore()

    def greet(other_tile, other_sub):
        pl.semaphore_signal(barrier, inc=1, device_id=(other_tile, other_sub), device_id_type=MESH)

    for other in (x_prev, x_next, y_prev, y_next):
        greet(other, sub)
    pl.when(has_below)(lambda: greet(tile, below))
    pl.when(has_above)(lambda: greet(tile, above))
    place_in_run = lax.rem(sub, RUN)
    start = sub - place_in_run
    run_above = start + RUN < subs
    run_below = start > 0
    crosses_up = jnp.logical_and(place_in_run == RUN - 1, run_above)
    crosses_down = jnp.logical_and(place_in_run == 0, run_below)
    odd = lax.rem(place_in_run, 2) == 1
    relays_up = jnp.logical_and(jnp.logical_and(odd, place_in_run < RUN - 1), run_above)
    relays_down = jnp.logical_and(jnp.logical_and(jnp.logical_not(odd), place_in_run > 0), run_below)
    relay_part = jnp.where(odd, place_in_run // 2, jnp.maximum(place_in_run // 2 - 1, 0))
    last_here = start + RUN - 1
    first_above = jnp.minimum(start + RUN, subs - 1)
    last_below = jnp.maximum(start - 1, 0)

    def up_relay(part):
        return start + 2 * part + 1

    def down_relay(part):
        return start + 2 * part + 2

    @pl.when(crosses_up)
    def _():
        for part in range(PARTS):
            greet(tile, up_relay(part))
            greet(tile, jnp.minimum(down_relay(part) + RUN, subs - 1))

    @pl.when(crosses_down)
    def _():
        for part in range(PARTS):
            greet(tile, down_relay(part))
            greet(tile, jnp.maximum(up_relay(part) - RUN, 0))

    @pl.when(relays_up)
    def _():
        greet(tile, last_here)
        greet(tile, first_above)

    @pl.when(relays_down)
    def _():
        greet(tile, start)
        greet(tile, last_below)

    lane = lax.broadcasted_iota(jnp.int32, (ROWS, TY), 1)
    not_last = lane < TY - 1
    not_first = lane > 0
    zeros_pad = jnp.zeros((PAD, TY), jnp.float32)
    for comp in range(3):
        for plane in range(2):
            for buf in (s0, s1):
                buf[comp, plane, PAD + TX : PAD + TX + PAD, :] = zeros_pad
            for buf in (h1, h2):
                buf[comp, plane, 0:PAD, :] = zeros_pad

    def at(buf, comp, plane, row):
        return buf[comp, plane, pl.ds(PAD + row, ROWS), :]

    def put(buf, comp, plane, row, value):
        buf[comp, plane, pl.ds(PAD + row, ROWS), :] = value

    def plus_x(buf, comp, plane, row):
        return buf[comp, plane, pl.ds(PAD + row + 1, ROWS), :] - at(buf, comp, plane, row)

    def minus_x(buf, comp, plane, row):
        return at(buf, comp, plane, row) - buf[comp, plane, pl.ds(PAD + row - 1, ROWS), :]

    def plus_y(value):
        return jnp.where(not_last, pltpu.roll(value, TY - 1, 1), 0.0) - value

    def minus_y(value):
        return value - jnp.where(not_first, pltpu.roll(value, 1, 1), 0.0)

    def curl_z(buf, plane, row):
        return plus_x(buf, 1, plane, row) - plus_y(at(buf, 0, plane, row))

    ramp_lane = lane.astype(jnp.float32) + 0.5
    ramp_y = jnp.minimum(jnp.minimum(ramp_lane, TY - ramp_lane) * (1.0 / BAND), 1.0)
    row_iota = lax.broadcasted_iota(jnp.int32, (ROWS, TY), 0)

    def weight(row):
        position = (row_iota + row).astype(jnp.float32) + 0.5
        return jnp.minimum(jnp.minimum(position, TX - position) * (1.0 / BAND), 1.0) * ramp_y

    def rows_of(buf, index, row):
        return buf[index, pl.ds(row, ROWS), :]

    def depth_rows(turn, upward, first, count):
        if upward:
            return (a1, a2)[turn].at[:, first : first + count]
        return (s0, s1)[turn].at[0:2, 0, PAD + first : PAD + first + count]

    def depth_copy(turn, upward, count):
        slot = turn * 2 + int(upward)
        return pltpu.make_async_remote_copy(
            depth_rows(turn, upward, 0, count), (up_in if upward else down_in).at[turn, :, 0:count],
            depth_send.at[slot], depth_recv.at[slot],
            device_id=(tile, above if upward else below), device_id_type=MESH)

    def part_copy(turn, upward, part):
        relay = up_relay(part) if upward else down_relay(part)
        return pltpu.make_async_remote_copy(
            depth_rows(turn, upward, DIRECT + part * PART_ROWS, PART_ROWS), relay_in.at[turn],
            part_send.at[turn * PARTS + part], relay_recv.at[turn],
            device_id=(tile, relay), device_id_type=MESH)

    def relay_copy(turn, upward, part):
        target = (up_in if upward else down_in).at[
            turn, :, pl.ds(pl.multiple_of(DIRECT + part * PART_ROWS, 8), PART_ROWS)]
        return pltpu.make_async_remote_copy(
            relay_in.at[turn], target, relay_send.at[turn], part_recv.at[turn * PARTS + part],
            device_id=(tile, first_above if upward else last_below), device_id_type=MESH)

    def send_depth(turn, upward):
        crosses = crosses_up if upward else crosses_down
        plain = jnp.logical_and(has_above if upward else has_below, jnp.logical_not(crosses))

        pl.when(plain)(lambda: depth_copy(turn, upward, TX).start())

        @pl.when(crosses)
        def _():
            for part in range(PARTS):
                part_copy(turn, upward, part).start()
            depth_copy(turn, upward, DIRECT).start()

    def relay_depth(turn):
        for upward, relays in ((True, relays_up), (False, relays_down)):

            @pl.when(relays)
            def _():
                part_copy(turn, upward, 0).wait_recv()
                relay_copy(turn, upward, relay_part).start()

    def wait_depth(turn):
        for upward, crosses in ((True, crosses_down), (False, crosses_up)):
            plain = jnp.logical_and(has_below if upward else has_above, jnp.logical_not(crosses))
            pl.when(plain)(lambda: depth_copy(turn, upward, TX).wait_recv())

            @pl.when(crosses)
            def _():
                depth_copy(turn, upward, DIRECT).wait_recv()
                for part in range(PARTS):
                    relay_copy(turn, upward, part).wait_recv()

    def finish_depth(turn):
        for upward, crosses, relays in ((True, crosses_up, relays_up), (False, crosses_down, relays_down)):
            plain = jnp.logical_and(has_above if upward else has_below, jnp.logical_not(crosses))
            pl.when(plain)(lambda: depth_copy(turn, upward, TX).wait_send())

            @pl.when(crosses)
            def _():
                for part in range(PARTS):
                    part_copy(turn, upward, part).wait_send()
                depth_copy(turn, upward, DIRECT).wait_send()

            pl.when(relays)(lambda: relay_copy(turn, upward, relay_part).wait_send())

    def band_copy(kind, group, toward_next):
        first, count = GROUPS[group]
        source, target = ((yc_out, yc_in), (xn_out, xn_in), (yn_out, yn_in), (xc_out, xc_in))[kind]
        direction = int(toward_next)
        if kind in (0, 2):
            other = y_next if toward_next else y_prev
        else:
            other = x_next if toward_next else x_prev
        slot = (kind * 2 + group) * 2 + direction
        part = slice(first, first + count)
        return pltpu.make_async_remote_copy(
            source.at[direction, part], target.at[direction, part],
            band_send.at[slot], band_recv.at[slot],
            device_id=(other, sub), device_id_type=MESH)

    def send_band(kind, group):
        for toward_next in (False, True):
            band_copy(kind, group, toward_next).start()

    def wait_band(kind, group):
        for toward_next in (False, True):
            band_copy(kind, group, toward_next).wait_recv()

    for number in (3, 4, 0, 1):
        loads[number].wait()
    d0, d1, d2, d3 = (decay[i] for i in range(4))
    c0, c1, c2, c3 = (coupling[i] for i in range(4))

    def scale(row):
        for plane in range(2):
            label = mat[plane, pl.ds(row, ROWS), :]
            is0, is1, is2 = label == 0, label == 1, label == 2
            couple = jnp.where(is0, c0, jnp.where(is1, c1, jnp.where(is2, c2, c3)))
            cb[plane, pl.ds(row, ROWS), :] = couple
            ca[plane, pl.ds(row, ROWS), :] = jnp.where(is0, d0, jnp.where(is1, d1, jnp.where(is2, d2, d3)))
            for comp in range(3):
                put(s0, comp, plane, row, couple * at(field, comp, plane, row))

    row_tiles(scale)
    count = lambda flag, number: jnp.where(flag, number, 0)
    crosses_any = jnp.logical_or(crosses_up, crosses_down)
    relays_any = jnp.logical_or(relays_up, relays_down)
    pl.semaphore_wait(
        barrier, 4 + count(has_below, 1) + count(has_above, 1) + count(crosses_any, 2 * PARTS) + count(relays_any, 2))
    send_depth(0, False)
    loads[2].wait()

    def partial(hbuf, offset, sbuf, abuf):
        def body(row):
            s_x, s_y, s_z = (at(sbuf, comp, 1, row) for comp in range(3))
            abuf[0, pl.ds(row, ROWS), :] = at(hbuf, offset, 1, row) + plus_y(s_z) + s_y
            abuf[1, pl.ds(row, ROWS), :] = at(hbuf, offset + 1, 1, row) - s_x - plus_x(sbuf, 2, 1, row)

        row_tiles(body)

    partial(field, HX, s0, a1)
    send_depth(0, True)

    def magnetic_local(hbuf, offset, sbuf, row):
        s_x0, s_y0, s_z0 = (at(sbuf, comp, 0, row) for comp in range(3))
        new_x = at(hbuf, offset, 0, row) + plus_y(s_z0) - (at(sbuf, 1, 1, row) - s_y0)
        new_y = at(hbuf, offset + 1, 0, row) + (at(sbuf, 0, 1, row) - s_x0) - plus_x(sbuf, 2, 0, row)
        new_z = at(hbuf, offset + 2, 0, row) + curl_z(sbuf, 0, row)
        new_z1 = at(hbuf, offset + 2, 1, row) + curl_z(sbuf, 1, row)
        return new_x, new_y, new_z, new_z1

    def first_local(row):
        new_x, new_y, new_z, new_z1 = magnetic_local(field, HX, s0, row)
        put(h1, 0, 0, row, new_x)
        put(h1, 1, 0, row, new_y)
        put(h1, 2, 0, row, new_z)
        put(h1, 2, 1, row, new_z1)

    row_tiles(first_local)

    def edge_planes(turn, sbuf):
        @pl.when(jnp.logical_not(has_above))
        def _():
            def body(row):
                for comp in range(2):
                    down_in[turn, comp, pl.ds(row, ROWS), :] = jnp.zeros((ROWS, TY), jnp.float32)

            row_tiles(body)

        @pl.when(jnp.logical_not(has_below))
        def _():
            def body(row):
                up_in[turn, 0, pl.ds(row, ROWS), :] = at(sbuf, 1, 0, row)
                up_in[turn, 1, pl.ds(row, ROWS), :] = -at(sbuf, 0, 0, row)

            row_tiles(body)

    def magnetic_rest(turn, abuf, sbuf, row):
        new_x = rows_of(abuf, 0, row) - down_in[turn, 1, pl.ds(row, ROWS), :]
        new_y = rows_of(abuf, 1, row) + down_in[turn, 0, pl.ds(row, ROWS), :]
        under_x = up_in[turn, 0, pl.ds(row, ROWS), :] - at(sbuf, 1, 0, row)
        under_y = up_in[turn, 1, pl.ds(row, ROWS), :] + at(sbuf, 0, 0, row)
        return new_x, new_y, under_x, under_y

    def electric_xy(ebuf, hbuf, plane, row, h_x, h_y, under_x, under_y):
        h_z = at(hbuf, 2, plane, row)
        decays = rows_of(ca, plane, row)
        new_x = decays * at(ebuf, 0, plane, row) - MAGNETIC * (minus_y(h_z) - (h_y - under_y))
        new_y = decays * at(ebuf, 1, plane, row) - MAGNETIC * ((h_x - under_x) - minus_x(hbuf, 2, plane, row))
        return new_x, new_y

    def electric_z(ebuf, hbuf, plane, row, h_x):
        decays = rows_of(ca, plane, row)
        return decays * at(ebuf, 2, plane, row) - MAGNETIC * (minus_x(hbuf, 1, plane, row) - minus_y(h_x))

    edge_planes(0, s0)
    relay_depth(0)
    wait_depth(0)

    def first_rest(row):
        x1, y1, under_x, under_y = magnetic_rest(0, a1, s0, row)
        put(h1, 0, 1, row, x1)
        put(h1, 1, 1, row, y1)
        x0, y0 = at(h1, 0, 0, row), at(h1, 1, 0, row)
        for plane, (h_x, h_y, b_x, b_y) in enumerate(((x0, y0, under_x, under_y), (x1, y1, x0, y0))):
            new = (*electric_xy(field, h1, plane, row, h_x, h_y, b_x, b_y), electric_z(field, h1, plane, row, h_x))
            couple = rows_of(cb, plane, row)
            for comp in range(3):
                put(e1, comp, plane, row, new[comp])
                put(s1, comp, plane, row, couple * new[comp])

    row_tiles(first_rest)
    send_depth(1, False)
    partial(h1, 0, s1, a2)
    send_depth(1, True)

    def keep(name, row, value, weights):
        w[ORDER.index(name), pl.ds(row, ROWS), :] = value * weights

    def second_local(row):
        new_x, new_y, new_z, new_z1 = magnetic_local(h1, 0, s1, row)
        put(h2, 0, 0, row, new_x)
        put(h2, 1, 0, row, new_y)
        put(h2, 2, 0, row, new_z)
        put(h2, 2, 1, row, new_z1)
        weights = weight(row)
        keep((HX, 0), row, new_x, weights)
        keep((HY, 0), row, new_y, weights)
        keep((HZ, 0), row, new_z, weights)
        keep((HZ, 1), row, new_z1, weights)
        keep((EZ, 0), row, electric_z(e1, h2, 0, row, new_x), weights)

    row_tiles(second_local)
    relay_depth(1)

    def slot_of(rows):
        return lax.broadcasted_iota(jnp.int32, (rows, TY), 1) // BAND

    def pack_lanes(values):
        slot = slot_of(values[0].shape[0])
        turned = [values[0]] + [pltpu.roll(values[k], BAND * k, 1) for k in (1, 2, 3)]
        low, high = turned[3], turned[0]
        for k in (2, 1, 0):
            low = jnp.where(slot == k, turned[k], low)
            high = jnp.where(slot == k, turned[k + 1], high)
        return low, high

    def unpack_lanes(low_side, high_side):
        slot = slot_of(low_side.shape[0])
        turned = []
        for k in range(4):
            mixed = jnp.where(slot == (k + 3) % 4, low_side, high_side)
            shift = (TY - BAND * (k - 1)) % TY
            turned.append(pltpu.roll(mixed, shift, 1) if shift else mixed)
        return [jnp.where(slot == 0, turned[k], jnp.where(slot == 3, turned[(k + 2) % 4], 0.0)) for k in range(4)]

    corner_rows = (0, 16, TX - 32, TX - 16)
    middle_rows = (32, 80, 128, 176)

    def middle_lanes():
        slot = slot_of(16)
        return jnp.logical_or(slot == 1, slot == 2)

    def pack_corners(index):
        values = [w[index, first : first + 16, :] for first in corner_rows]
        low, high = pack_lanes(values)
        yc_out[0, index], yc_out[1, index] = low, high
        middle = middle_lanes()
        for direction in range(2):
            xn_out[direction, index] = jnp.where(
                middle, values[2 * direction], pltpu.roll(values[2 * direction + 1], TY // 2, 1))

    def pack_middle(index):
        low, high = pack_lanes([w[index, first : first + 48, :] for first in middle_rows])
        yn_out[0, index], yn_out[1, index] = low, high

    def add_corners(index):
        added = unpack_lanes(yc_in[1, index], yc_in[0, index])
        values = []
        for first, more in zip(corner_rows, added):
            total = w[index, first : first + 16, :] + more
            w[index, first : first + 16, :] = total
            values.append(total)
        middle = middle_lanes()
        for direction in range(2):
            xc_out[direction, index] = jnp.where(
                middle, pltpu.roll(values[2 * direction + 1], TY // 2, 1), values[2 * direction])

    def add_middle(index):
        added = unpack_lanes(yn_in[1, index], yn_in[0, index])
        for first, more in zip(middle_rows, added):
            w[index, first : first + 48, :] += more

    def add_x_bands(index):
        middle = middle_lanes()
        for side_of, first in ((1, 0), (0, TX - 32)):
            plain, summed = xn_in[side_of, index], xc_in[side_of, index]
            w[index, first : first + 16, :] += jnp.where(middle, plain, summed)
            w[index, first + 16 : first + 32, :] += pltpu.roll(jnp.where(middle, summed, plain), TY // 2, 1)

    def send_group(group):
        planes_of(group, pack_corners)
        send_band(0, group)
        send_band(1, group)
        planes_of(group, pack_middle)
        send_band(2, group)

    send_group(0)
    edge_planes(1, s1)
    wait_depth(1)

    def second_rest(row):
        x1, y1, under_x, under_y = magnetic_rest(1, a2, s1, row)
        put(h2, 0, 1, row, x1)
        put(h2, 1, 1, row, y1)
        x0, y0 = at(h2, 0, 0, row), at(h2, 1, 0, row)
        weights = weight(row)
        keep((HX, 1), row, x1, weights)
        keep((HY, 1), row, y1, weights)
        for plane, (h_x, h_y, b_x, b_y) in enumerate(((x0, y0, under_x, under_y), (x1, y1, x0, y0))):
            new_x, new_y = electric_xy(e1, h2, plane, row, h_x, h_y, b_x, b_y)
            keep((EX, plane), row, new_x, weights)
            keep((EY, plane), row, new_y, weights)
        keep((EZ, 1), row, electric_z(e1, h2, 1, row, x1), weights)

    row_tiles(second_rest)
    send_group(1)

    for group in range(2):
        wait_band(0, group)
        planes_of(group, add_corners)
        send_band(3, group)

    for group in range(2):
        wait_band(2, group)
        planes_of(group, add_middle)
        wait_band(1, group)
        wait_band(3, group)
        planes_of(group, add_x_bands)

    for turn in range(2):
        finish_depth(turn)
    for group in range(2):
        for kind in range(4):
            for toward_next in (False, True):
                band_copy(kind, group, toward_next).wait_send()


def place(planes, out, sems):
    copies = [
        pltpu.make_async_copy(planes.at[index], out.at[0, comp, plane], sems.at[index])
        for index, (comp, plane) in enumerate(ORDER)
    ]
    for copy in copies:
        copy.start()
    for copy in copies:
        copy.wait()


def on_device(tiles, subs, seeds, material, decay, coupling):
    f32 = jnp.float32
    padded = (3, 2, PAD + TX + PAD, TY)
    planes = len(ORDER)
    narrow, wide = pltpu.VMEM((2, planes, 16, TY), f32), pltpu.VMEM((2, planes, 48, TY), f32)
    hbm = pl.BlockSpec(memory_space=pltpu.HBM)
    done = pl.pallas_call(
        functools.partial(kernel, tiles, subs),
        out_shape=jax.ShapeDtypeStruct((planes, TX, TY), f32),
        in_specs=[hbm] * 4,
        out_specs=pl.BlockSpec(memory_space=pltpu.VMEM),
        scratch_shapes=[
            pltpu.SMEM(decay.shape, f32),
            pltpu.SMEM(coupling.shape, f32),
            pltpu.VMEM((6, *padded[1:]), f32),
            pltpu.VMEM((2, TX, TY), jnp.int32),
            pltpu.VMEM((2, TX, TY), f32),
            pltpu.VMEM((2, TX, TY), f32),
            *[pltpu.VMEM(padded, f32)] * 5,
            pltpu.VMEM((2, TX, TY), f32),
            pltpu.VMEM((2, TX, TY), f32),
            pltpu.VMEM((2, 2, TX, TY), f32),
            pltpu.VMEM((2, 2, TX, TY), f32),
            pltpu.VMEM((2, 2, PART_ROWS, TY), f32),
            narrow, wide, narrow, narrow,
            narrow, wide, narrow, narrow,
            pltpu.SemaphoreType.DMA((5,)),
            pltpu.SemaphoreType.DMA((4,)),
            pltpu.SemaphoreType.DMA((4,)),
            pltpu.SemaphoreType.DMA((2 * PARTS,)),
            pltpu.SemaphoreType.DMA((2 * PARTS,)),
            pltpu.SemaphoreType.DMA((2,)),
            pltpu.SemaphoreType.DMA((2,)),
            pltpu.SemaphoreType.DMA((16,)),
            pltpu.SemaphoreType.DMA((16,)),
        ],
        compiler_params=pltpu.CompilerParams(
            collective_id=0, has_side_effects=True, vmem_limit_bytes=20 * 2**20),
    )(*(pltpu.with_memory_space_constraint(array, pltpu.HBM) for array in (decay, coupling, seeds, material)))
    return pl.pallas_call(
        place,
        out_shape=jax.ShapeDtypeStruct(seeds.shape, f32),
        in_specs=[pl.BlockSpec(memory_space=pltpu.VMEM)],
        out_specs=hbm,
        scratch_shapes=[pltpu.SemaphoreType.DMA((planes,))],
        compiler_params=pltpu.CompilerParams(vmem_limit_bytes=4 * 2**20),
    )(done)


def solution(mesh):
    placed = (P("tile", None, "sub", None, None), P("tile", "sub", None, None), P(), P())
    return jax.shard_map(
        functools.partial(on_device, mesh.shape["tile"], mesh.shape["sub"]),
        mesh=mesh,
        in_specs=placed,
        out_specs=P("tile", None, "sub", None, None),
        check_vma=False,
    )
```

```python
import functools
import math

import jax
import jax.numpy as jnp
from jax import lax
from jax.experimental import pallas as pl
from jax.experimental.pallas import tpu as pltpu
from jax.sharding import PartitionSpec as P

BAND = 32
MESH = pl.DeviceIdType.MESH
MAGNETIC = 0.5
TX = 256
TY = 128
PAD = 8
ROWS = 32
EX, EY, EZ, HX, HY, HZ = range(6)

EARLY = ((HX, 0), (HY, 0), (HZ, 0), (HZ, 1), (EZ, 0))
LATE = ((HX, 1), (HY, 1), (EX, 0), (EY, 0), (EX, 1), (EY, 1), (EZ, 1))
ORDER = EARLY + LATE
GROUPS = ((0, len(EARLY)), (len(EARLY), len(LATE)))

RUN = 8
PARTS = 3
PART_ROWS = 56
DIRECT = TX - PARTS * PART_ROWS


def row_tiles(body):
    def step(index, carry):
        body(pl.multiple_of(index * ROWS, ROWS))
        return carry

    lax.fori_loop(0, TX // ROWS, step, 0, unroll=2)


def planes_of(group, body):
    first, count = GROUPS[group]

    def step(index, carry):
        body(index)
        return carry

    lax.fori_loop(first, first + count, step, 0, unroll=True)


def kernel(
    tiles, subs, decay_in, coupling_in, seeds, material, w,
    decay, coupling, field, mat, ca, cb, s0, s1, h1, h2, e1, a1, a2, up_in, down_in, relay_in,
    yc_out, yn_out, xn_out, xc_out, yc_in, yn_in, xn_in, xc_in,
    load_sem, depth_send, depth_recv, part_send, part_recv, relay_recv, relay_send, band_send, band_recv,
):
    tile = lax.axis_index("tile")
    sub = lax.axis_index("sub")
    side = math.isqrt(tiles)
    has_below = sub > 0
    has_above = sub < subs - 1
    below = jnp.maximum(sub - 1, 0)
    above = jnp.minimum(sub + 1, subs - 1)
    x_prev = lax.rem(tile + tiles - 1, tiles)
    x_next = lax.rem(tile + 1, tiles)
    y_prev = lax.rem(tile + tiles - side, tiles)
    y_next = lax.rem(tile + side, tiles)

    loads = [
        pltpu.make_async_copy(material.at[0], mat, load_sem.at[0]),
        pltpu.make_async_copy(seeds.at[0, 0:3], field.at[0:3, :, PAD : PAD + TX], load_sem.at[1]),
        pltpu.make_async_copy(seeds.at[0, 3:6], field.at[3:6, :, PAD : PAD + TX], load_sem.at[2]),
        pltpu.make_async_copy(decay_in, decay, load_sem.at[3]),
        pltpu.make_async_copy(coupling_in, coupling, load_sem.at[4]),
    ]
    for load in loads:
        load.start()

    barrier = pltpu.get_barrier_semaphore()

    def greet(other_tile, other_sub):
        pl.semaphore_signal(barrier, inc=1, device_id=(other_tile, other_sub), device_id_type=MESH)

    for other in (x_prev, x_next, y_prev, y_next):
        greet(other, sub)
    pl.when(has_below)(lambda: greet(tile, below))
    pl.when(has_above)(lambda: greet(tile, above))
    place_in_run = lax.rem(sub, RUN)
    start = sub - place_in_run
    run_above = start + RUN < subs
    run_below = start > 0
    crosses_up = jnp.logical_and(place_in_run == RUN - 1, run_above)
    crosses_down = jnp.logical_and(place_in_run == 0, run_below)
    odd = lax.rem(place_in_run, 2) == 1
    relays_up = jnp.logical_and(jnp.logical_and(odd, place_in_run < RUN - 1), run_above)
    relays_down = jnp.logical_and(jnp.logical_and(jnp.logical_not(odd), place_in_run > 0), run_below)
    relay_part = jnp.where(odd, place_in_run // 2, jnp.maximum(place_in_run // 2 - 1, 0))
    last_here = start + RUN - 1
    first_above = jnp.minimum(start + RUN, subs - 1)
    last_below = jnp.maximum(start - 1, 0)

    def up_relay(part):
        return start + 2 * part + 1

    def down_relay(part):
        return start + 2 * part + 2

    @pl.when(crosses_up)
    def _():
        for part in range(PARTS):
            greet(tile, up_relay(part))
            greet(tile, jnp.minimum(down_relay(part) + RUN, subs - 1))

    @pl.when(crosses_down)
    def _():
        for part in range(PARTS):
            greet(tile, down_relay(part))
            greet(tile, jnp.maximum(up_relay(part) - RUN, 0))

    @pl.when(relays_up)
    def _():
        greet(tile, last_here)
        greet(tile, first_above)

    @pl.when(relays_down)
    def _():
        greet(tile, start)
        greet(tile, last_below)

    lane = lax.broadcasted_iota(jnp.int32, (ROWS, TY), 1)
    not_last = lane < TY - 1
    not_first = lane > 0
    zeros_pad = jnp.zeros((PAD, TY), jnp.float32)
    for comp in range(3):
        for plane in range(2):
            for buf in (s0, s1):
                buf[comp, plane, PAD + TX : PAD + TX + PAD, :] = zeros_pad
            for buf in (h1, h2):
                buf[comp, plane, 0:PAD, :] = zeros_pad

    def at(buf, comp, plane, row):
        return buf[comp, plane, pl.ds(PAD + row, ROWS), :]

    def put(buf, comp, plane, row, value):
        buf[comp, plane, pl.ds(PAD + row, ROWS), :] = value

    def plus_x(buf, comp, plane, row):
        return buf[comp, plane, pl.ds(PAD + row + 1, ROWS), :] - at(buf, comp, plane, row)

    def minus_x(buf, comp, plane, row):
        return at(buf, comp, plane, row) - buf[comp, plane, pl.ds(PAD + row - 1, ROWS), :]

    def plus_y(value):
        return jnp.where(not_last, pltpu.roll(value, TY - 1, 1), 0.0) - value

    def minus_y(value):
        return value - jnp.where(not_first, pltpu.roll(value, 1, 1), 0.0)

    def curl_z(buf, plane, row):
        return plus_x(buf, 1, plane, row) - plus_y(at(buf, 0, plane, row))

    ramp_lane = lane.astype(jnp.float32) + 0.5
    ramp_y = jnp.minimum(jnp.minimum(ramp_lane, TY - ramp_lane) * (1.0 / BAND), 1.0)
    row_iota = lax.broadcasted_iota(jnp.int32, (ROWS, TY), 0)

    def weight(row):
        position = (row_iota + row).astype(jnp.float32) + 0.5
        return jnp.minimum(jnp.minimum(position, TX - position) * (1.0 / BAND), 1.0) * ramp_y

    def rows_of(buf, index, row):
        return buf[index, pl.ds(row, ROWS), :]

    def depth_rows(turn, upward, first, count):
        if upward:
            return (a1, a2)[turn].at[:, first : first + count]
        return (s0, s1)[turn].at[0:2, 0, PAD + first : PAD + first + count]

    def depth_copy(turn, upward, count):
        slot = turn * 2 + int(upward)
        return pltpu.make_async_remote_copy(
            depth_rows(turn, upward, 0, count), (up_in if upward else down_in).at[turn, :, 0:count],
            depth_send.at[slot], depth_recv.at[slot],
            device_id=(tile, above if upward else below), device_id_type=MESH)

    def part_copy(turn, upward, part):
        relay = up_relay(part) if upward else down_relay(part)
        return pltpu.make_async_remote_copy(
            depth_rows(turn, upward, DIRECT + part * PART_ROWS, PART_ROWS), relay_in.at[turn],
            part_send.at[turn * PARTS + part], relay_recv.at[turn],
            device_id=(tile, relay), device_id_type=MESH)

    def relay_copy(turn, upward, part):
        target = (up_in if upward else down_in).at[
            turn, :, pl.ds(pl.multiple_of(DIRECT + part * PART_ROWS, 8), PART_ROWS)]
        return pltpu.make_async_remote_copy(
            relay_in.at[turn], target, relay_send.at[turn], part_recv.at[turn * PARTS + part],
            device_id=(tile, first_above if upward else last_below), device_id_type=MESH)

    def send_depth(turn, upward):
        crosses = crosses_up if upward else crosses_down
        plain = jnp.logical_and(has_above if upward else has_below, jnp.logical_not(crosses))

        pl.when(plain)(lambda: depth_copy(turn, upward, TX).start())

        @pl.when(crosses)
        def _():
            for part in range(PARTS):
                part_copy(turn, upward, part).start()
            depth_copy(turn, upward, DIRECT).start()

    def relay_depth(turn):
        for upward, relays in ((True, relays_up), (False, relays_down)):

            @pl.when(relays)
            def _():
                part_copy(turn, upward, 0).wait_recv()
                relay_copy(turn, upward, relay_part).start()

    def wait_depth(turn):
        for upward, crosses in ((True, crosses_down), (False, crosses_up)):
            plain = jnp.logical_and(has_below if upward else has_above, jnp.logical_not(crosses))
            pl.when(plain)(lambda: depth_copy(turn, upward, TX).wait_recv())

            @pl.when(crosses)
            def _():
                depth_copy(turn, upward, DIRECT).wait_recv()
                for part in range(PARTS):
                    relay_copy(turn, upward, part).wait_recv()

    def finish_depth(turn):
        for upward, crosses, relays in ((True, crosses_up, relays_up), (False, crosses_down, relays_down)):
            plain = jnp.logical_and(has_above if upward else has_below, jnp.logical_not(crosses))
            pl.when(plain)(lambda: depth_copy(turn, upward, TX).wait_send())

            @pl.when(crosses)
            def _():
                for part in range(PARTS):
                    part_copy(turn, upward, part).wait_send()
                depth_copy(turn, upward, DIRECT).wait_send()

            pl.when(relays)(lambda: relay_copy(turn, upward, relay_part).wait_send())

    def band_copy(kind, group, toward_next):
        first, count = GROUPS[group]
        source, target = ((yc_out, yc_in), (xn_out, xn_in), (yn_out, yn_in), (xc_out, xc_in))[kind]
        direction = int(toward_next)
        if kind in (0, 2):
            other = y_next if toward_next else y_prev
        else:
            other = x_next if toward_next else x_prev
        slot = (kind * 2 + group) * 2 + direction
        part = slice(first, first + count)
        return pltpu.make_async_remote_copy(
            source.at[direction, part], target.at[direction, part],
            band_send.at[slot], band_recv.at[slot],
            device_id=(other, sub), device_id_type=MESH)

    def send_band(kind, group):
        for toward_next in (False, True):
            band_copy(kind, group, toward_next).start()

    def wait_band(kind, group):
        for toward_next in (False, True):
            band_copy(kind, group, toward_next).wait_recv()

    for number in (3, 4, 0, 1):
        loads[number].wait()
    d0, d1, d2, d3 = (decay[i] for i in range(4))
    c0, c1, c2, c3 = (coupling[i] for i in range(4))

    def scale(row):
        for plane in range(2):
            label = mat[plane, pl.ds(row, ROWS), :]
            is0, is1, is2 = label == 0, label == 1, label == 2
            couple = jnp.where(is0, c0, jnp.where(is1, c1, jnp.where(is2, c2, c3)))
            cb[plane, pl.ds(row, ROWS), :] = couple
            ca[plane, pl.ds(row, ROWS), :] = jnp.where(is0, d0, jnp.where(is1, d1, jnp.where(is2, d2, d3)))
            for comp in range(3):
                put(s0, comp, plane, row, couple * at(field, comp, plane, row))

    row_tiles(scale)
    count = lambda flag, number: jnp.where(flag, number, 0)
    crosses_any = jnp.logical_or(crosses_up, crosses_down)
    relays_any = jnp.logical_or(relays_up, relays_down)
    pl.semaphore_wait(
        barrier, 4 + count(has_below, 1) + count(has_above, 1) + count(crosses_any, 2 * PARTS) + count(relays_any, 2))
    send_depth(0, False)
    loads[2].wait()

    def partial(hbuf, offset, sbuf, abuf):
        def body(row):
            s_x, s_y, s_z = (at(sbuf, comp, 1, row) for comp in range(3))
            abuf[0, pl.ds(row, ROWS), :] = at(hbuf, offset, 1, row) + plus_y(s_z) + s_y
            abuf[1, pl.ds(row, ROWS), :] = at(hbuf, offset + 1, 1, row) - s_x - plus_x(sbuf, 2, 1, row)

        row_tiles(body)

    partial(field, HX, s0, a1)
    send_depth(0, True)

    def magnetic_local(hbuf, offset, sbuf, row):
        s_x0, s_y0, s_z0 = (at(sbuf, comp, 0, row) for comp in range(3))
        new_x = at(hbuf, offset, 0, row) + plus_y(s_z0) - (at(sbuf, 1, 1, row) - s_y0)
        new_y = at(hbuf, offset + 1, 0, row) + (at(sbuf, 0, 1, row) - s_x0) - plus_x(sbuf, 2, 0, row)
        new_z = at(hbuf, offset + 2, 0, row) + curl_z(sbuf, 0, row)
        new_z1 = at(hbuf, offset + 2, 1, row) + curl_z(sbuf, 1, row)
        return new_x, new_y, new_z, new_z1

    def first_local(row):
        new_x, new_y, new_z, new_z1 = magnetic_local(field, HX, s0, row)
        put(h1, 0, 0, row, new_x)
        put(h1, 1, 0, row, new_y)
        put(h1, 2, 0, row, new_z)
        put(h1, 2, 1, row, new_z1)

    row_tiles(first_local)

    def edge_planes(turn, sbuf):
        @pl.when(jnp.logical_not(has_above))
        def _():
            def body(row):
                for comp in range(2):
                    down_in[turn, comp, pl.ds(row, ROWS), :] = jnp.zeros((ROWS, TY), jnp.float32)

            row_tiles(body)

        @pl.when(jnp.logical_not(has_below))
        def _():
            def body(row):
                up_in[turn, 0, pl.ds(row, ROWS), :] = at(sbuf, 1, 0, row)
                up_in[turn, 1, pl.ds(row, ROWS), :] = -at(sbuf, 0, 0, row)

            row_tiles(body)

    def magnetic_rest(turn, abuf, sbuf, row):
        new_x = rows_of(abuf, 0, row) - down_in[turn, 1, pl.ds(row, ROWS), :]
        new_y = rows_of(abuf, 1, row) + down_in[turn, 0, pl.ds(row, ROWS), :]
        under_x = up_in[turn, 0, pl.ds(row, ROWS), :] - at(sbuf, 1, 0, row)
        under_y = up_in[turn, 1, pl.ds(row, ROWS), :] + at(sbuf, 0, 0, row)
        return new_x, new_y, under_x, under_y

    def electric_xy(ebuf, hbuf, plane, row, h_x, h_y, under_x, under_y):
        h_z = at(hbuf, 2, plane, row)
        decays = rows_of(ca, plane, row)
        new_x = decays * at(ebuf, 0, plane, row) - MAGNETIC * (minus_y(h_z) - (h_y - under_y))
        new_y = decays * at(ebuf, 1, plane, row) - MAGNETIC * ((h_x - under_x) - minus_x(hbuf, 2, plane, row))
        return new_x, new_y

    def electric_z(ebuf, hbuf, plane, row, h_x):
        decays = rows_of(ca, plane, row)
        return decays * at(ebuf, 2, plane, row) - MAGNETIC * (minus_x(hbuf, 1, plane, row) - minus_y(h_x))

    edge_planes(0, s0)
    relay_depth(0)
    wait_depth(0)

    def first_rest(row):
        x1, y1, under_x, under_y = magnetic_rest(0, a1, s0, row)
        put(h1, 0, 1, row, x1)
        put(h1, 1, 1, row, y1)
        x0, y0 = at(h1, 0, 0, row), at(h1, 1, 0, row)
        for plane, (h_x, h_y, b_x, b_y) in enumerate(((x0, y0, under_x, under_y), (x1, y1, x0, y0))):
            new = (*electric_xy(field, h1, plane, row, h_x, h_y, b_x, b_y), electric_z(field, h1, plane, row, h_x))
            couple = rows_of(cb, plane, row)
            for comp in range(3):
                put(e1, comp, plane, row, new[comp])
                put(s1, comp, plane, row, couple * new[comp])

    row_tiles(first_rest)
    send_depth(1, False)
    partial(h1, 0, s1, a2)
    send_depth(1, True)

    def keep(name, row, value, weights):
        w[ORDER.index(name), pl.ds(row, ROWS), :] = value * weights

    def second_local(row):
        new_x, new_y, new_z, new_z1 = magnetic_local(h1, 0, s1, row)
        put(h2, 0, 0, row, new_x)
        put(h2, 1, 0, row, new_y)
        put(h2, 2, 0, row, new_z)
        put(h2, 2, 1, row, new_z1)
        weights = weight(row)
        keep((HX, 0), row, new_x, weights)
        keep((HY, 0), row, new_y, weights)
        keep((HZ, 0), row, new_z, weights)
        keep((HZ, 1), row, new_z1, weights)
        keep((EZ, 0), row, electric_z(e1, h2, 0, row, new_x), weights)

    row_tiles(second_local)

    def slot_of(rows):
        return lax.broadcasted_iota(jnp.int32, (rows, TY), 1) // BAND

    def pack_lanes(values):
        slot = slot_of(values[0].shape[0])
        turned = [values[0]] + [pltpu.roll(values[k], BAND * k, 1) for k in (1, 2, 3)]
        low, high = turned[3], turned[0]
        for k in (2, 1, 0):
            low = jnp.where(slot == k, turned[k], low)
            high = jnp.where(slot == k, turned[k + 1], high)
        return low, high

    def unpack_lanes(low_side, high_side):
        slot = slot_of(low_side.shape[0])
        turned = []
        for k in range(4):
            mixed = jnp.where(slot == (k + 3) % 4, low_side, high_side)
            shift = (TY - BAND * (k - 1)) % TY
            turned.append(pltpu.roll(mixed, shift, 1) if shift else mixed)
        return [jnp.where(slot == 0, turned[k], jnp.where(slot == 3, turned[(k + 2) % 4], 0.0)) for k in range(4)]

    corner_rows = (0, 16, TX - 32, TX - 16)
    middle_rows = (32, 80, 128, 176)

    def middle_lanes():
        slot = slot_of(16)
        return jnp.logical_or(slot == 1, slot == 2)

    def pack_corners(index):
        values = [w[index, first : first + 16, :] for first in corner_rows]
        low, high = pack_lanes(values)
        yc_out[0, index], yc_out[1, index] = low, high
        middle = middle_lanes()
        for direction in range(2):
            xn_out[direction, index] = jnp.where(
                middle, values[2 * direction], pltpu.roll(values[2 * direction + 1], TY // 2, 1))

    def pack_middle(index):
        low, high = pack_lanes([w[index, first : first + 48, :] for first in middle_rows])
        yn_out[0, index], yn_out[1, index] = low, high

    def add_corners(index):
        added = unpack_lanes(yc_in[1, index], yc_in[0, index])
        values = []
        for first, more in zip(corner_rows, added):
            total = w[index, first : first + 16, :] + more
            w[index, first : first + 16, :] = total
            values.append(total)
        middle = middle_lanes()
        for direction in range(2):
            xc_out[direction, index] = jnp.where(
                middle, pltpu.roll(values[2 * direction + 1], TY // 2, 1), values[2 * direction])

    def add_middle(index):
        added = unpack_lanes(yn_in[1, index], yn_in[0, index])
        for first, more in zip(middle_rows, added):
            w[index, first : first + 48, :] += more

    def add_x_bands(index):
        middle = middle_lanes()
        for side_of, first in ((1, 0), (0, TX - 32)):
            plain, summed = xn_in[side_of, index], xc_in[side_of, index]
            w[index, first : first + 16, :] += jnp.where(middle, plain, summed)
            w[index, first + 16 : first + 32, :] += pltpu.roll(jnp.where(middle, summed, plain), TY // 2, 1)

    def send_group(group):
        planes_of(group, pack_corners)
        send_band(0, group)
        send_band(1, group)
        planes_of(group, pack_middle)
        send_band(2, group)

    send_group(0)
    relay_depth(1)
    edge_planes(1, s1)
    wait_depth(1)

    def second_rest(row):
        x1, y1, under_x, under_y = magnetic_rest(1, a2, s1, row)
        put(h2, 0, 1, row, x1)
        put(h2, 1, 1, row, y1)
        x0, y0 = at(h2, 0, 0, row), at(h2, 1, 0, row)
        weights = weight(row)
        keep((HX, 1), row, x1, weights)
        keep((HY, 1), row, y1, weights)
        for plane, (h_x, h_y, b_x, b_y) in enumerate(((x0, y0, under_x, under_y), (x1, y1, x0, y0))):
            new_x, new_y = electric_xy(e1, h2, plane, row, h_x, h_y, b_x, b_y)
            keep((EX, plane), row, new_x, weights)
            keep((EY, plane), row, new_y, weights)
        keep((EZ, 1), row, electric_z(e1, h2, 1, row, x1), weights)

    row_tiles(second_rest)
    send_group(1)

    for group in range(2):
        wait_band(0, group)
        planes_of(group, add_corners)
        send_band(3, group)

    for group in range(2):
        wait_band(2, group)
        planes_of(group, add_middle)
        wait_band(1, group)
        wait_band(3, group)
        planes_of(group, add_x_bands)

    for turn in range(2):
        finish_depth(turn)
    for group in range(2):
        for kind in range(4):
            for toward_next in (False, True):
                band_copy(kind, group, toward_next).wait_send()


def place(planes, out, sems):
    copies = [
        pltpu.make_async_copy(planes.at[index], out.at[0, comp, plane], sems.at[index])
        for index, (comp, plane) in enumerate(ORDER)
    ]
    for copy in copies:
        copy.start()
    for copy in copies:
        copy.wait()


def on_device(tiles, subs, seeds, material, decay, coupling):
    f32 = jnp.float32
    padded = (3, 2, PAD + TX + PAD, TY)
    planes = len(ORDER)
    narrow, wide = pltpu.VMEM((2, planes, 16, TY), f32), pltpu.VMEM((2, planes, 48, TY), f32)
    hbm = pl.BlockSpec(memory_space=pltpu.HBM)
    done = pl.pallas_call(
        functools.partial(kernel, tiles, subs),
        out_shape=jax.ShapeDtypeStruct((planes, TX, TY), f32),
        in_specs=[hbm] * 4,
        out_specs=pl.BlockSpec(memory_space=pltpu.VMEM),
        scratch_shapes=[
            pltpu.SMEM(decay.shape, f32),
            pltpu.SMEM(coupling.shape, f32),
            pltpu.VMEM((6, *padded[1:]), f32),
            pltpu.VMEM((2, TX, TY), jnp.int32),
            pltpu.VMEM((2, TX, TY), f32),
            pltpu.VMEM((2, TX, TY), f32),
            *[pltpu.VMEM(padded, f32)] * 5,
            pltpu.VMEM((2, TX, TY), f32),
            pltpu.VMEM((2, TX, TY), f32),
            pltpu.VMEM((2, 2, TX, TY), f32),
            pltpu.VMEM((2, 2, TX, TY), f32),
            pltpu.VMEM((2, 2, PART_ROWS, TY), f32),
            narrow, wide, narrow, narrow,
            narrow, wide, narrow, narrow,
            pltpu.SemaphoreType.DMA((5,)),
            pltpu.SemaphoreType.DMA((4,)),
            pltpu.SemaphoreType.DMA((4,)),
            pltpu.SemaphoreType.DMA((2 * PARTS,)),
            pltpu.SemaphoreType.DMA((2 * PARTS,)),
            pltpu.SemaphoreType.DMA((2,)),
            pltpu.SemaphoreType.DMA((2,)),
            pltpu.SemaphoreType.DMA((16,)),
            pltpu.SemaphoreType.DMA((16,)),
        ],
        compiler_params=pltpu.CompilerParams(
            collective_id=0, has_side_effects=True, vmem_limit_bytes=20 * 2**20),
    )(*(pltpu.with_memory_space_constraint(array, pltpu.HBM) for array in (decay, coupling, seeds, material)))
    return pl.pallas_call(
        place,
        out_shape=jax.ShapeDtypeStruct(seeds.shape, f32),
        in_specs=[pl.BlockSpec(memory_space=pltpu.VMEM)],
        out_specs=hbm,
        scratch_shapes=[pltpu.SemaphoreType.DMA((planes,))],
        compiler_params=pltpu.CompilerParams(vmem_limit_bytes=4 * 2**20),
    )(done)


def solution(mesh):
    placed = (P("tile", None, "sub", None, None), P("tile", "sub", None, None), P(), P())
    return jax.shard_map(
        functools.partial(on_device, mesh.shape["tile"], mesh.shape["sub"]),
        mesh=mesh,
        in_specs=placed,
        out_specs=P("tile", None, "sub", None, None),
        check_vma=False,
    )
```

```python
import functools
import math

import jax
import jax.numpy as jnp
from jax import lax
from jax.experimental import pallas as pl
from jax.experimental.pallas import tpu as pltpu
from jax.sharding import PartitionSpec as P

BAND = 32
MESH = pl.DeviceIdType.MESH
MAGNETIC = 0.5
TX = 256
TY = 128
PAD = 8
ROWS = 32
EX, EY, EZ, HX, HY, HZ = range(6)

EARLY = ((HX, 0), (HY, 0), (HZ, 0), (HZ, 1), (EZ, 0))
LATE = ((HX, 1), (HY, 1), (EX, 0), (EY, 0), (EX, 1), (EY, 1), (EZ, 1))
ORDER = EARLY + LATE
GROUPS = ((0, len(EARLY)), (len(EARLY), len(LATE)))

RUN = 8
PARTS = 3
PART_ROWS = 56
DIRECT = TX - PARTS * PART_ROWS

LINE = 4
WAYS = (((0, 2), (2, 4), (4, 5)), ((5, 7), (7, 9), (9, 12)))


def row_tiles(body):
    def step(index, carry):
        body(pl.multiple_of(index * ROWS, ROWS))
        return carry

    lax.fori_loop(0, TX // ROWS, step, 0, unroll=2)


def planes_of(group, body):
    first, count = GROUPS[group]

    def step(index, carry):
        body(index)
        return carry

    lax.fori_loop(first, first + count, step, 0, unroll=True)


def kernel(
    tiles, subs, decay_in, coupling_in, seeds, material, w,
    decay, coupling, field, mat, ca, cb, s0, s1, h1, h2, e1, a1, a2, up_in, down_in, relay_in, xr_in,
    yc_out, yn_out, xn_out, xc_out, yc_in, yn_in, xn_in, xc_in,
    load_sem, depth_send, depth_recv, part_send, part_recv, relay_recv, relay_send, band_send, band_recv,
    way_send, way_recv, pass_send, pass_recv,
):
    tile = lax.axis_index("tile")
    sub = lax.axis_index("sub")
    side = math.isqrt(tiles)
    has_below = sub > 0
    has_above = sub < subs - 1
    below = jnp.maximum(sub - 1, 0)
    above = jnp.minimum(sub + 1, subs - 1)
    x_prev = lax.rem(tile + tiles - 1, tiles)
    x_next = lax.rem(tile + 1, tiles)
    y_prev = lax.rem(tile + tiles - side, tiles)
    y_next = lax.rem(tile + side, tiles)

    loads = [
        pltpu.make_async_copy(material.at[0], mat, load_sem.at[0]),
        pltpu.make_async_copy(seeds.at[0, 0:3], field.at[0:3, :, PAD : PAD + TX], load_sem.at[1]),
        pltpu.make_async_copy(seeds.at[0, 3:6], field.at[3:6, :, PAD : PAD + TX], load_sem.at[2]),
        pltpu.make_async_copy(decay_in, decay, load_sem.at[3]),
        pltpu.make_async_copy(coupling_in, coupling, load_sem.at[4]),
    ]
    for load in loads:
        load.start()

    barrier = pltpu.get_barrier_semaphore()

    def greet(other_tile, other_sub):
        pl.semaphore_signal(barrier, inc=1, device_id=(other_tile, other_sub), device_id_type=MESH)

    for other in (x_prev, x_next, y_prev, y_next):
        greet(other, sub)
    pl.when(has_below)(lambda: greet(tile, below))
    pl.when(has_above)(lambda: greet(tile, above))
    place_in_run = lax.rem(sub, RUN)
    start = sub - place_in_run
    run_above = start + RUN < subs
    run_below = start > 0
    crosses_up = jnp.logical_and(place_in_run == RUN - 1, run_above)
    crosses_down = jnp.logical_and(place_in_run == 0, run_below)
    odd = lax.rem(place_in_run, 2) == 1
    relays_up = jnp.logical_and(jnp.logical_and(odd, place_in_run < RUN - 1), run_above)
    relays_down = jnp.logical_and(jnp.logical_and(jnp.logical_not(odd), place_in_run > 0), run_below)
    relay_part = jnp.where(odd, place_in_run // 2, jnp.maximum(place_in_run // 2 - 1, 0))
    last_here = start + RUN - 1
    first_above = jnp.minimum(start + RUN, subs - 1)
    last_below = jnp.maximum(start - 1, 0)

    def up_relay(part):
        return start + 2 * part + 1

    def down_relay(part):
        return start + 2 * part + 2

    in_line = lax.rem(tile, LINE)

    def tile_at(distance):
        return lax.rem(tile + tiles + distance, tiles)

    def sends_around(direction):
        return in_line == (LINE - 1 if direction else 0)

    def gets_around(direction):
        return in_line == (0 if direction else LINE - 1)

    def passes_on(direction, way):
        return in_line == (way if direction else LINE - 1 - way)

    for direction in range(2):
        sign = 1 if direction else -1
        for way in range(1, LINE):
            pl.when(sends_around(direction))(lambda: greet(tile_at(sign * (1 + way)), sub))
            pl.when(gets_around(direction))(lambda: greet(tile_at(sign * way), sub))

            @pl.when(passes_on(direction, way))
            def _():
                greet(tile_at(-sign * (1 + way)), sub)
                greet(tile_at(-sign * way), sub)

    ends_line = jnp.logical_or(in_line == 0, in_line == LINE - 1)

    @pl.when(crosses_up)
    def _():
        for part in range(PARTS):
            greet(tile, up_relay(part))
            greet(tile, jnp.minimum(down_relay(part) + RUN, subs - 1))

    @pl.when(crosses_down)
    def _():
        for part in range(PARTS):
            greet(tile, down_relay(part))
            greet(tile, jnp.maximum(up_relay(part) - RUN, 0))

    @pl.when(relays_up)
    def _():
        greet(tile, last_here)
        greet(tile, first_above)

    @pl.when(relays_down)
    def _():
        greet(tile, start)
        greet(tile, last_below)

    lane = lax.broadcasted_iota(jnp.int32, (ROWS, TY), 1)
    not_last = lane < TY - 1
    not_first = lane > 0
    zeros_pad = jnp.zeros((PAD, TY), jnp.float32)
    for comp in range(3):
        for plane in range(2):
            for buf in (s0, s1):
                buf[comp, plane, PAD + TX : PAD + TX + PAD, :] = zeros_pad
            for buf in (h1, h2):
                buf[comp, plane, 0:PAD, :] = zeros_pad

    def at(buf, comp, plane, row):
        return buf[comp, plane, pl.ds(PAD + row, ROWS), :]

    def put(buf, comp, plane, row, value):
        buf[comp, plane, pl.ds(PAD + row, ROWS), :] = value

    def plus_x(buf, comp, plane, row):
        return buf[comp, plane, pl.ds(PAD + row + 1, ROWS), :] - at(buf, comp, plane, row)

    def minus_x(buf, comp, plane, row):
        return at(buf, comp, plane, row) - buf[comp, plane, pl.ds(PAD + row - 1, ROWS), :]

    def plus_y(value):
        return jnp.where(not_last, pltpu.roll(value, TY - 1, 1), 0.0) - value

    def minus_y(value):
        return value - jnp.where(not_first, pltpu.roll(value, 1, 1), 0.0)

    def curl_z(buf, plane, row):
        return plus_x(buf, 1, plane, row) - plus_y(at(buf, 0, plane, row))

    ramp_lane = lane.astype(jnp.float32) + 0.5
    ramp_y = jnp.minimum(jnp.minimum(ramp_lane, TY - ramp_lane) * (1.0 / BAND), 1.0)
    row_iota = lax.broadcasted_iota(jnp.int32, (ROWS, TY), 0)

    def weight(row):
        position = (row_iota + row).astype(jnp.float32) + 0.5
        return jnp.minimum(jnp.minimum(position, TX - position) * (1.0 / BAND), 1.0) * ramp_y

    def rows_of(buf, index, row):
        return buf[index, pl.ds(row, ROWS), :]

    def depth_rows(turn, upward, first, count):
        if upward:
            return (a1, a2)[turn].at[:, first : first + count]
        return (s0, s1)[turn].at[0:2, 0, PAD + first : PAD + first + count]

    def depth_copy(turn, upward, count):
        slot = turn * 2 + int(upward)
        return pltpu.make_async_remote_copy(
            depth_rows(turn, upward, 0, count), (up_in if upward else down_in).at[turn, :, 0:count],
            depth_send.at[slot], depth_recv.at[slot],
            device_id=(tile, above if upward else below), device_id_type=MESH)

    def part_copy(turn, upward, part):
        relay = up_relay(part) if upward else down_relay(part)
        return pltpu.make_async_remote_copy(
            depth_rows(turn, upward, DIRECT + part * PART_ROWS, PART_ROWS), relay_in.at[turn],
            part_send.at[turn * PARTS + part], relay_recv.at[turn],
            device_id=(tile, relay), device_id_type=MESH)

    def relay_copy(turn, upward, part):
        target = (up_in if upward else down_in).at[
            turn, :, pl.ds(pl.multiple_of(DIRECT + part * PART_ROWS, 8), PART_ROWS)]
        return pltpu.make_async_remote_copy(
            relay_in.at[turn], target, relay_send.at[turn], part_recv.at[turn * PARTS + part],
            device_id=(tile, first_above if upward else last_below), device_id_type=MESH)

    def send_depth(turn, upward):
        crosses = crosses_up if upward else crosses_down
        plain = jnp.logical_and(has_above if upward else has_below, jnp.logical_not(crosses))

        pl.when(plain)(lambda: depth_copy(turn, upward, TX).start())

        @pl.when(crosses)
        def _():
            for part in range(PARTS):
                part_copy(turn, upward, part).start()
            depth_copy(turn, upward, DIRECT).start()

    def relay_depth(turn):
        for upward, relays in ((True, relays_up), (False, relays_down)):

            @pl.when(relays)
            def _():
                part_copy(turn, upward, 0).wait_recv()
                relay_copy(turn, upward, relay_part).start()

    def wait_depth(turn):
        for upward, crosses in ((True, crosses_down), (False, crosses_up)):
            plain = jnp.logical_and(has_below if upward else has_above, jnp.logical_not(crosses))
            pl.when(plain)(lambda: depth_copy(turn, upward, TX).wait_recv())

            @pl.when(crosses)
            def _():
                depth_copy(turn, upward, DIRECT).wait_recv()
                for part in range(PARTS):
                    relay_copy(turn, upward, part).wait_recv()

    def finish_depth(turn):
        for upward, crosses, relays in ((True, crosses_up, relays_up), (False, crosses_down, relays_down)):
            plain = jnp.logical_and(has_above if upward else has_below, jnp.logical_not(crosses))
            pl.when(plain)(lambda: depth_copy(turn, upward, TX).wait_send())

            @pl.when(crosses)
            def _():
                for part in range(PARTS):
                    part_copy(turn, upward, part).wait_send()
                depth_copy(turn, upward, DIRECT).wait_send()

            pl.when(relays)(lambda: relay_copy(turn, upward, relay_part).wait_send())

    def band_copy(kind, group, toward_next):
        first, count = GROUPS[group]
        source, target = ((yc_out, yc_in), (xn_out, xn_in), (yn_out, yn_in), (xc_out, xc_in))[kind]
        direction = int(toward_next)
        if kind in (0, 2):
            other = y_next if toward_next else y_prev
        else:
            other = x_next if toward_next else x_prev
        slot = (kind * 2 + group) * 2 + direction
        part = slice(first, first + count)
        return pltpu.make_async_remote_copy(
            source.at[direction, part], target.at[direction, part],
            band_send.at[slot], band_recv.at[slot],
            device_id=(other, sub), device_id_type=MESH)

    def way_slot(group, direction, way):
        return (group * 2 + direction) * (LINE - 1) + way - 1

    def way_copy(group, direction, way):
        part = slice(*WAYS[group][way - 1])
        sign = 1 if direction else -1
        return pltpu.make_async_remote_copy(
            xn_out.at[direction, part], xr_in.at[direction, part],
            way_send.at[way_slot(group, direction, way)], way_recv.at[group * 2 + direction],
            device_id=(tile_at(sign * (1 + way)), sub), device_id_type=MESH)

    def pass_copy(group, direction, way):
        part = slice(*WAYS[group][way - 1])
        sign = 1 if direction else -1
        return pltpu.make_async_remote_copy(
            xr_in.at[direction, part], xn_in.at[direction, part],
            pass_send.at[group * 2 + direction], pass_recv.at[way_slot(group, direction, way)],
            device_id=(tile_at(-sign * way), sub), device_id_type=MESH)

    def each_band(kind, group, role, straight, around):
        for direction in (0, 1):
            if kind != 1:
                straight(band_copy(kind, group, direction))
                continue
            pl.when(jnp.logical_not(role(direction)))(lambda: straight(band_copy(kind, group, direction)))

            @pl.when(role(direction))
            def _():
                for way in range(1, LINE):
                    around(group, direction, way)

    def send_band(kind, group):
        each_band(kind, group, sends_around, lambda copy: copy.start(), lambda *at: way_copy(*at).start())

    def wait_band(kind, group):
        each_band(kind, group, gets_around, lambda copy: copy.wait_recv(), lambda *at: pass_copy(*at).wait_recv())

    def finish_band(kind, group):
        each_band(kind, group, sends_around, lambda copy: copy.wait_send(), lambda *at: way_copy(*at).wait_send())

    def pass_bands(group):
        for direction in range(2):
            for way in range(1, LINE):

                @pl.when(passes_on(direction, way))
                def _():
                    way_copy(group, direction, way).wait_recv()
                    pass_copy(group, direction, way).start()

    def finish_passing(group):
        for direction in range(2):
            for way in range(1, LINE):
                pl.when(passes_on(direction, way))(lambda: pass_copy(group, direction, way).wait_send())

    for number in (3, 4, 0, 1):
        loads[number].wait()
    d0, d1, d2, d3 = (decay[i] for i in range(4))
    c0, c1, c2, c3 = (coupling[i] for i in range(4))

    def scale(row):
        for plane in range(2):
            label = mat[plane, pl.ds(row, ROWS), :]
            is0, is1, is2 = label == 0, label == 1, label == 2
            couple = jnp.where(is0, c0, jnp.where(is1, c1, jnp.where(is2, c2, c3)))
            cb[plane, pl.ds(row, ROWS), :] = couple
            ca[plane, pl.ds(row, ROWS), :] = jnp.where(is0, d0, jnp.where(is1, d1, jnp.where(is2, d2, d3)))
            for comp in range(3):
                put(s0, comp, plane, row, couple * at(field, comp, plane, row))

    row_tiles(scale)
    count = lambda flag, number: jnp.where(flag, number, 0)
    crosses_any = jnp.logical_or(crosses_up, crosses_down)
    relays_any = jnp.logical_or(relays_up, relays_down)
    pl.semaphore_wait(
        barrier, 4 + jnp.where(ends_line, 8, 4) + count(has_below, 1) + count(has_above, 1) + count(crosses_any, 2 * PARTS) + count(relays_any, 2))
    send_depth(0, False)
    loads[2].wait()

    def partial(hbuf, offset, sbuf, abuf):
        def body(row):
            s_x, s_y, s_z = (at(sbuf, comp, 1, row) for comp in range(3))
            abuf[0, pl.ds(row, ROWS), :] = at(hbuf, offset, 1, row) + plus_y(s_z) + s_y
            abuf[1, pl.ds(row, ROWS), :] = at(hbuf, offset + 1, 1, row) - s_x - plus_x(sbuf, 2, 1, row)

        row_tiles(body)

    partial(field, HX, s0, a1)
    send_depth(0, True)

    def magnetic_local(hbuf, offset, sbuf, row):
        s_x0, s_y0, s_z0 = (at(sbuf, comp, 0, row) for comp in range(3))
        new_x = at(hbuf, offset, 0, row) + plus_y(s_z0) - (at(sbuf, 1, 1, row) - s_y0)
        new_y = at(hbuf, offset + 1, 0, row) + (at(sbuf, 0, 1, row) - s_x0) - plus_x(sbuf, 2, 0, row)
        new_z = at(hbuf, offset + 2, 0, row) + curl_z(sbuf, 0, row)
        new_z1 = at(hbuf, offset + 2, 1, row) + curl_z(sbuf, 1, row)
        return new_x, new_y, new_z, new_z1

    def first_local(row):
        new_x, new_y, new_z, new_z1 = magnetic_local(field, HX, s0, row)
        put(h1, 0, 0, row, new_x)
        put(h1, 1, 0, row, new_y)
        put(h1, 2, 0, row, new_z)
        put(h1, 2, 1, row, new_z1)

    row_tiles(first_local)

    def edge_planes(turn, sbuf):
        @pl.when(jnp.logical_not(has_above))
        def _():
            def body(row):
                for comp in range(2):
                    down_in[turn, comp, pl.ds(row, ROWS), :] = jnp.zeros((ROWS, TY), jnp.float32)

            row_tiles(body)

        @pl.when(jnp.logical_not(has_below))
        def _():
            def body(row):
                up_in[turn, 0, pl.ds(row, ROWS), :] = at(sbuf, 1, 0, row)
                up_in[turn, 1, pl.ds(row, ROWS), :] = -at(sbuf, 0, 0, row)

            row_tiles(body)

    def magnetic_rest(turn, abuf, sbuf, row):
        new_x = rows_of(abuf, 0, row) - down_in[turn, 1, pl.ds(row, ROWS), :]
        new_y = rows_of(abuf, 1, row) + down_in[turn, 0, pl.ds(row, ROWS), :]
        under_x = up_in[turn, 0, pl.ds(row, ROWS), :] - at(sbuf, 1, 0, row)
        under_y = up_in[turn, 1, pl.ds(row, ROWS), :] + at(sbuf, 0, 0, row)
        return new_x, new_y, under_x, under_y

    def electric_xy(ebuf, hbuf, plane, row, h_x, h_y, under_x, under_y):
        h_z = at(hbuf, 2, plane, row)
        decays = rows_of(ca, plane, row)
        new_x = decays * at(ebuf, 0, plane, row) - MAGNETIC * (minus_y(h_z) - (h_y - under_y))
        new_y = decays * at(ebuf, 1, plane, row) - MAGNETIC * ((h_x - under_x) - minus_x(hbuf, 2, plane, row))
        return new_x, new_y

    def electric_z(ebuf, hbuf, plane, row, h_x):
        decays = rows_of(ca, plane, row)
        return decays * at(ebuf, 2, plane, row) - MAGNETIC * (minus_x(hbuf, 1, plane, row) - minus_y(h_x))

    edge_planes(0, s0)
    relay_depth(0)
    wait_depth(0)

    def first_rest(row):
        x1, y1, under_x, under_y = magnetic_rest(0, a1, s0, row)
        put(h1, 0, 1, row, x1)
        put(h1, 1, 1, row, y1)
        x0, y0 = at(h1, 0, 0, row), at(h1, 1, 0, row)
        for plane, (h_x, h_y, b_x, b_y) in enumerate(((x0, y0, under_x, under_y), (x1, y1, x0, y0))):
            new = (*electric_xy(field, h1, plane, row, h_x, h_y, b_x, b_y), electric_z(field, h1, plane, row, h_x))
            couple = rows_of(cb, plane, row)
            for comp in range(3):
                put(e1, comp, plane, row, new[comp])
                put(s1, comp, plane, row, couple * new[comp])

    row_tiles(first_rest)
    send_depth(1, False)
    partial(h1, 0, s1, a2)
    send_depth(1, True)

    def keep(name, row, value, weights):
        w[ORDER.index(name), pl.ds(row, ROWS), :] = value * weights

    def second_local(row):
        new_x, new_y, new_z, new_z1 = magnetic_local(h1, 0, s1, row)
        put(h2, 0, 0, row, new_x)
        put(h2, 1, 0, row, new_y)
        put(h2, 2, 0, row, new_z)
        put(h2, 2, 1, row, new_z1)
        weights = weight(row)
        keep((HX, 0), row, new_x, weights)
        keep((HY, 0), row, new_y, weights)
        keep((HZ, 0), row, new_z, weights)
        keep((HZ, 1), row, new_z1, weights)
        keep((EZ, 0), row, electric_z(e1, h2, 0, row, new_x), weights)

    row_tiles(second_local)

    def slot_of(rows):
        return lax.broadcasted_iota(jnp.int32, (rows, TY), 1) // BAND

    def pack_lanes(values):
        slot = slot_of(values[0].shape[0])
        turned = [values[0]] + [pltpu.roll(values[k], BAND * k, 1) for k in (1, 2, 3)]
        low, high = turned[3], turned[0]
        for k in (2, 1, 0):
            low = jnp.where(slot == k, turned[k], low)
            high = jnp.where(slot == k, turned[k + 1], high)
        return low, high

    def unpack_lanes(low_side, high_side):
        slot = slot_of(low_side.shape[0])
        turned = []
        for k in range(4):
            mixed = jnp.where(slot == (k + 3) % 4, low_side, high_side)
            shift = (TY - BAND * (k - 1)) % TY
            turned.append(pltpu.roll(mixed, shift, 1) if shift else mixed)
        return [jnp.where(slot == 0, turned[k], jnp.where(slot == 3, turned[(k + 2) % 4], 0.0)) for k in range(4)]

    corner_rows = (0, 16, TX - 32, TX - 16)
    middle_rows = (32, 80, 128, 176)

    def middle_lanes():
        slot = slot_of(16)
        return jnp.logical_or(slot == 1, slot == 2)

    def pack_corners(index):
        values = [w[index, first : first + 16, :] for first in corner_rows]
        low, high = pack_lanes(values)
        yc_out[0, index], yc_out[1, index] = low, high
        middle = middle_lanes()
        for direction in range(2):
            xn_out[direction, index] = jnp.where(
                middle, values[2 * direction], pltpu.roll(values[2 * direction + 1], TY // 2, 1))

    def pack_middle(index):
        low, high = pack_lanes([w[index, first : first + 48, :] for first in middle_rows])
        yn_out[0, index], yn_out[1, index] = low, high

    def add_corners(index):
        added = unpack_lanes(yc_in[1, index], yc_in[0, index])
        values = []
        for first, more in zip(corner_rows, added):
            total = w[index, first : first + 16, :] + more
            w[index, first : first + 16, :] = total
            values.append(total)
        middle = middle_lanes()
        for direction in range(2):
            xc_out[direction, index] = jnp.where(
                middle, pltpu.roll(values[2 * direction + 1], TY // 2, 1), values[2 * direction])

    def add_middle(index):
        added = unpack_lanes(yn_in[1, index], yn_in[0, index])
        for first, more in zip(middle_rows, added):
            w[index, first : first + 48, :] += more

    def add_x_bands(index):
        middle = middle_lanes()
        for side_of, first in ((1, 0), (0, TX - 32)):
            plain, summed = xn_in[side_of, index], xc_in[side_of, index]
            w[index, first : first + 16, :] += jnp.where(middle, plain, summed)
            w[index, first + 16 : first + 32, :] += pltpu.roll(jnp.where(middle, summed, plain), TY // 2, 1)

    def send_group(group):
        planes_of(group, pack_corners)
        send_band(0, group)
        send_band(1, group)
        planes_of(group, pack_middle)
        send_band(2, group)

    send_group(0)
    relay_depth(1)
    edge_planes(1, s1)
    wait_depth(1)

    def second_rest(row):
        x1, y1, under_x, under_y = magnetic_rest(1, a2, s1, row)
        put(h2, 0, 1, row, x1)
        put(h2, 1, 1, row, y1)
        x0, y0 = at(h2, 0, 0, row), at(h2, 1, 0, row)
        weights = weight(row)
        keep((HX, 1), row, x1, weights)
        keep((HY, 1), row, y1, weights)
        for plane, (h_x, h_y, b_x, b_y) in enumerate(((x0, y0, under_x, under_y), (x1, y1, x0, y0))):
            new_x, new_y = electric_xy(e1, h2, plane, row, h_x, h_y, b_x, b_y)
            keep((EX, plane), row, new_x, weights)
            keep((EY, plane), row, new_y, weights)
        keep((EZ, 1), row, electric_z(e1, h2, 1, row, x1), weights)

    row_tiles(second_rest)
    send_group(1)

    for group in range(2):
        pass_bands(group)
        wait_band(0, group)
        planes_of(group, add_corners)
        send_band(3, group)

    for group in range(2):
        wait_band(2, group)
        planes_of(group, add_middle)
        wait_band(1, group)
        wait_band(3, group)
        planes_of(group, add_x_bands)

    for turn in range(2):
        finish_depth(turn)
    for group in range(2):
        for kind in range(4):
            finish_band(kind, group)
        finish_passing(group)


def place(planes, out, sems):
    copies = [
        pltpu.make_async_copy(planes.at[index], out.at[0, comp, plane], sems.at[index])
        for index, (comp, plane) in enumerate(ORDER)
    ]
    for copy in copies:
        copy.start()
    for copy in copies:
        copy.wait()


def on_device(tiles, subs, seeds, material, decay, coupling):
    f32 = jnp.float32
    padded = (3, 2, PAD + TX + PAD, TY)
    planes = len(ORDER)
    narrow, wide = pltpu.VMEM((2, planes, 16, TY), f32), pltpu.VMEM((2, planes, 48, TY), f32)
    hbm = pl.BlockSpec(memory_space=pltpu.HBM)
    done = pl.pallas_call(
        functools.partial(kernel, tiles, subs),
        out_shape=jax.ShapeDtypeStruct((planes, TX, TY), f32),
        in_specs=[hbm] * 4,
        out_specs=pl.BlockSpec(memory_space=pltpu.VMEM),
        scratch_shapes=[
            pltpu.SMEM(decay.shape, f32),
            pltpu.SMEM(coupling.shape, f32),
            pltpu.VMEM((6, *padded[1:]), f32),
            pltpu.VMEM((2, TX, TY), jnp.int32),
            pltpu.VMEM((2, TX, TY), f32),
            pltpu.VMEM((2, TX, TY), f32),
            *[pltpu.VMEM(padded, f32)] * 5,
            pltpu.VMEM((2, TX, TY), f32),
            pltpu.VMEM((2, TX, TY), f32),
            pltpu.VMEM((2, 2, TX, TY), f32),
            pltpu.VMEM((2, 2, TX, TY), f32),
            pltpu.VMEM((2, 2, PART_ROWS, TY), f32),
            narrow,
            narrow, wide, narrow, narrow,
            narrow, wide, narrow, narrow,
            pltpu.SemaphoreType.DMA((5,)),
            pltpu.SemaphoreType.DMA((4,)),
            pltpu.SemaphoreType.DMA((4,)),
            pltpu.SemaphoreType.DMA((2 * PARTS,)),
            pltpu.SemaphoreType.DMA((2 * PARTS,)),
            pltpu.SemaphoreType.DMA((2,)),
            pltpu.SemaphoreType.DMA((2,)),
            pltpu.SemaphoreType.DMA((16,)),
            pltpu.SemaphoreType.DMA((16,)),
            pltpu.SemaphoreType.DMA((4 * (LINE - 1),)),
            pltpu.SemaphoreType.DMA((4,)),
            pltpu.SemaphoreType.DMA((4,)),
            pltpu.SemaphoreType.DMA((4 * (LINE - 1),)),
        ],
        compiler_params=pltpu.CompilerParams(
            collective_id=0, has_side_effects=True, vmem_limit_bytes=20 * 2**20),
    )(*(pltpu.with_memory_space_constraint(array, pltpu.HBM) for array in (decay, coupling, seeds, material)))
    return pl.pallas_call(
        place,
        out_shape=jax.ShapeDtypeStruct(seeds.shape, f32),
        in_specs=[pl.BlockSpec(memory_space=pltpu.VMEM)],
        out_specs=hbm,
        scratch_shapes=[pltpu.SemaphoreType.DMA((planes,))],
        compiler_params=pltpu.CompilerParams(vmem_limit_bytes=4 * 2**20),
    )(done)


def solution(mesh):
    placed = (P("tile", None, "sub", None, None), P("tile", "sub", None, None), P(), P())
    return jax.shard_map(
        functools.partial(on_device, mesh.shape["tile"], mesh.shape["sub"]),
        mesh=mesh,
        in_specs=placed,
        out_specs=P("tile", None, "sub", None, None),
        check_vma=False,
    )
```

```python
import functools
import math

import jax
import jax.numpy as jnp
from jax import lax
from jax.experimental import pallas as pl
from jax.experimental.pallas import tpu as pltpu
from jax.sharding import PartitionSpec as P

BAND = 32
MESH = pl.DeviceIdType.MESH
MAGNETIC = 0.5
TX = 256
TY = 128
PAD = 8
ROWS = 32
EX, EY, EZ, HX, HY, HZ = range(6)

EARLY = ((HX, 0), (HY, 0), (HZ, 0), (HZ, 1), (EZ, 0))
LATE = ((HX, 1), (HY, 1), (EX, 0), (EY, 0), (EX, 1), (EY, 1), (EZ, 1))
ORDER = EARLY + LATE
GROUPS = ((0, len(EARLY)), (len(EARLY), len(LATE)))

RUN = 8
PARTS = 3
DIRECT = 104
PIECES = (((104, 40), (144, 40), (184, 72)), ((104, 72), (176, 40), (216, 40)))
MOST = 72


def row_tiles(body):
    def step(index, carry):
        body(pl.multiple_of(index * ROWS, ROWS))
        return carry

    lax.fori_loop(0, TX // ROWS, step, 0, unroll=2)


def planes_of(group, body):
    first, count = GROUPS[group]

    def step(index, carry):
        body(index)
        return carry

    lax.fori_loop(first, first + count, step, 0, unroll=True)


def kernel(
    tiles, subs, decay_in, coupling_in, seeds, material, w,
    decay, coupling, field, mat, ca, cb, s0, s1, h1, h2, e1, decayed, under, mixed,
    up_out0, up_out1, down_out0, down_out1, up_in0, up_in1, down_in0, down_in1, relay_in0, relay_in1,
    yc_out, yn_out, xn_out, xc_out, yc_in, yn_in, xn_in, xc_in,
    load_sem, depth_send, depth_recv, part_send, part_recv, relay_recv, relay_send, band_send, band_recv,
):
    tile = lax.axis_index("tile")
    sub = lax.axis_index("sub")
    side = math.isqrt(tiles)
    has_below = sub > 0
    has_above = sub < subs - 1
    below = jnp.maximum(sub - 1, 0)
    above = jnp.minimum(sub + 1, subs - 1)
    x_prev = lax.rem(tile + tiles - 1, tiles)
    x_next = lax.rem(tile + 1, tiles)
    y_prev = lax.rem(tile + tiles - side, tiles)
    y_next = lax.rem(tile + side, tiles)

    loads = [
        pltpu.make_async_copy(material.at[0], mat, load_sem.at[0]),
        pltpu.make_async_copy(seeds.at[0, 0:3], field.at[0:3, :, PAD : PAD + TX], load_sem.at[1]),
        pltpu.make_async_copy(seeds.at[0, 3:6], field.at[3:6, :, PAD : PAD + TX], load_sem.at[2]),
        pltpu.make_async_copy(decay_in, decay, load_sem.at[3]),
        pltpu.make_async_copy(coupling_in, coupling, load_sem.at[4]),
    ]
    for load in loads:
        load.start()

    barrier = pltpu.get_barrier_semaphore()

    def greet(other_tile, other_sub):
        pl.semaphore_signal(barrier, inc=1, device_id=(other_tile, other_sub), device_id_type=MESH)

    for other in (x_prev, x_next, y_prev, y_next):
        greet(other, sub)
    pl.when(has_below)(lambda: greet(tile, below))
    pl.when(has_above)(lambda: greet(tile, above))
    place_in_run = lax.rem(sub, RUN)
    start = sub - place_in_run
    run_above = start + RUN < subs
    run_below = start > 0
    crosses_up = jnp.logical_and(place_in_run == RUN - 1, run_above)
    crosses_down = jnp.logical_and(place_in_run == 0, run_below)
    odd = lax.rem(place_in_run, 2) == 1
    relays_up = jnp.logical_and(jnp.logical_and(odd, place_in_run < RUN - 1), run_above)
    relays_down = jnp.logical_and(jnp.logical_and(jnp.logical_not(odd), place_in_run > 0), run_below)

    def relays(upward, part):
        return jnp.logical_and(place_in_run == 2 * part + (1 if upward else 2), run_above if upward else run_below)

    last_here = start + RUN - 1
    first_above = jnp.minimum(start + RUN, subs - 1)
    last_below = jnp.maximum(start - 1, 0)

    def up_relay(part):
        return start + 2 * part + 1

    def down_relay(part):
        return start + 2 * part + 2

    @pl.when(crosses_up)
    def _():
        for part in range(PARTS):
            greet(tile, up_relay(part))
            greet(tile, jnp.minimum(down_relay(part) + RUN, subs - 1))

    @pl.when(crosses_down)
    def _():
        for part in range(PARTS):
            greet(tile, down_relay(part))
            greet(tile, jnp.maximum(up_relay(part) - RUN, 0))

    @pl.when(relays_up)
    def _():
        greet(tile, last_here)
        greet(tile, first_above)

    @pl.when(relays_down)
    def _():
        greet(tile, start)
        greet(tile, last_below)

    lane = lax.broadcasted_iota(jnp.int32, (ROWS, TY), 1)
    not_last = lane < TY - 1
    not_first = lane > 0
    zeros_pad = jnp.zeros((PAD, TY), jnp.float32)
    for comp in range(3):
        for plane in range(2):
            for buf in (s0, s1):
                buf[comp, plane, PAD + TX : PAD + TX + PAD, :] = zeros_pad
            for buf in (h1, h2):
                buf[comp, plane, 0:PAD, :] = zeros_pad
    for buf in (decayed, mixed):
        buf[0, 0, PAD + TX : PAD + TX + PAD, :] = zeros_pad
    under[1, 0, 0:PAD, :] = zeros_pad
    up_out, down_out = (up_out0, up_out1), (down_out0, down_out1)
    up_in, down_in, relay_in = (up_in0, up_in1), (down_in0, down_in1), (relay_in0, relay_in1)

    def at(buf, comp, plane, row):
        return buf[comp, plane, pl.ds(PAD + row, ROWS), :]

    def put(buf, comp, plane, row, value):
        buf[comp, plane, pl.ds(PAD + row, ROWS), :] = value

    def plus_x(buf, comp, plane, row):
        return buf[comp, plane, pl.ds(PAD + row + 1, ROWS), :] - at(buf, comp, plane, row)

    def minus_x(buf, comp, plane, row):
        return at(buf, comp, plane, row) - buf[comp, plane, pl.ds(PAD + row - 1, ROWS), :]

    def plus_y(value):
        return jnp.where(not_last, pltpu.roll(value, TY - 1, 1), 0.0) - value

    def minus_y(value):
        return value - jnp.where(not_first, pltpu.roll(value, 1, 1), 0.0)

    def curl_z(buf, plane, row):
        return plus_x(buf, 1, plane, row) - plus_y(at(buf, 0, plane, row))

    ramp_lane = lane.astype(jnp.float32) + 0.5
    ramp_y = jnp.minimum(jnp.minimum(ramp_lane, TY - ramp_lane) * (1.0 / BAND), 1.0)
    row_iota = lax.broadcasted_iota(jnp.int32, (ROWS, TY), 0)

    def weight(row):
        position = (row_iota + row).astype(jnp.float32) + 0.5
        return jnp.minimum(jnp.minimum(position, TX - position) * (1.0 / BAND), 1.0) * ramp_y

    def rows_of(buf, index, row):
        return buf[index, pl.ds(row, ROWS), :]

    def depth_rows(turn, upward, first, count):
        return (up_out if upward else down_out)[turn].at[:, first : first + count]

    def depth_copy(turn, upward, count):
        slot = turn * 2 + int(upward)
        return pltpu.make_async_remote_copy(
            depth_rows(turn, upward, 0, count), (up_in if upward else down_in)[turn].at[:, 0:count],
            depth_send.at[slot], depth_recv.at[slot],
            device_id=(tile, above if upward else below), device_id_type=MESH)

    def part_copy(turn, upward, part):
        relay = up_relay(part) if upward else down_relay(part)
        first, count = PIECES[int(upward)][part]
        return pltpu.make_async_remote_copy(
            depth_rows(turn, upward, first, count), relay_in[turn].at[:, 0:count],
            part_send.at[turn * PARTS + part], relay_recv.at[turn],
            device_id=(tile, relay), device_id_type=MESH)

    def relay_copy(turn, upward, part):
        first, count = PIECES[int(upward)][part]
        return pltpu.make_async_remote_copy(
            relay_in[turn].at[:, 0:count], (up_in if upward else down_in)[turn].at[:, first : first + count],
            relay_send.at[turn], part_recv.at[turn * PARTS + part],
            device_id=(tile, first_above if upward else last_below), device_id_type=MESH)

    def send_depth(turn, upward):
        crosses = crosses_up if upward else crosses_down
        plain = jnp.logical_and(has_above if upward else has_below, jnp.logical_not(crosses))

        pl.when(plain)(lambda: depth_copy(turn, upward, TX).start())

        @pl.when(crosses)
        def _():
            for part in (1, 0, 2) if not upward else (1, 2, 0):
                part_copy(turn, upward, part).start()
            depth_copy(turn, upward, DIRECT).start()

    def relay_depth(turn):
        for upward in (True, False):
            for part in range(PARTS):

                @pl.when(relays(upward, part))
                def _():
                    part_copy(turn, upward, part).wait_recv()
                    relay_copy(turn, upward, part).start()

    def wait_depth(turn):
        for upward, crosses in ((True, crosses_down), (False, crosses_up)):
            plain = jnp.logical_and(has_below if upward else has_above, jnp.logical_not(crosses))
            pl.when(plain)(lambda: depth_copy(turn, upward, TX).wait_recv())

            @pl.when(crosses)
            def _():
                depth_copy(turn, upward, DIRECT).wait_recv()
                for part in range(PARTS):
                    relay_copy(turn, upward, part).wait_recv()

    def finish_depth(turn):
        for upward, crosses in ((True, crosses_up), (False, crosses_down)):
            plain = jnp.logical_and(has_above if upward else has_below, jnp.logical_not(crosses))
            pl.when(plain)(lambda: depth_copy(turn, upward, TX).wait_send())

            @pl.when(crosses)
            def _():
                for part in range(PARTS):
                    part_copy(turn, upward, part).wait_send()
                depth_copy(turn, upward, DIRECT).wait_send()

            for part in range(PARTS):
                pl.when(relays(upward, part))(lambda: relay_copy(turn, upward, part).wait_send())

    def band_copy(kind, group, toward_next):
        first, count = GROUPS[group]
        source, target = ((yc_out, yc_in), (xn_out, xn_in), (yn_out, yn_in), (xc_out, xc_in))[kind]
        direction = int(toward_next)
        if kind in (0, 2):
            other = y_next if toward_next else y_prev
        else:
            other = x_next if toward_next else x_prev
        slot = (kind * 2 + group) * 2 + direction
        part = slice(first, first + count)
        return pltpu.make_async_remote_copy(
            source.at[direction, part], target.at[direction, part],
            band_send.at[slot], band_recv.at[slot],
            device_id=(other, sub), device_id_type=MESH)

    def send_band(kind, group):
        for toward_next in (False, True):
            band_copy(kind, group, toward_next).start()

    def wait_band(kind, group):
        for toward_next in (False, True):
            band_copy(kind, group, toward_next).wait_recv()

    for number in (3, 4, 0, 1):
        loads[number].wait()
    d0, d1, d2, d3 = (decay[i] for i in range(4))
    c0, c1, c2, c3 = (coupling[i] for i in range(4))

    def scale(row):
        for plane in range(2):
            label = mat[plane, pl.ds(row, ROWS), :]
            is0, is1, is2 = label == 0, label == 1, label == 2
            couple = jnp.where(is0, c0, jnp.where(is1, c1, jnp.where(is2, c2, c3)))
            decays = jnp.where(is0, d0, jnp.where(is1, d1, jnp.where(is2, d2, d3)))
            cb[plane, pl.ds(row, ROWS), :] = couple
            ca[plane, pl.ds(row, ROWS), :] = decays
            (down_out, up_out)[plane][1][2, pl.ds(row, ROWS), :] = couple
            scaled = [couple * at(field, comp, plane, row) for comp in range(3)]
            for comp in range(3):
                put(s0, comp, plane, row, scaled[comp])
            if plane == 0:
                for comp in range(2):
                    down_out[0][comp, pl.ds(row, ROWS), :] = scaled[comp]
            else:
                put(decayed, 0, 0, row, decays * scaled[2])

    row_tiles(scale)
    count = lambda flag, number: jnp.where(flag, number, 0)
    crosses_any = jnp.logical_or(crosses_up, crosses_down)
    relays_any = jnp.logical_or(relays_up, relays_down)
    pl.semaphore_wait(
        barrier, 4 + count(has_below, 1) + count(has_above, 1) + count(crosses_any, 2 * PARTS) + count(relays_any, 2))
    send_depth(0, False)
    loads[2].wait()

    def without_above(hbuf, offset, sbuf, row):
        s_x, s_y, s_z = (at(sbuf, comp, 1, row) for comp in range(3))
        part_x = at(hbuf, offset, 1, row) + plus_y(s_z) + s_y
        part_y = at(hbuf, offset + 1, 1, row) - s_x - plus_x(sbuf, 2, 1, row)
        return part_x, part_y

    def first_partial(row):
        up_out[0][0, pl.ds(row, ROWS), :], up_out[0][1, pl.ds(row, ROWS), :] = without_above(field, HX, s0, row)

    row_tiles(first_partial)
    send_depth(0, True)

    def magnetic_local(hbuf, offset, sbuf, row):
        s_x0, s_y0, s_z0 = (at(sbuf, comp, 0, row) for comp in range(3))
        new_x = at(hbuf, offset, 0, row) + plus_y(s_z0) - (at(sbuf, 1, 1, row) - s_y0)
        new_y = at(hbuf, offset + 1, 0, row) + (at(sbuf, 0, 1, row) - s_x0) - plus_x(sbuf, 2, 0, row)
        new_z = at(hbuf, offset + 2, 0, row) + curl_z(sbuf, 0, row)
        new_z1 = at(hbuf, offset + 2, 1, row) + curl_z(sbuf, 1, row)
        return new_x, new_y, new_z, new_z1

    def first_local(row):
        new_x, new_y, new_z, new_z1 = magnetic_local(field, HX, s0, row)
        put(h1, 0, 0, row, new_x)
        put(h1, 1, 0, row, new_y)
        put(h1, 2, 0, row, new_z)
        put(h1, 2, 1, row, new_z1)

    row_tiles(first_local)

    def second_terms(row):
        h_x, h_y = at(h1, 0, 0, row), at(h1, 1, 0, row)
        decays, couple = rows_of(ca, 1, row), rows_of(cb, 1, row)
        part_x = decays * at(field, EX, 1, row) - MAGNETIC * (minus_y(at(h1, 2, 1, row)) + h_y)
        part_y = decays * at(field, EY, 1, row) + MAGNETIC * (h_x + minus_x(h1, 2, 1, row))
        up_out[1][0, pl.ds(row, ROWS), :] = plus_y(at(decayed, 0, 0, row)) + couple * part_y
        up_out[1][1, pl.ds(row, ROWS), :] = -couple * part_x - plus_x(decayed, 0, 0, row)
        decays, couple = rows_of(ca, 0, row), rows_of(cb, 0, row)
        down_out[1][0, pl.ds(row, ROWS), :] = couple * (
            decays * at(field, EX, 0, row) - MAGNETIC * (minus_y(at(h1, 2, 0, row)) - h_y))
        down_out[1][1, pl.ds(row, ROWS), :] = couple * (
            decays * at(field, EY, 0, row) - MAGNETIC * (h_x - minus_x(h1, 2, 0, row)))

    row_tiles(second_terms)
    send_depth(1, False)
    send_depth(1, True)

    @pl.when(jnp.logical_not(has_above))
    def _():
        def clear(row):
            for buf in down_in:
                for comp in range(buf.shape[0]):
                    buf[comp, pl.ds(row, ROWS), :] = jnp.zeros((ROWS, TY), jnp.float32)

        row_tiles(clear)

    @pl.when(jnp.logical_not(has_below))
    def _():
        def cancel(row):
            up_in[0][0, pl.ds(row, ROWS), :] = at(s0, 1, 0, row)
            up_in[0][1, pl.ds(row, ROWS), :] = -at(s0, 0, 0, row)
            for comp in range(3):
                up_in[1][comp, pl.ds(row, ROWS), :] = jnp.zeros((ROWS, TY), jnp.float32)

        row_tiles(cancel)

    def electric_xy(ebuf, hbuf, plane, row, h_x, h_y, under_x, under_y):
        h_z = at(hbuf, 2, plane, row)
        decays = rows_of(ca, plane, row)
        new_x = decays * at(ebuf, 0, plane, row) - MAGNETIC * (minus_y(h_z) - (h_y - under_y))
        new_y = decays * at(ebuf, 1, plane, row) - MAGNETIC * ((h_x - under_x) - minus_x(hbuf, 2, plane, row))
        return new_x, new_y

    def electric_z(ebuf, hbuf, plane, row, h_x):
        decays = rows_of(ca, plane, row)
        return decays * at(ebuf, 2, plane, row) - MAGNETIC * (minus_x(hbuf, 1, plane, row) - minus_y(h_x))

    relay_depth(0)
    wait_depth(0)
    relay_depth(1)

    def first_rest(row):
        x1 = rows_of(up_out[0], 0, row) - rows_of(down_in[0], 1, row)
        y1 = rows_of(up_out[0], 1, row) + rows_of(down_in[0], 0, row)
        under_x = rows_of(up_in[0], 0, row) - at(s0, 1, 0, row)
        under_y = rows_of(up_in[0], 1, row) + at(s0, 0, 0, row)
        put(h1, 0, 1, row, x1)
        put(h1, 1, 1, row, y1)
        put(under, 0, 0, row, under_x)
        put(under, 1, 0, row, under_y)
        x0, y0 = at(h1, 0, 0, row), at(h1, 1, 0, row)
        for plane, (h_x, h_y, b_x, b_y) in enumerate(((x0, y0, under_x, under_y), (x1, y1, x0, y0))):
            new = (*electric_xy(field, h1, plane, row, h_x, h_y, b_x, b_y), electric_z(field, h1, plane, row, h_x))
            couple = rows_of(cb, plane, row)
            for comp in range(3):
                put(e1, comp, plane, row, new[comp])
                put(s1, comp, plane, row, couple * new[comp])

    row_tiles(first_rest)

    def keep(name, row, value, weights):
        w[ORDER.index(name), pl.ds(row, ROWS), :] = value * weights

    def second_local(row):
        new_x, new_y, new_z, new_z1 = magnetic_local(h1, 0, s1, row)
        put(h2, 0, 0, row, new_x)
        put(h2, 1, 0, row, new_y)
        put(h2, 2, 0, row, new_z)
        put(h2, 2, 1, row, new_z1)
        weights = weight(row)
        keep((HX, 0), row, new_x, weights)
        keep((HY, 0), row, new_y, weights)
        keep((HZ, 0), row, new_z, weights)
        keep((HZ, 1), row, new_z1, weights)
        keep((EZ, 0), row, electric_z(e1, h2, 0, row, new_x), weights)

    row_tiles(second_local)

    def slot_of(rows):
        return lax.broadcasted_iota(jnp.int32, (rows, TY), 1) // BAND

    def pack_lanes(values):
        slot = slot_of(values[0].shape[0])
        turned = [values[0]] + [pltpu.roll(values[k], BAND * k, 1) for k in (1, 2, 3)]
        low, high = turned[3], turned[0]
        for k in (2, 1, 0):
            low = jnp.where(slot == k, turned[k], low)
            high = jnp.where(slot == k, turned[k + 1], high)
        return low, high

    def unpack_lanes(low_side, high_side):
        slot = slot_of(low_side.shape[0])
        turned = []
        for k in range(4):
            mixed = jnp.where(slot == (k + 3) % 4, low_side, high_side)
            shift = (TY - BAND * (k - 1)) % TY
            turned.append(pltpu.roll(mixed, shift, 1) if shift else mixed)
        return [jnp.where(slot == 0, turned[k], jnp.where(slot == 3, turned[(k + 2) % 4], 0.0)) for k in range(4)]

    corner_rows = (0, 16, TX - 32, TX - 16)
    middle_rows = (32, 80, 128, 176)

    def middle_lanes():
        slot = slot_of(16)
        return jnp.logical_or(slot == 1, slot == 2)

    def pack_corners(index):
        values = [w[index, first : first + 16, :] for first in corner_rows]
        low, high = pack_lanes(values)
        yc_out[0, index], yc_out[1, index] = low, high
        middle = middle_lanes()
        for direction in range(2):
            xn_out[direction, index] = jnp.where(
                middle, values[2 * direction], pltpu.roll(values[2 * direction + 1], TY // 2, 1))

    def pack_middle(index):
        low, high = pack_lanes([w[index, first : first + 48, :] for first in middle_rows])
        yn_out[0, index], yn_out[1, index] = low, high

    def add_corners(index):
        added = unpack_lanes(yc_in[1, index], yc_in[0, index])
        values = []
        for first, more in zip(corner_rows, added):
            total = w[index, first : first + 16, :] + more
            w[index, first : first + 16, :] = total
            values.append(total)
        middle = middle_lanes()
        for direction in range(2):
            xc_out[direction, index] = jnp.where(
                middle, pltpu.roll(values[2 * direction + 1], TY // 2, 1), values[2 * direction])

    def add_middle(index):
        added = unpack_lanes(yn_in[1, index], yn_in[0, index])
        for first, more in zip(middle_rows, added):
            w[index, first : first + 48, :] += more

    def add_x_bands(index):
        middle = middle_lanes()
        for side_of, first in ((1, 0), (0, TX - 32)):
            plain, summed = xn_in[side_of, index], xc_in[side_of, index]
            w[index, first : first + 16, :] += jnp.where(middle, plain, summed)
            w[index, first + 16 : first + 32, :] += pltpu.roll(jnp.where(middle, summed, plain), TY // 2, 1)

    def send_group(group):
        planes_of(group, pack_corners)
        send_band(0, group)
        send_band(1, group)
        planes_of(group, pack_middle)
        send_band(2, group)

    send_group(0)
    wait_depth(1)

    def mix(row):
        turn_z = minus_x(under, 1, 0, row) - minus_y(at(under, 0, 0, row))
        put(mixed, 0, 0, row, MAGNETIC * rows_of(up_in[1], 2, row) * turn_z)

    row_tiles(mix)

    def second_rest(row):
        x1, y1 = without_above(h1, 0, s1, row)
        couple = MAGNETIC * rows_of(down_in[1], 2, row)
        x1 -= rows_of(down_in[1], 1, row) + couple * at(h1, 0, 1, row)
        y1 += rows_of(down_in[1], 0, row) - couple * at(h1, 1, 1, row)
        couple = MAGNETIC * rows_of(up_in[1], 2, row)
        under_x, under_y = at(under, 0, 0, row), at(under, 1, 0, row)
        under_x += rows_of(up_in[1], 0, row) - couple * under_x - plus_y(at(mixed, 0, 0, row)) - at(s1, 1, 0, row)
        under_y += rows_of(up_in[1], 1, row) - couple * under_y + plus_x(mixed, 0, 0, row) + at(s1, 0, 0, row)
        under_x = jnp.where(has_below, under_x, 0.0)
        under_y = jnp.where(has_below, under_y, 0.0)
        put(h2, 0, 1, row, x1)
        put(h2, 1, 1, row, y1)
        x0, y0 = at(h2, 0, 0, row), at(h2, 1, 0, row)
        weights = weight(row)
        keep((HX, 1), row, x1, weights)
        keep((HY, 1), row, y1, weights)
        for plane, (h_x, h_y, b_x, b_y) in enumerate(((x0, y0, under_x, under_y), (x1, y1, x0, y0))):
            new_x, new_y = electric_xy(e1, h2, plane, row, h_x, h_y, b_x, b_y)
            keep((EX, plane), row, new_x, weights)
            keep((EY, plane), row, new_y, weights)
        keep((EZ, 1), row, electric_z(e1, h2, 1, row, x1), weights)

    row_tiles(second_rest)
    send_group(1)

    for group in range(2):
        wait_band(0, group)
        planes_of(group, add_corners)
        send_band(3, group)

    for group in range(2):
        wait_band(2, group)
        planes_of(group, add_middle)
        wait_band(1, group)
        wait_band(3, group)
        planes_of(group, add_x_bands)

    for turn in range(2):
        finish_depth(turn)
    for group in range(2):
        for kind in range(4):
            for toward_next in (False, True):
                band_copy(kind, group, toward_next).wait_send()


def place(planes, out, sems):
    copies = [
        pltpu.make_async_copy(planes.at[index], out.at[0, comp, plane], sems.at[index])
        for index, (comp, plane) in enumerate(ORDER)
    ]
    for copy in copies:
        copy.start()
    for copy in copies:
        copy.wait()


def on_device(tiles, subs, seeds, material, decay, coupling):
    f32 = jnp.float32
    padded = (3, 2, PAD + TX + PAD, TY)
    planes = len(ORDER)
    narrow, wide = pltpu.VMEM((2, planes, 16, TY), f32), pltpu.VMEM((2, planes, 48, TY), f32)
    hbm = pl.BlockSpec(memory_space=pltpu.HBM)
    done = pl.pallas_call(
        functools.partial(kernel, tiles, subs),
        out_shape=jax.ShapeDtypeStruct((planes, TX, TY), f32),
        in_specs=[hbm] * 4,
        out_specs=pl.BlockSpec(memory_space=pltpu.VMEM),
        scratch_shapes=[
            pltpu.SMEM(decay.shape, f32),
            pltpu.SMEM(coupling.shape, f32),
            pltpu.VMEM((6, *padded[1:]), f32),
            pltpu.VMEM((2, TX, TY), jnp.int32),
            pltpu.VMEM((2, TX, TY), f32),
            pltpu.VMEM((2, TX, TY), f32),
            *[pltpu.VMEM(padded, f32)] * 5,
            *[pltpu.VMEM((count, 1, *padded[2:]), f32) for count in (1, 2, 1)],
            *[pltpu.VMEM((count, TX, TY), f32) for count in (2, 3)] * 4,
            *[pltpu.VMEM((count, MOST, TY), f32) for count in (2, 3)],
            narrow, wide, narrow, narrow,
            narrow, wide, narrow, narrow,
            pltpu.SemaphoreType.DMA((5,)),
            pltpu.SemaphoreType.DMA((4,)),
            pltpu.SemaphoreType.DMA((4,)),
            pltpu.SemaphoreType.DMA((2 * PARTS,)),
            pltpu.SemaphoreType.DMA((2 * PARTS,)),
            pltpu.SemaphoreType.DMA((2,)),
            pltpu.SemaphoreType.DMA((2,)),
            pltpu.SemaphoreType.DMA((16,)),
            pltpu.SemaphoreType.DMA((16,)),
        ],
        compiler_params=pltpu.CompilerParams(
            collective_id=0, has_side_effects=True, vmem_limit_bytes=20 * 2**20),
    )(*(pltpu.with_memory_space_constraint(array, pltpu.HBM) for array in (decay, coupling, seeds, material)))
    return pl.pallas_call(
        place,
        out_shape=jax.ShapeDtypeStruct(seeds.shape, f32),
        in_specs=[pl.BlockSpec(memory_space=pltpu.VMEM)],
        out_specs=hbm,
        scratch_shapes=[pltpu.SemaphoreType.DMA((planes,))],
        compiler_params=pltpu.CompilerParams(vmem_limit_bytes=4 * 2**20),
    )(done)


def solution(mesh):
    placed = (P("tile", None, "sub", None, None), P("tile", "sub", None, None), P(), P())
    return jax.shard_map(
        functools.partial(on_device, mesh.shape["tile"], mesh.shape["sub"]),
        mesh=mesh,
        in_specs=placed,
        out_specs=P("tile", None, "sub", None, None),
        check_vma=False,
    )
```

```python
import functools
import math

import jax
import jax.numpy as jnp
from jax import lax
from jax.experimental import pallas as pl
from jax.experimental.pallas import tpu as pltpu
from jax.sharding import PartitionSpec as P

BAND = 32
MESH = pl.DeviceIdType.MESH
MAGNETIC = 0.5
TX = 256
TY = 128
PAD = 8
ROWS = 32
EX, EY, EZ, HX, HY, HZ = range(6)

EARLY = ((HX, 0), (HY, 0), (HZ, 0), (HZ, 1), (EZ, 0))
LATE = ((HX, 1), (HY, 1), (EX, 0), (EY, 0), (EX, 1), (EY, 1), (EZ, 1))
ORDER = EARLY + LATE
GROUPS = ((0, len(EARLY)), (len(EARLY), len(LATE)))

RUN = 8
PARTS = 3
DIRECT = 104
PIECES = (((104, 40), (144, 40), (184, 72)), ((104, 72), (176, 40), (216, 40)))
MOST = 72


def row_tiles(body):
    def step(index, carry):
        body(pl.multiple_of(index * ROWS, ROWS))
        return carry

    lax.fori_loop(0, TX // ROWS, step, 0, unroll=2)


def planes_of(group, body):
    first, count = GROUPS[group]

    def step(index, carry):
        body(index)
        return carry

    lax.fori_loop(first, first + count, step, 0, unroll=True)


def kernel(
    tiles, subs, decay_in, coupling_in, seeds, material, w,
    decay, coupling, field, mat, ca, cb, s0, s1, h1, h2, e1, decayed, under, mixed,
    up_out0, up_out1, down_out0, down_out1, up_in0, up_in1, down_in0, down_in1, relay_in0, relay_in1,
    yc_out, yn_out, xn_out, xc_out, yc_in, yn_in, xn_in, xc_in,
    load_sem, depth_send, depth_recv, part_send, part_recv, relay_recv, relay_send, band_send, band_recv,
):
    tile = lax.axis_index("tile")
    sub = lax.axis_index("sub")
    side = math.isqrt(tiles)
    has_below = sub > 0
    has_above = sub < subs - 1
    below = jnp.maximum(sub - 1, 0)
    above = jnp.minimum(sub + 1, subs - 1)
    x_prev = lax.rem(tile + tiles - 1, tiles)
    x_next = lax.rem(tile + 1, tiles)
    y_prev = lax.rem(tile + tiles - side, tiles)
    y_next = lax.rem(tile + side, tiles)

    loads = [
        pltpu.make_async_copy(material.at[0], mat, load_sem.at[0]),
        pltpu.make_async_copy(seeds.at[0, 0:3], field.at[0:3, :, PAD : PAD + TX], load_sem.at[1]),
        pltpu.make_async_copy(seeds.at[0, 3:6], field.at[3:6, :, PAD : PAD + TX], load_sem.at[2]),
        pltpu.make_async_copy(decay_in, decay, load_sem.at[3]),
        pltpu.make_async_copy(coupling_in, coupling, load_sem.at[4]),
    ]
    for load in loads:
        load.start()

    barrier = pltpu.get_barrier_semaphore()

    def greet(other_tile, other_sub):
        pl.semaphore_signal(barrier, inc=1, device_id=(other_tile, other_sub), device_id_type=MESH)

    pl.when(has_below)(lambda: greet(tile, below))
    pl.when(has_above)(lambda: greet(tile, above))
    for other in (x_prev, x_next, y_prev, y_next):
        greet(other, sub)
    place_in_run = lax.rem(sub, RUN)
    start = sub - place_in_run
    run_above = start + RUN < subs
    run_below = start > 0
    crosses_up = jnp.logical_and(place_in_run == RUN - 1, run_above)
    crosses_down = jnp.logical_and(place_in_run == 0, run_below)

    def relays(upward, part):
        return jnp.logical_and(place_in_run == 2 * part + (1 if upward else 2), run_above if upward else run_below)

    last_here = start + RUN - 1
    first_above = jnp.minimum(start + RUN, subs - 1)
    last_below = jnp.maximum(start - 1, 0)

    def up_relay(part):
        return start + 2 * part + 1

    def down_relay(part):
        return start + 2 * part + 2

    for part in range(PARTS):
        pl.when(relays(True, part))(lambda: greet(tile, last_here))
        pl.when(relays(False, part))(lambda: greet(tile, start))

    lane = lax.broadcasted_iota(jnp.int32, (ROWS, TY), 1)
    not_last = lane < TY - 1
    not_first = lane > 0
    zeros_pad = jnp.zeros((PAD, TY), jnp.float32)
    for comp in range(3):
        for plane in range(2):
            for buf in (s0, s1):
                buf[comp, plane, PAD + TX : PAD + TX + PAD, :] = zeros_pad
            for buf in (h1, h2):
                buf[comp, plane, 0:PAD, :] = zeros_pad
    for buf in (decayed, mixed):
        buf[0, 0, PAD + TX : PAD + TX + PAD, :] = zeros_pad
    under[1, 0, 0:PAD, :] = zeros_pad
    up_out, down_out = (up_out0, up_out1), (down_out0, down_out1)
    up_in, down_in, relay_in = (up_in0, up_in1), (down_in0, down_in1), (relay_in0, relay_in1)

    def at(buf, comp, plane, row):
        return buf[comp, plane, pl.ds(PAD + row, ROWS), :]

    def put(buf, comp, plane, row, value):
        buf[comp, plane, pl.ds(PAD + row, ROWS), :] = value

    def plus_x(buf, comp, plane, row):
        return buf[comp, plane, pl.ds(PAD + row + 1, ROWS), :] - at(buf, comp, plane, row)

    def minus_x(buf, comp, plane, row):
        return at(buf, comp, plane, row) - buf[comp, plane, pl.ds(PAD + row - 1, ROWS), :]

    def plus_y(value):
        return jnp.where(not_last, pltpu.roll(value, TY - 1, 1), 0.0) - value

    def minus_y(value):
        return value - jnp.where(not_first, pltpu.roll(value, 1, 1), 0.0)

    def curl_z(buf, plane, row):
        return plus_x(buf, 1, plane, row) - plus_y(at(buf, 0, plane, row))

    ramp_lane = lane.astype(jnp.float32) + 0.5
    ramp_y = jnp.minimum(jnp.minimum(ramp_lane, TY - ramp_lane) * (1.0 / BAND), 1.0)
    row_iota = lax.broadcasted_iota(jnp.int32, (ROWS, TY), 0)

    def weight(row):
        position = (row_iota + row).astype(jnp.float32) + 0.5
        return jnp.minimum(jnp.minimum(position, TX - position) * (1.0 / BAND), 1.0) * ramp_y

    def rows_of(buf, index, row):
        return buf[index, pl.ds(row, ROWS), :]

    def depth_rows(turn, upward, first, count):
        return (up_out if upward else down_out)[turn].at[:, first : first + count]

    def depth_copy(turn, upward, count):
        slot = turn * 2 + int(upward)
        return pltpu.make_async_remote_copy(
            depth_rows(turn, upward, 0, count), (up_in if upward else down_in)[turn].at[:, 0:count],
            depth_send.at[slot], depth_recv.at[slot],
            device_id=(tile, above if upward else below), device_id_type=MESH)

    def part_copy(turn, upward, part):
        relay = up_relay(part) if upward else down_relay(part)
        first, count = PIECES[int(upward)][part]
        return pltpu.make_async_remote_copy(
            depth_rows(turn, upward, first, count), relay_in[turn].at[:, 0:count],
            part_send.at[turn * PARTS + part], relay_recv.at[turn],
            device_id=(tile, relay), device_id_type=MESH)

    def relay_copy(turn, upward, part):
        first, count = PIECES[int(upward)][part]
        return pltpu.make_async_remote_copy(
            relay_in[turn].at[:, 0:count], (up_in if upward else down_in)[turn].at[:, first : first + count],
            relay_send.at[turn], part_recv.at[turn * PARTS + part],
            device_id=(tile, first_above if upward else last_below), device_id_type=MESH)

    def send_depth(turn, upward):
        crosses = crosses_up if upward else crosses_down
        plain = jnp.logical_and(has_above if upward else has_below, jnp.logical_not(crosses))

        pl.when(plain)(lambda: depth_copy(turn, upward, TX).start())

        @pl.when(crosses)
        def _():
            for part in (1, 0, 2) if not upward else (1, 2, 0):
                part_copy(turn, upward, part).start()
            depth_copy(turn, upward, DIRECT).start()

    late_up = start == 0

    def relay_depth(turn, late):
        for upward in (True, False):
            if late and not upward:
                continue
            for part in range(PARTS):
                now = relays(upward, part)
                if upward:
                    now = jnp.logical_and(now, late_up if late else jnp.logical_not(late_up))

                @pl.when(now)
                def _():
                    part_copy(turn, upward, part).wait_recv()
                    relay_copy(turn, upward, part).start()

    def wait_depth(turn):
        for upward, crosses in ((True, crosses_down), (False, crosses_up)):
            plain = jnp.logical_and(has_below if upward else has_above, jnp.logical_not(crosses))
            pl.when(plain)(lambda: depth_copy(turn, upward, TX).wait_recv())

            @pl.when(crosses)
            def _():
                depth_copy(turn, upward, DIRECT).wait_recv()
                for part in range(PARTS):
                    relay_copy(turn, upward, part).wait_recv()

    def finish_depth(turn):
        for upward, crosses in ((True, crosses_up), (False, crosses_down)):
            plain = jnp.logical_and(has_above if upward else has_below, jnp.logical_not(crosses))
            pl.when(plain)(lambda: depth_copy(turn, upward, TX).wait_send())

            @pl.when(crosses)
            def _():
                for part in range(PARTS):
                    part_copy(turn, upward, part).wait_send()
                depth_copy(turn, upward, DIRECT).wait_send()

            for part in range(PARTS):
                pl.when(relays(upward, part))(lambda: relay_copy(turn, upward, part).wait_send())

    def band_copy(kind, group, toward_next):
        first, count = GROUPS[group]
        source, target = ((yc_out, yc_in), (xn_out, xn_in), (yn_out, yn_in), (xc_out, xc_in))[kind]
        direction = int(toward_next)
        if kind in (0, 2):
            other = y_next if toward_next else y_prev
        else:
            other = x_next if toward_next else x_prev
        slot = (kind * 2 + group) * 2 + direction
        part = slice(first, first + count)
        return pltpu.make_async_remote_copy(
            source.at[direction, part], target.at[direction, part],
            band_send.at[slot], band_recv.at[slot],
            device_id=(other, sub), device_id_type=MESH)

    def send_band(kind, group):
        for toward_next in (False, True):
            band_copy(kind, group, toward_next).start()

    def wait_band(kind, group):
        for toward_next in (False, True):
            band_copy(kind, group, toward_next).wait_recv()

    for number in (3, 4, 0, 1):
        loads[number].wait()
    d0, d1, d2, d3 = (decay[i] for i in range(4))
    c0, c1, c2, c3 = (coupling[i] for i in range(4))

    def scale(row):
        for plane in range(2):
            label = mat[plane, pl.ds(row, ROWS), :]
            is0, is1, is2 = label == 0, label == 1, label == 2
            couple = jnp.where(is0, c0, jnp.where(is1, c1, jnp.where(is2, c2, c3)))
            decays = jnp.where(is0, d0, jnp.where(is1, d1, jnp.where(is2, d2, d3)))
            cb[plane, pl.ds(row, ROWS), :] = couple
            ca[plane, pl.ds(row, ROWS), :] = decays
            (down_out, up_out)[plane][1][2, pl.ds(row, ROWS), :] = couple
            scaled = [couple * at(field, comp, plane, row) for comp in range(3)]
            for comp in range(3):
                put(s0, comp, plane, row, scaled[comp])
            if plane == 0:
                for comp in range(2):
                    down_out[0][comp, pl.ds(row, ROWS), :] = scaled[comp]
            else:
                put(decayed, 0, 0, row, decays * scaled[2])

    row_tiles(scale)
    count = lambda flag, number: jnp.where(flag, number, 0)
    crosses_any = jnp.logical_or(crosses_up, crosses_down)
    pl.semaphore_wait(barrier, 4 + count(has_below, 1) + count(has_above, 1) + count(crosses_any, PARTS))
    send_depth(0, False)
    loads[2].wait()

    def without_above(hbuf, offset, sbuf, row):
        s_x, s_y, s_z = (at(sbuf, comp, 1, row) for comp in range(3))
        part_x = at(hbuf, offset, 1, row) + plus_y(s_z) + s_y
        part_y = at(hbuf, offset + 1, 1, row) - s_x - plus_x(sbuf, 2, 1, row)
        return part_x, part_y

    def first_partial(row):
        up_out[0][0, pl.ds(row, ROWS), :], up_out[0][1, pl.ds(row, ROWS), :] = without_above(field, HX, s0, row)

    row_tiles(first_partial)
    send_depth(0, True)

    def magnetic_local(hbuf, offset, sbuf, row):
        s_x0, s_y0, s_z0 = (at(sbuf, comp, 0, row) for comp in range(3))
        new_x = at(hbuf, offset, 0, row) + plus_y(s_z0) - (at(sbuf, 1, 1, row) - s_y0)
        new_y = at(hbuf, offset + 1, 0, row) + (at(sbuf, 0, 1, row) - s_x0) - plus_x(sbuf, 2, 0, row)
        new_z = at(hbuf, offset + 2, 0, row) + curl_z(sbuf, 0, row)
        new_z1 = at(hbuf, offset + 2, 1, row) + curl_z(sbuf, 1, row)
        return new_x, new_y, new_z, new_z1

    def first_local(row):
        new_x, new_y, new_z, new_z1 = magnetic_local(field, HX, s0, row)
        put(h1, 0, 0, row, new_x)
        put(h1, 1, 0, row, new_y)
        put(h1, 2, 0, row, new_z)
        put(h1, 2, 1, row, new_z1)

    row_tiles(first_local)

    def second_terms(row):
        h_x, h_y = at(h1, 0, 0, row), at(h1, 1, 0, row)
        decays, couple = rows_of(ca, 1, row), rows_of(cb, 1, row)
        part_x = decays * at(field, EX, 1, row) - MAGNETIC * (minus_y(at(h1, 2, 1, row)) + h_y)
        part_y = decays * at(field, EY, 1, row) + MAGNETIC * (h_x + minus_x(h1, 2, 1, row))
        up_out[1][0, pl.ds(row, ROWS), :] = plus_y(at(decayed, 0, 0, row)) + couple * part_y
        up_out[1][1, pl.ds(row, ROWS), :] = -couple * part_x - plus_x(decayed, 0, 0, row)
        decays, couple = rows_of(ca, 0, row), rows_of(cb, 0, row)
        down_out[1][0, pl.ds(row, ROWS), :] = couple * (
            decays * at(field, EX, 0, row) - MAGNETIC * (minus_y(at(h1, 2, 0, row)) - h_y))
        down_out[1][1, pl.ds(row, ROWS), :] = couple * (
            decays * at(field, EY, 0, row) - MAGNETIC * (h_x - minus_x(h1, 2, 0, row)))

    row_tiles(second_terms)
    send_depth(1, False)
    send_depth(1, True)

    @pl.when(jnp.logical_not(has_above))
    def _():
        def clear(row):
            for buf in down_in:
                for comp in range(buf.shape[0]):
                    buf[comp, pl.ds(row, ROWS), :] = jnp.zeros((ROWS, TY), jnp.float32)

        row_tiles(clear)

    @pl.when(jnp.logical_not(has_below))
    def _():
        def cancel(row):
            up_in[0][0, pl.ds(row, ROWS), :] = at(s0, 1, 0, row)
            up_in[0][1, pl.ds(row, ROWS), :] = -at(s0, 0, 0, row)
            for comp in range(3):
                up_in[1][comp, pl.ds(row, ROWS), :] = jnp.zeros((ROWS, TY), jnp.float32)

        row_tiles(cancel)

    def electric_xy(ebuf, hbuf, plane, row, h_x, h_y, under_x, under_y):
        h_z = at(hbuf, 2, plane, row)
        decays = rows_of(ca, plane, row)
        new_x = decays * at(ebuf, 0, plane, row) - MAGNETIC * (minus_y(h_z) - (h_y - under_y))
        new_y = decays * at(ebuf, 1, plane, row) - MAGNETIC * ((h_x - under_x) - minus_x(hbuf, 2, plane, row))
        return new_x, new_y

    def electric_z(ebuf, hbuf, plane, row, h_x):
        decays = rows_of(ca, plane, row)
        return decays * at(ebuf, 2, plane, row) - MAGNETIC * (minus_x(hbuf, 1, plane, row) - minus_y(h_x))

    relay_depth(0, False)
    wait_depth(0)
    relay_depth(1, False)

    def first_rest(row):
        x1 = rows_of(up_out[0], 0, row) - rows_of(down_in[0], 1, row)
        y1 = rows_of(up_out[0], 1, row) + rows_of(down_in[0], 0, row)
        under_x = rows_of(up_in[0], 0, row) - at(s0, 1, 0, row)
        under_y = rows_of(up_in[0], 1, row) + at(s0, 0, 0, row)
        put(h1, 0, 1, row, x1)
        put(h1, 1, 1, row, y1)
        put(under, 0, 0, row, under_x)
        put(under, 1, 0, row, under_y)
        x0, y0 = at(h1, 0, 0, row), at(h1, 1, 0, row)
        for plane, (h_x, h_y, b_x, b_y) in enumerate(((x0, y0, under_x, under_y), (x1, y1, x0, y0))):
            new = (*electric_xy(field, h1, plane, row, h_x, h_y, b_x, b_y), electric_z(field, h1, plane, row, h_x))
            couple = rows_of(cb, plane, row)
            for comp in range(3):
                put(e1, comp, plane, row, new[comp])
                put(s1, comp, plane, row, couple * new[comp])

    row_tiles(first_rest)

    def keep(name, row, value, weights):
        w[ORDER.index(name), pl.ds(row, ROWS), :] = value * weights

    def second_local(row):
        new_x, new_y, new_z, new_z1 = magnetic_local(h1, 0, s1, row)
        put(h2, 0, 0, row, new_x)
        put(h2, 1, 0, row, new_y)
        put(h2, 2, 0, row, new_z)
        put(h2, 2, 1, row, new_z1)
        weights = weight(row)
        keep((HX, 0), row, new_x, weights)
        keep((HY, 0), row, new_y, weights)
        keep((HZ, 0), row, new_z, weights)
        keep((HZ, 1), row, new_z1, weights)
        keep((EZ, 0), row, electric_z(e1, h2, 0, row, new_x), weights)

    row_tiles(second_local)

    def slot_of(rows):
        return lax.broadcasted_iota(jnp.int32, (rows, TY), 1) // BAND

    def pack_lanes(values):
        slot = slot_of(values[0].shape[0])
        turned = [values[0]] + [pltpu.roll(values[k], BAND * k, 1) for k in (1, 2, 3)]
        low, high = turned[3], turned[0]
        for k in (2, 1, 0):
            low = jnp.where(slot == k, turned[k], low)
            high = jnp.where(slot == k, turned[k + 1], high)
        return low, high

    def unpack_lanes(low_side, high_side):
        slot = slot_of(low_side.shape[0])
        turned = []
        for k in range(4):
            mixed = jnp.where(slot == (k + 3) % 4, low_side, high_side)
            shift = (TY - BAND * (k - 1)) % TY
            turned.append(pltpu.roll(mixed, shift, 1) if shift else mixed)
        return [jnp.where(slot == 0, turned[k], jnp.where(slot == 3, turned[(k + 2) % 4], 0.0)) for k in range(4)]

    corner_rows = (0, 16, TX - 32, TX - 16)
    middle_rows = (32, 80, 128, 176)

    def middle_lanes():
        slot = slot_of(16)
        return jnp.logical_or(slot == 1, slot == 2)

    def pack_corners(index):
        values = [w[index, first : first + 16, :] for first in corner_rows]
        low, high = pack_lanes(values)
        yc_out[0, index], yc_out[1, index] = low, high
        middle = middle_lanes()
        for direction in range(2):
            xn_out[direction, index] = jnp.where(
                middle, values[2 * direction], pltpu.roll(values[2 * direction + 1], TY // 2, 1))

    def pack_middle(index):
        low, high = pack_lanes([w[index, first : first + 48, :] for first in middle_rows])
        yn_out[0, index], yn_out[1, index] = low, high

    def add_corners(index):
        added = unpack_lanes(yc_in[1, index], yc_in[0, index])
        values = []
        for first, more in zip(corner_rows, added):
            total = w[index, first : first + 16, :] + more
            w[index, first : first + 16, :] = total
            values.append(total)
        middle = middle_lanes()
        for direction in range(2):
            xc_out[direction, index] = jnp.where(
                middle, pltpu.roll(values[2 * direction + 1], TY // 2, 1), values[2 * direction])

    def add_middle(index):
        added = unpack_lanes(yn_in[1, index], yn_in[0, index])
        for first, more in zip(middle_rows, added):
            w[index, first : first + 48, :] += more

    def add_x_bands(index):
        middle = middle_lanes()
        for side_of, first in ((1, 0), (0, TX - 32)):
            plain, summed = xn_in[side_of, index], xc_in[side_of, index]
            w[index, first : first + 16, :] += jnp.where(middle, plain, summed)
            w[index, first + 16 : first + 32, :] += pltpu.roll(jnp.where(middle, summed, plain), TY // 2, 1)

    def send_group(group):
        planes_of(group, pack_corners)
        send_band(0, group)
        send_band(1, group)
        planes_of(group, pack_middle)
        send_band(2, group)

    send_group(0)
    relay_depth(0, True)
    relay_depth(1, True)
    wait_depth(1)

    def mix(row):
        turn_z = minus_x(under, 1, 0, row) - minus_y(at(under, 0, 0, row))
        put(mixed, 0, 0, row, MAGNETIC * rows_of(up_in[1], 2, row) * turn_z)

    row_tiles(mix)

    def second_rest(row):
        x1, y1 = without_above(h1, 0, s1, row)
        couple = MAGNETIC * rows_of(down_in[1], 2, row)
        x1 -= rows_of(down_in[1], 1, row) + couple * at(h1, 0, 1, row)
        y1 += rows_of(down_in[1], 0, row) - couple * at(h1, 1, 1, row)
        couple = MAGNETIC * rows_of(up_in[1], 2, row)
        under_x, under_y = at(under, 0, 0, row), at(under, 1, 0, row)
        under_x += rows_of(up_in[1], 0, row) - couple * under_x - plus_y(at(mixed, 0, 0, row)) - at(s1, 1, 0, row)
        under_y += rows_of(up_in[1], 1, row) - couple * under_y + plus_x(mixed, 0, 0, row) + at(s1, 0, 0, row)
        under_x = jnp.where(has_below, under_x, 0.0)
        under_y = jnp.where(has_below, under_y, 0.0)
        put(h2, 0, 1, row, x1)
        put(h2, 1, 1, row, y1)
        x0, y0 = at(h2, 0, 0, row), at(h2, 1, 0, row)
        weights = weight(row)
        keep((HX, 1), row, x1, weights)
        keep((HY, 1), row, y1, weights)
        for plane, (h_x, h_y, b_x, b_y) in enumerate(((x0, y0, under_x, under_y), (x1, y1, x0, y0))):
            new_x, new_y = electric_xy(e1, h2, plane, row, h_x, h_y, b_x, b_y)
            keep((EX, plane), row, new_x, weights)
            keep((EY, plane), row, new_y, weights)
        keep((EZ, 1), row, electric_z(e1, h2, 1, row, x1), weights)

    row_tiles(second_rest)
    send_group(1)

    for group in range(2):
        wait_band(0, group)
        planes_of(group, add_corners)
        send_band(3, group)

    for group in range(2):
        wait_band(2, group)
        planes_of(group, add_middle)
        wait_band(1, group)
        wait_band(3, group)
        planes_of(group, add_x_bands)

    for turn in range(2):
        finish_depth(turn)
    for group in range(2):
        for kind in range(4):
            for toward_next in (False, True):
                band_copy(kind, group, toward_next).wait_send()


def place(planes, out, sems):
    copies = [
        pltpu.make_async_copy(planes.at[index], out.at[0, comp, plane], sems.at[index])
        for index, (comp, plane) in enumerate(ORDER)
    ]
    for copy in copies:
        copy.start()
    for copy in copies:
        copy.wait()


def on_device(tiles, subs, seeds, material, decay, coupling):
    f32 = jnp.float32
    padded = (3, 2, PAD + TX + PAD, TY)
    planes = len(ORDER)
    narrow, wide = pltpu.VMEM((2, planes, 16, TY), f32), pltpu.VMEM((2, planes, 48, TY), f32)
    hbm = pl.BlockSpec(memory_space=pltpu.HBM)
    done = pl.pallas_call(
        functools.partial(kernel, tiles, subs),
        out_shape=jax.ShapeDtypeStruct((planes, TX, TY), f32),
        in_specs=[hbm] * 4,
        out_specs=pl.BlockSpec(memory_space=pltpu.VMEM),
        scratch_shapes=[
            pltpu.SMEM(decay.shape, f32),
            pltpu.SMEM(coupling.shape, f32),
            pltpu.VMEM((6, *padded[1:]), f32),
            pltpu.VMEM((2, TX, TY), jnp.int32),
            pltpu.VMEM((2, TX, TY), f32),
            pltpu.VMEM((2, TX, TY), f32),
            *[pltpu.VMEM(padded, f32)] * 5,
            *[pltpu.VMEM((count, 1, *padded[2:]), f32) for count in (1, 2, 1)],
            *[pltpu.VMEM((count, TX, TY), f32) for count in (2, 3)] * 4,
            *[pltpu.VMEM((count, MOST, TY), f32) for count in (2, 3)],
            narrow, wide, narrow, narrow,
            narrow, wide, narrow, narrow,
            pltpu.SemaphoreType.DMA((5,)),
            pltpu.SemaphoreType.DMA((4,)),
            pltpu.SemaphoreType.DMA((4,)),
            pltpu.SemaphoreType.DMA((2 * PARTS,)),
            pltpu.SemaphoreType.DMA((2 * PARTS,)),
            pltpu.SemaphoreType.DMA((2,)),
            pltpu.SemaphoreType.DMA((2,)),
            pltpu.SemaphoreType.DMA((16,)),
            pltpu.SemaphoreType.DMA((16,)),
        ],
        compiler_params=pltpu.CompilerParams(
            collective_id=0, has_side_effects=True, vmem_limit_bytes=20 * 2**20),
    )(*(pltpu.with_memory_space_constraint(array, pltpu.HBM) for array in (decay, coupling, seeds, material)))
    return pl.pallas_call(
        place,
        out_shape=jax.ShapeDtypeStruct(seeds.shape, f32),
        in_specs=[pl.BlockSpec(memory_space=pltpu.VMEM)],
        out_specs=hbm,
        scratch_shapes=[pltpu.SemaphoreType.DMA((planes,))],
        compiler_params=pltpu.CompilerParams(vmem_limit_bytes=4 * 2**20),
    )(done)


def solution(mesh):
    placed = (P("tile", None, "sub", None, None), P("tile", "sub", None, None), P(), P())
    return jax.shard_map(
        functools.partial(on_device, mesh.shape["tile"], mesh.shape["sub"]),
        mesh=mesh,
        in_specs=placed,
        out_specs=P("tile", None, "sub", None, None),
        check_vma=False,
    )
```

```python
import functools
import math

import jax
import jax.numpy as jnp
from jax import lax
from jax.experimental import pallas as pl
from jax.experimental.pallas import tpu as pltpu
from jax.sharding import PartitionSpec as P

BAND = 32
MESH = pl.DeviceIdType.MESH
MAGNETIC = 0.5
TX = 256
TY = 128
PAD = 8
ROWS = 32
EX, EY, EZ, HX, HY, HZ = range(6)

EARLY = ((HX, 0), (HY, 0), (HZ, 0), (HZ, 1), (EZ, 0))
UPPER = ((HX, 1), (HY, 1), (EX, 1), (EY, 1), (EZ, 1))
LOWER = ((EX, 0), (EY, 0))
ORDER = EARLY + UPPER + LOWER
GROUPS = ((0, 5), (5, 5), (10, 2))

RUN = 8
PARTS = 3
DIRECT = 104
PIECES = (((104, 40), (144, 40), (184, 72)), ((104, 72), (176, 40), (216, 40)))
MOST = 72


def row_tiles(body):
    def step(index, carry):
        body(pl.multiple_of(index * ROWS, ROWS))
        return carry

    lax.fori_loop(0, TX // ROWS, step, 0, unroll=2)


def planes_of(group, body):
    first, count = GROUPS[group]

    def step(index, carry):
        body(index)
        return carry

    lax.fori_loop(first, first + count, step, 0, unroll=True)


def kernel(
    tiles, subs, decay_in, coupling_in, seeds, material, w,
    decay, coupling, field, mat, ca, cb, s0, s1, h1, h2, e1, decayed, under, mixed,
    up_out0, up_out1, down_out0, down_out1, up_in0, up_in1, down_in0, down_in1, relay_in0, relay_in1,
    yc_out, yn_out, xn_out, xc_out, yc_in, yn_in, xn_in, xc_in,
    load_sem, depth_send, depth_recv, part_send, part_recv, relay_recv, relay_send, band_send, band_recv,
):
    tile = lax.axis_index("tile")
    sub = lax.axis_index("sub")
    side = math.isqrt(tiles)
    has_below = sub > 0
    has_above = sub < subs - 1
    below = jnp.maximum(sub - 1, 0)
    above = jnp.minimum(sub + 1, subs - 1)
    x_prev = lax.rem(tile + tiles - 1, tiles)
    x_next = lax.rem(tile + 1, tiles)
    y_prev = lax.rem(tile + tiles - side, tiles)
    y_next = lax.rem(tile + side, tiles)

    loads = [
        pltpu.make_async_copy(material.at[0], mat, load_sem.at[0]),
        pltpu.make_async_copy(seeds.at[0, 0:3], field.at[0:3, :, PAD : PAD + TX], load_sem.at[1]),
        pltpu.make_async_copy(seeds.at[0, 3:6], field.at[3:6, :, PAD : PAD + TX], load_sem.at[2]),
        pltpu.make_async_copy(decay_in, decay, load_sem.at[3]),
        pltpu.make_async_copy(coupling_in, coupling, load_sem.at[4]),
    ]
    for load in loads:
        load.start()

    barrier = pltpu.get_barrier_semaphore()

    def greet(other_tile, other_sub):
        pl.semaphore_signal(barrier, inc=1, device_id=(other_tile, other_sub), device_id_type=MESH)

    pl.when(has_below)(lambda: greet(tile, below))
    pl.when(has_above)(lambda: greet(tile, above))
    for other in (x_prev, x_next, y_prev, y_next):
        greet(other, sub)
    place_in_run = lax.rem(sub, RUN)
    start = sub - place_in_run
    run_above = start + RUN < subs
    run_below = start > 0
    crosses_up = jnp.logical_and(place_in_run == RUN - 1, run_above)
    crosses_down = jnp.logical_and(place_in_run == 0, run_below)

    def relays(upward, part):
        return jnp.logical_and(place_in_run == 2 * part + (1 if upward else 2), run_above if upward else run_below)

    last_here = start + RUN - 1
    first_above = jnp.minimum(start + RUN, subs - 1)
    last_below = jnp.maximum(start - 1, 0)

    def up_relay(part):
        return start + 2 * part + 1

    def down_relay(part):
        return start + 2 * part + 2

    for part in range(PARTS):
        pl.when(relays(True, part))(lambda: greet(tile, last_here))
        pl.when(relays(False, part))(lambda: greet(tile, start))

    lane = lax.broadcasted_iota(jnp.int32, (ROWS, TY), 1)
    not_last = lane < TY - 1
    not_first = lane > 0
    zeros_pad = jnp.zeros((PAD, TY), jnp.float32)
    for comp in range(3):
        for plane in range(2):
            for buf in (s0, s1):
                buf[comp, plane, PAD + TX : PAD + TX + PAD, :] = zeros_pad
            for buf in (h1, h2):
                buf[comp, plane, 0:PAD, :] = zeros_pad
    for buf in (decayed, mixed):
        buf[0, 0, PAD + TX : PAD + TX + PAD, :] = zeros_pad
    under[1, 0, 0:PAD, :] = zeros_pad
    up_out, down_out = (up_out0, up_out1), (down_out0, down_out1)
    up_in, down_in, relay_in = (up_in0, up_in1), (down_in0, down_in1), (relay_in0, relay_in1)

    def at(buf, comp, plane, row):
        return buf[comp, plane, pl.ds(PAD + row, ROWS), :]

    def put(buf, comp, plane, row, value):
        buf[comp, plane, pl.ds(PAD + row, ROWS), :] = value

    def plus_x(buf, comp, plane, row):
        return buf[comp, plane, pl.ds(PAD + row + 1, ROWS), :] - at(buf, comp, plane, row)

    def minus_x(buf, comp, plane, row):
        return at(buf, comp, plane, row) - buf[comp, plane, pl.ds(PAD + row - 1, ROWS), :]

    def plus_y(value):
        return jnp.where(not_last, pltpu.roll(value, TY - 1, 1), 0.0) - value

    def minus_y(value):
        return value - jnp.where(not_first, pltpu.roll(value, 1, 1), 0.0)

    def curl_z(buf, plane, row):
        return plus_x(buf, 1, plane, row) - plus_y(at(buf, 0, plane, row))

    ramp_lane = lane.astype(jnp.float32) + 0.5
    ramp_y = jnp.minimum(jnp.minimum(ramp_lane, TY - ramp_lane) * (1.0 / BAND), 1.0)
    row_iota = lax.broadcasted_iota(jnp.int32, (ROWS, TY), 0)

    def weight(row):
        position = (row_iota + row).astype(jnp.float32) + 0.5
        return jnp.minimum(jnp.minimum(position, TX - position) * (1.0 / BAND), 1.0) * ramp_y

    def rows_of(buf, index, row):
        return buf[index, pl.ds(row, ROWS), :]

    def depth_rows(turn, upward, first, count):
        return (up_out if upward else down_out)[turn].at[:, first : first + count]

    def depth_copy(turn, upward, count):
        slot = turn * 2 + int(upward)
        return pltpu.make_async_remote_copy(
            depth_rows(turn, upward, 0, count), (up_in if upward else down_in)[turn].at[:, 0:count],
            depth_send.at[slot], depth_recv.at[slot],
            device_id=(tile, above if upward else below), device_id_type=MESH)

    def part_copy(turn, upward, part):
        relay = up_relay(part) if upward else down_relay(part)
        first, count = PIECES[int(upward)][part]
        return pltpu.make_async_remote_copy(
            depth_rows(turn, upward, first, count), relay_in[turn].at[:, 0:count],
            part_send.at[turn * PARTS + part], relay_recv.at[turn],
            device_id=(tile, relay), device_id_type=MESH)

    def relay_copy(turn, upward, part):
        first, count = PIECES[int(upward)][part]
        return pltpu.make_async_remote_copy(
            relay_in[turn].at[:, 0:count], (up_in if upward else down_in)[turn].at[:, first : first + count],
            relay_send.at[turn], part_recv.at[turn * PARTS + part],
            device_id=(tile, first_above if upward else last_below), device_id_type=MESH)

    def send_depth(turn, upward):
        crosses = crosses_up if upward else crosses_down
        plain = jnp.logical_and(has_above if upward else has_below, jnp.logical_not(crosses))

        pl.when(plain)(lambda: depth_copy(turn, upward, TX).start())

        @pl.when(crosses)
        def _():
            for part in (1, 0, 2) if not upward else (1, 2, 0):
                part_copy(turn, upward, part).start()
            depth_copy(turn, upward, DIRECT).start()

    late_up = start == 0

    def relay_depth(turn, late):
        for upward in (True, False):
            if late and not upward:
                continue
            for part in range(PARTS):
                now = relays(upward, part)
                if upward:
                    now = jnp.logical_and(now, late_up if late else jnp.logical_not(late_up))

                @pl.when(now)
                def _():
                    part_copy(turn, upward, part).wait_recv()
                    relay_copy(turn, upward, part).start()

    def wait_depth(turn, upward):
        crosses = crosses_down if upward else crosses_up
        plain = jnp.logical_and(has_below if upward else has_above, jnp.logical_not(crosses))
        pl.when(plain)(lambda: depth_copy(turn, upward, TX).wait_recv())

        @pl.when(crosses)
        def _():
            depth_copy(turn, upward, DIRECT).wait_recv()
            for part in range(PARTS):
                relay_copy(turn, upward, part).wait_recv()

    def finish_depth(turn):
        for upward, crosses in ((True, crosses_up), (False, crosses_down)):
            plain = jnp.logical_and(has_above if upward else has_below, jnp.logical_not(crosses))
            pl.when(plain)(lambda: depth_copy(turn, upward, TX).wait_send())

            @pl.when(crosses)
            def _():
                for part in range(PARTS):
                    part_copy(turn, upward, part).wait_send()
                depth_copy(turn, upward, DIRECT).wait_send()

            for part in range(PARTS):
                pl.when(relays(upward, part))(lambda: relay_copy(turn, upward, part).wait_send())

    def band_copy(kind, group, toward_next):
        first, count = GROUPS[group]
        source, target = ((yc_out, yc_in), (xn_out, xn_in), (yn_out, yn_in), (xc_out, xc_in))[kind]
        direction = int(toward_next)
        if kind in (0, 2):
            other = y_next if toward_next else y_prev
        else:
            other = x_next if toward_next else x_prev
        slot = (kind * len(GROUPS) + group) * 2 + direction
        part = slice(first, first + count)
        return pltpu.make_async_remote_copy(
            source.at[direction, part], target.at[direction, part],
            band_send.at[slot], band_recv.at[slot],
            device_id=(other, sub), device_id_type=MESH)

    def send_band(kind, group):
        for toward_next in (False, True):
            band_copy(kind, group, toward_next).start()

    def wait_band(kind, group):
        for toward_next in (False, True):
            band_copy(kind, group, toward_next).wait_recv()

    for number in (3, 4, 0, 1):
        loads[number].wait()
    d0, d1, d2, d3 = (decay[i] for i in range(4))
    c0, c1, c2, c3 = (coupling[i] for i in range(4))

    def scale(row):
        for plane in range(2):
            label = mat[plane, pl.ds(row, ROWS), :]
            is0, is1, is2 = label == 0, label == 1, label == 2
            couple = jnp.where(is0, c0, jnp.where(is1, c1, jnp.where(is2, c2, c3)))
            decays = jnp.where(is0, d0, jnp.where(is1, d1, jnp.where(is2, d2, d3)))
            cb[plane, pl.ds(row, ROWS), :] = couple
            ca[plane, pl.ds(row, ROWS), :] = decays
            (down_out, up_out)[plane][1][2, pl.ds(row, ROWS), :] = couple
            scaled = [couple * at(field, comp, plane, row) for comp in range(3)]
            for comp in range(3):
                put(s0, comp, plane, row, scaled[comp])
            if plane == 0:
                for comp in range(2):
                    down_out[0][comp, pl.ds(row, ROWS), :] = scaled[comp]
            else:
                put(decayed, 0, 0, row, decays * scaled[2])

    row_tiles(scale)
    count = lambda flag, number: jnp.where(flag, number, 0)
    crosses_any = jnp.logical_or(crosses_up, crosses_down)
    pl.semaphore_wait(barrier, 4 + count(has_below, 1) + count(has_above, 1) + count(crosses_any, PARTS))
    send_depth(0, False)
    loads[2].wait()

    def without_above(hbuf, offset, sbuf, row):
        s_x, s_y, s_z = (at(sbuf, comp, 1, row) for comp in range(3))
        part_x = at(hbuf, offset, 1, row) + plus_y(s_z) + s_y
        part_y = at(hbuf, offset + 1, 1, row) - s_x - plus_x(sbuf, 2, 1, row)
        return part_x, part_y

    def first_partial(row):
        up_out[0][0, pl.ds(row, ROWS), :], up_out[0][1, pl.ds(row, ROWS), :] = without_above(field, HX, s0, row)

    row_tiles(first_partial)
    send_depth(0, True)

    def magnetic_local(hbuf, offset, sbuf, row):
        s_x0, s_y0, s_z0 = (at(sbuf, comp, 0, row) for comp in range(3))
        new_x = at(hbuf, offset, 0, row) + plus_y(s_z0) - (at(sbuf, 1, 1, row) - s_y0)
        new_y = at(hbuf, offset + 1, 0, row) + (at(sbuf, 0, 1, row) - s_x0) - plus_x(sbuf, 2, 0, row)
        new_z = at(hbuf, offset + 2, 0, row) + curl_z(sbuf, 0, row)
        new_z1 = at(hbuf, offset + 2, 1, row) + curl_z(sbuf, 1, row)
        return new_x, new_y, new_z, new_z1

    def first_local(row):
        new_x, new_y, new_z, new_z1 = magnetic_local(field, HX, s0, row)
        put(h1, 0, 0, row, new_x)
        put(h1, 1, 0, row, new_y)
        put(h1, 2, 0, row, new_z)
        put(h1, 2, 1, row, new_z1)

    row_tiles(first_local)

    def second_terms(row):
        h_x, h_y = at(h1, 0, 0, row), at(h1, 1, 0, row)
        decays, couple = rows_of(ca, 1, row), rows_of(cb, 1, row)
        part_x = decays * at(field, EX, 1, row) - MAGNETIC * (minus_y(at(h1, 2, 1, row)) + h_y)
        part_y = decays * at(field, EY, 1, row) + MAGNETIC * (h_x + minus_x(h1, 2, 1, row))
        up_out[1][0, pl.ds(row, ROWS), :] = plus_y(at(decayed, 0, 0, row)) + couple * part_y
        up_out[1][1, pl.ds(row, ROWS), :] = -couple * part_x - plus_x(decayed, 0, 0, row)
        decays, couple = rows_of(ca, 0, row), rows_of(cb, 0, row)
        down_out[1][0, pl.ds(row, ROWS), :] = couple * (
            decays * at(field, EX, 0, row) - MAGNETIC * (minus_y(at(h1, 2, 0, row)) - h_y))
        down_out[1][1, pl.ds(row, ROWS), :] = couple * (
            decays * at(field, EY, 0, row) - MAGNETIC * (h_x - minus_x(h1, 2, 0, row)))

    row_tiles(second_terms)
    send_depth(1, False)
    send_depth(1, True)

    @pl.when(jnp.logical_not(has_above))
    def _():
        def clear(row):
            for buf in down_in:
                for comp in range(buf.shape[0]):
                    buf[comp, pl.ds(row, ROWS), :] = jnp.zeros((ROWS, TY), jnp.float32)

        row_tiles(clear)

    @pl.when(jnp.logical_not(has_below))
    def _():
        def cancel(row):
            up_in[0][0, pl.ds(row, ROWS), :] = at(s0, 1, 0, row)
            up_in[0][1, pl.ds(row, ROWS), :] = -at(s0, 0, 0, row)
            for comp in range(3):
                up_in[1][comp, pl.ds(row, ROWS), :] = jnp.zeros((ROWS, TY), jnp.float32)

        row_tiles(cancel)

    def electric_xy(ebuf, hbuf, plane, row, h_x, h_y, under_x, under_y):
        h_z = at(hbuf, 2, plane, row)
        decays = rows_of(ca, plane, row)
        new_x = decays * at(ebuf, 0, plane, row) - MAGNETIC * (minus_y(h_z) - (h_y - under_y))
        new_y = decays * at(ebuf, 1, plane, row) - MAGNETIC * ((h_x - under_x) - minus_x(hbuf, 2, plane, row))
        return new_x, new_y

    def electric_z(ebuf, hbuf, plane, row, h_x):
        decays = rows_of(ca, plane, row)
        return decays * at(ebuf, 2, plane, row) - MAGNETIC * (minus_x(hbuf, 1, plane, row) - minus_y(h_x))

    relay_depth(0, False)
    wait_depth(0, True)
    wait_depth(0, False)
    relay_depth(1, False)

    def first_rest(row):
        x1 = rows_of(up_out[0], 0, row) - rows_of(down_in[0], 1, row)
        y1 = rows_of(up_out[0], 1, row) + rows_of(down_in[0], 0, row)
        under_x = rows_of(up_in[0], 0, row) - at(s0, 1, 0, row)
        under_y = rows_of(up_in[0], 1, row) + at(s0, 0, 0, row)
        put(h1, 0, 1, row, x1)
        put(h1, 1, 1, row, y1)
        put(under, 0, 0, row, under_x)
        put(under, 1, 0, row, under_y)
        x0, y0 = at(h1, 0, 0, row), at(h1, 1, 0, row)
        for plane, (h_x, h_y, b_x, b_y) in enumerate(((x0, y0, under_x, under_y), (x1, y1, x0, y0))):
            new = (*electric_xy(field, h1, plane, row, h_x, h_y, b_x, b_y), electric_z(field, h1, plane, row, h_x))
            couple = rows_of(cb, plane, row)
            for comp in range(3):
                put(e1, comp, plane, row, new[comp])
                put(s1, comp, plane, row, couple * new[comp])

    row_tiles(first_rest)

    def keep(name, row, value, weights):
        w[ORDER.index(name), pl.ds(row, ROWS), :] = value * weights

    def second_local(row):
        new_x, new_y, new_z, new_z1 = magnetic_local(h1, 0, s1, row)
        put(h2, 0, 0, row, new_x)
        put(h2, 1, 0, row, new_y)
        put(h2, 2, 0, row, new_z)
        put(h2, 2, 1, row, new_z1)
        weights = weight(row)
        keep((HX, 0), row, new_x, weights)
        keep((HY, 0), row, new_y, weights)
        keep((HZ, 0), row, new_z, weights)
        keep((HZ, 1), row, new_z1, weights)
        keep((EZ, 0), row, electric_z(e1, h2, 0, row, new_x), weights)

    row_tiles(second_local)

    def slot_of(rows):
        return lax.broadcasted_iota(jnp.int32, (rows, TY), 1) // BAND

    def pack_lanes(values):
        slot = slot_of(values[0].shape[0])
        turned = [values[0]] + [pltpu.roll(values[k], BAND * k, 1) for k in (1, 2, 3)]
        low, high = turned[3], turned[0]
        for k in (2, 1, 0):
            low = jnp.where(slot == k, turned[k], low)
            high = jnp.where(slot == k, turned[k + 1], high)
        return low, high

    def unpack_lanes(low_side, high_side):
        slot = slot_of(low_side.shape[0])
        turned = []
        for k in range(4):
            mixed = jnp.where(slot == (k + 3) % 4, low_side, high_side)
            shift = (TY - BAND * (k - 1)) % TY
            turned.append(pltpu.roll(mixed, shift, 1) if shift else mixed)
        return [jnp.where(slot == 0, turned[k], jnp.where(slot == 3, turned[(k + 2) % 4], 0.0)) for k in range(4)]

    corner_rows = (0, 16, TX - 32, TX - 16)
    middle_rows = (32, 80, 128, 176)

    def middle_lanes():
        slot = slot_of(16)
        return jnp.logical_or(slot == 1, slot == 2)

    def pack_corners(index):
        values = [w[index, first : first + 16, :] for first in corner_rows]
        low, high = pack_lanes(values)
        yc_out[0, index], yc_out[1, index] = low, high
        middle = middle_lanes()
        for direction in range(2):
            xn_out[direction, index] = jnp.where(
                middle, values[2 * direction], pltpu.roll(values[2 * direction + 1], TY // 2, 1))

    def pack_middle(index):
        low, high = pack_lanes([w[index, first : first + 48, :] for first in middle_rows])
        yn_out[0, index], yn_out[1, index] = low, high

    def add_corners(index):
        added = unpack_lanes(yc_in[1, index], yc_in[0, index])
        values = []
        for first, more in zip(corner_rows, added):
            total = w[index, first : first + 16, :] + more
            w[index, first : first + 16, :] = total
            values.append(total)
        middle = middle_lanes()
        for direction in range(2):
            xc_out[direction, index] = jnp.where(
                middle, pltpu.roll(values[2 * direction + 1], TY // 2, 1), values[2 * direction])

    def add_middle(index):
        added = unpack_lanes(yn_in[1, index], yn_in[0, index])
        for first, more in zip(middle_rows, added):
            w[index, first : first + 48, :] += more

    def add_x_bands(index):
        middle = middle_lanes()
        for side_of, first in ((1, 0), (0, TX - 32)):
            plain, summed = xn_in[side_of, index], xc_in[side_of, index]
            w[index, first : first + 16, :] += jnp.where(middle, plain, summed)
            w[index, first + 16 : first + 32, :] += pltpu.roll(jnp.where(middle, summed, plain), TY // 2, 1)

    def send_group(group):
        planes_of(group, pack_corners)
        send_band(0, group)
        send_band(1, group)
        planes_of(group, pack_middle)
        send_band(2, group)

    send_group(0)
    relay_depth(0, True)
    relay_depth(1, True)
    def upper_rows(row):
        x1, y1 = without_above(h1, 0, s1, row)
        couple = MAGNETIC * rows_of(down_in[1], 2, row)
        x1 -= rows_of(down_in[1], 1, row) + couple * at(h1, 0, 1, row)
        y1 += rows_of(down_in[1], 0, row) - couple * at(h1, 1, 1, row)
        put(h2, 0, 1, row, x1)
        put(h2, 1, 1, row, y1)
        weights = weight(row)
        keep((HX, 1), row, x1, weights)
        keep((HY, 1), row, y1, weights)
        new_x, new_y = electric_xy(e1, h2, 1, row, x1, y1, at(h2, 0, 0, row), at(h2, 1, 0, row))
        keep((EX, 1), row, new_x, weights)
        keep((EY, 1), row, new_y, weights)
        keep((EZ, 1), row, electric_z(e1, h2, 1, row, x1), weights)

    def mix(row):
        turn_z = minus_x(under, 1, 0, row) - minus_y(at(under, 0, 0, row))
        put(mixed, 0, 0, row, MAGNETIC * rows_of(up_in[1], 2, row) * turn_z)

    def lower_rows(row):
        couple = MAGNETIC * rows_of(up_in[1], 2, row)
        under_x, under_y = at(under, 0, 0, row), at(under, 1, 0, row)
        under_x += rows_of(up_in[1], 0, row) - couple * under_x - plus_y(at(mixed, 0, 0, row)) - at(s1, 1, 0, row)
        under_y += rows_of(up_in[1], 1, row) - couple * under_y + plus_x(mixed, 0, 0, row) + at(s1, 0, 0, row)
        under_x = jnp.where(has_below, under_x, 0.0)
        under_y = jnp.where(has_below, under_y, 0.0)
        weights = weight(row)
        new_x, new_y = electric_xy(e1, h2, 0, row, at(h2, 0, 0, row), at(h2, 1, 0, row), under_x, under_y)
        keep((EX, 0), row, new_x, weights)
        keep((EY, 0), row, new_y, weights)

    def upper():
        wait_depth(1, False)
        row_tiles(upper_rows)
        send_group(1)

    def lower():
        wait_depth(1, True)
        row_tiles(mix)
        row_tiles(lower_rows)
        send_group(2)

    def sum_corners(group):
        wait_band(0, group)
        planes_of(group, add_corners)
        send_band(3, group)

    odd = lax.rem(sub, 2) == 1
    even = jnp.logical_not(odd)
    pl.when(odd)(lower)
    pl.when(even)(upper)
    sum_corners(0)
    pl.when(odd)(upper)
    pl.when(even)(lower)

    @pl.when(odd)
    def _():
        sum_corners(2)
        sum_corners(1)

    @pl.when(even)
    def _():
        sum_corners(1)
        sum_corners(2)

    for group in range(len(GROUPS)):
        wait_band(2, group)
        planes_of(group, add_middle)
        wait_band(1, group)
        wait_band(3, group)
        planes_of(group, add_x_bands)

    for turn in range(2):
        finish_depth(turn)
    for group in range(len(GROUPS)):
        for kind in range(4):
            for toward_next in (False, True):
                band_copy(kind, group, toward_next).wait_send()


def place(planes, out, sems):
    copies = [
        pltpu.make_async_copy(planes.at[index], out.at[0, comp, plane], sems.at[index])
        for index, (comp, plane) in enumerate(ORDER)
    ]
    for copy in copies:
        copy.start()
    for copy in copies:
        copy.wait()


def on_device(tiles, subs, seeds, material, decay, coupling):
    f32 = jnp.float32
    padded = (3, 2, PAD + TX + PAD, TY)
    planes = len(ORDER)
    narrow, wide = pltpu.VMEM((2, planes, 16, TY), f32), pltpu.VMEM((2, planes, 48, TY), f32)
    hbm = pl.BlockSpec(memory_space=pltpu.HBM)
    done = pl.pallas_call(
        functools.partial(kernel, tiles, subs),
        out_shape=jax.ShapeDtypeStruct((planes, TX, TY), f32),
        in_specs=[hbm] * 4,
        out_specs=pl.BlockSpec(memory_space=pltpu.VMEM),
        scratch_shapes=[
            pltpu.SMEM(decay.shape, f32),
            pltpu.SMEM(coupling.shape, f32),
            pltpu.VMEM((6, *padded[1:]), f32),
            pltpu.VMEM((2, TX, TY), jnp.int32),
            pltpu.VMEM((2, TX, TY), f32),
            pltpu.VMEM((2, TX, TY), f32),
            *[pltpu.VMEM(padded, f32)] * 5,
            *[pltpu.VMEM((count, 1, *padded[2:]), f32) for count in (1, 2, 1)],
            *[pltpu.VMEM((count, TX, TY), f32) for count in (2, 3)] * 4,
            *[pltpu.VMEM((count, MOST, TY), f32) for count in (2, 3)],
            narrow, wide, narrow, narrow,
            narrow, wide, narrow, narrow,
            pltpu.SemaphoreType.DMA((5,)),
            pltpu.SemaphoreType.DMA((4,)),
            pltpu.SemaphoreType.DMA((4,)),
            pltpu.SemaphoreType.DMA((2 * PARTS,)),
            pltpu.SemaphoreType.DMA((2 * PARTS,)),
            pltpu.SemaphoreType.DMA((2,)),
            pltpu.SemaphoreType.DMA((2,)),
            pltpu.SemaphoreType.DMA((8 * len(GROUPS),)),
            pltpu.SemaphoreType.DMA((8 * len(GROUPS),)),
        ],
        compiler_params=pltpu.CompilerParams(
            collective_id=0, has_side_effects=True, vmem_limit_bytes=20 * 2**20),
    )(*(pltpu.with_memory_space_constraint(array, pltpu.HBM) for array in (decay, coupling, seeds, material)))
    return pl.pallas_call(
        place,
        out_shape=jax.ShapeDtypeStruct(seeds.shape, f32),
        in_specs=[pl.BlockSpec(memory_space=pltpu.VMEM)],
        out_specs=hbm,
        scratch_shapes=[pltpu.SemaphoreType.DMA((planes,))],
        compiler_params=pltpu.CompilerParams(vmem_limit_bytes=4 * 2**20),
    )(done)


def solution(mesh):
    placed = (P("tile", None, "sub", None, None), P("tile", "sub", None, None), P(), P())
    return jax.shard_map(
        functools.partial(on_device, mesh.shape["tile"], mesh.shape["sub"]),
        mesh=mesh,
        in_specs=placed,
        out_specs=P("tile", None, "sub", None, None),
        check_vma=False,
    )
```

```python
import functools
import math

import jax
import jax.numpy as jnp
from jax import lax
from jax.experimental import pallas as pl
from jax.experimental.pallas import tpu as pltpu
from jax.sharding import PartitionSpec as P

BAND = 32
MESH = pl.DeviceIdType.MESH
MAGNETIC = 0.5
TX = 256
TY = 128
PAD = 8
ROWS = 32
EX, EY, EZ, HX, HY, HZ = range(6)

EARLY = ((HX, 0), (HY, 0), (HZ, 0), (HZ, 1), (EZ, 0))
LATE = ((HX, 1), (HY, 1), (EX, 0), (EY, 0), (EX, 1), (EY, 1), (EZ, 1))
ORDER = EARLY + LATE
GROUPS = ((0, len(EARLY)), (len(EARLY), len(LATE)))

RUN = 8
PARTS = 3
LINE = 4
DIRECT = 104
PIECES = (((104, 40), (144, 40), (184, 72)), ((104, 72), (176, 40), (216, 40)))
MOST = 72


def row_tiles(body):
    def step(index, carry):
        body(pl.multiple_of(index * ROWS, ROWS))
        return carry

    lax.fori_loop(0, TX // ROWS, step, 0, unroll=2)


def planes_of(group, body):
    first, count = GROUPS[group]

    def step(index, carry):
        body(index)
        return carry

    lax.fori_loop(first, first + count, step, 0, unroll=True)


def kernel(
    tiles, subs, decay_in, coupling_in, seeds, material, w,
    decay, coupling, field, mat, ca, cb, s0, s1, h1, h2, e1, decayed, under, mixed,
    up_out0, up_out1, down_out0, down_out1, up_in0, up_in1, down_in0, down_in1, relay_in0, relay_in1,
    yc_out, yn_out, xn_out, xc_out, yc_in, yn_in, xn_in, xc_in,
    load_sem, depth_send, depth_recv, part_send, part_recv, relay_recv, relay_send, band_send, band_recv, word_sem,
):
    tile = lax.axis_index("tile")
    sub = lax.axis_index("sub")
    side = math.isqrt(tiles)
    has_below = sub > 0
    has_above = sub < subs - 1
    below = jnp.maximum(sub - 1, 0)
    above = jnp.minimum(sub + 1, subs - 1)
    x_prev = lax.rem(tile + tiles - 1, tiles)
    x_next = lax.rem(tile + 1, tiles)
    y_prev = lax.rem(tile + tiles - side, tiles)
    y_next = lax.rem(tile + side, tiles)

    loads = [
        pltpu.make_async_copy(material.at[0], mat, load_sem.at[0]),
        pltpu.make_async_copy(seeds.at[0, 0:3], field.at[0:3, :, PAD : PAD + TX], load_sem.at[1]),
        pltpu.make_async_copy(seeds.at[0, 3:6], field.at[3:6, :, PAD : PAD + TX], load_sem.at[2]),
        pltpu.make_async_copy(decay_in, decay, load_sem.at[3]),
        pltpu.make_async_copy(coupling_in, coupling, load_sem.at[4]),
    ]
    for load in loads:
        load.start()

    barrier = pltpu.get_barrier_semaphore()

    def greet(other_tile, other_sub):
        pl.semaphore_signal(barrier, inc=1, device_id=(other_tile, other_sub), device_id_type=MESH)

    pl.when(has_below)(lambda: greet(tile, below))
    pl.when(has_above)(lambda: greet(tile, above))
    in_line = lax.rem(tile, LINE)
    for other in (y_prev, y_next):
        greet(other, sub)
    pl.when(in_line > 0)(lambda: greet(x_prev, sub))
    pl.when(in_line < LINE - 1)(lambda: greet(x_next, sub))
    place_in_run = lax.rem(sub, RUN)
    start = sub - place_in_run
    run_above = start + RUN < subs
    run_below = start > 0
    crosses_up = jnp.logical_and(place_in_run == RUN - 1, run_above)
    crosses_down = jnp.logical_and(place_in_run == 0, run_below)

    def relays(upward, part):
        return jnp.logical_and(place_in_run == 2 * part + (1 if upward else 2), run_above if upward else run_below)

    last_here = start + RUN - 1
    first_above = jnp.minimum(start + RUN, subs - 1)
    last_below = jnp.maximum(start - 1, 0)

    def up_relay(part):
        return start + 2 * part + 1

    def down_relay(part):
        return start + 2 * part + 2

    for part in range(PARTS):
        pl.when(relays(True, part))(lambda: greet(tile, last_here))
        pl.when(relays(False, part))(lambda: greet(tile, start))

    lane = lax.broadcasted_iota(jnp.int32, (ROWS, TY), 1)
    not_last = lane < TY - 1
    not_first = lane > 0
    zeros_pad = jnp.zeros((PAD, TY), jnp.float32)
    for comp in range(3):
        for plane in range(2):
            for buf in (s0, s1):
                buf[comp, plane, PAD + TX : PAD + TX + PAD, :] = zeros_pad
            for buf in (h1, h2):
                buf[comp, plane, 0:PAD, :] = zeros_pad
    for buf in (decayed, mixed):
        buf[0, 0, PAD + TX : PAD + TX + PAD, :] = zeros_pad
    under[1, 0, 0:PAD, :] = zeros_pad
    up_out, down_out = (up_out0, up_out1), (down_out0, down_out1)
    up_in, down_in, relay_in = (up_in0, up_in1), (down_in0, down_in1), (relay_in0, relay_in1)

    def at(buf, comp, plane, row):
        return buf[comp, plane, pl.ds(PAD + row, ROWS), :]

    def put(buf, comp, plane, row, value):
        buf[comp, plane, pl.ds(PAD + row, ROWS), :] = value

    def plus_x(buf, comp, plane, row):
        return buf[comp, plane, pl.ds(PAD + row + 1, ROWS), :] - at(buf, comp, plane, row)

    def minus_x(buf, comp, plane, row):
        return at(buf, comp, plane, row) - buf[comp, plane, pl.ds(PAD + row - 1, ROWS), :]

    def plus_y(value):
        return jnp.where(not_last, pltpu.roll(value, TY - 1, 1), 0.0) - value

    def minus_y(value):
        return value - jnp.where(not_first, pltpu.roll(value, 1, 1), 0.0)

    def curl_z(buf, plane, row):
        return plus_x(buf, 1, plane, row) - plus_y(at(buf, 0, plane, row))

    ramp_lane = lane.astype(jnp.float32) + 0.5
    ramp_y = jnp.minimum(jnp.minimum(ramp_lane, TY - ramp_lane) * (1.0 / BAND), 1.0)
    row_iota = lax.broadcasted_iota(jnp.int32, (ROWS, TY), 0)

    def weight(row):
        position = (row_iota + row).astype(jnp.float32) + 0.5
        return jnp.minimum(jnp.minimum(position, TX - position) * (1.0 / BAND), 1.0) * ramp_y

    def rows_of(buf, index, row):
        return buf[index, pl.ds(row, ROWS), :]

    def depth_rows(turn, upward, first, count):
        return (up_out if upward else down_out)[turn].at[:, first : first + count]

    def depth_copy(turn, upward, count):
        slot = turn * 2 + int(upward)
        return pltpu.make_async_remote_copy(
            depth_rows(turn, upward, 0, count), (up_in if upward else down_in)[turn].at[:, 0:count],
            depth_send.at[slot], depth_recv.at[slot],
            device_id=(tile, above if upward else below), device_id_type=MESH)

    def part_copy(turn, upward, part):
        relay = up_relay(part) if upward else down_relay(part)
        first, count = PIECES[int(upward)][part]
        return pltpu.make_async_remote_copy(
            depth_rows(turn, upward, first, count), relay_in[turn].at[:, 0:count],
            part_send.at[turn * PARTS + part], relay_recv.at[turn],
            device_id=(tile, relay), device_id_type=MESH)

    def relay_copy(turn, upward, part):
        first, count = PIECES[int(upward)][part]
        return pltpu.make_async_remote_copy(
            relay_in[turn].at[:, 0:count], (up_in if upward else down_in)[turn].at[:, first : first + count],
            relay_send.at[turn], part_recv.at[turn * PARTS + part],
            device_id=(tile, first_above if upward else last_below), device_id_type=MESH)

    def send_depth(turn, upward):
        crosses = crosses_up if upward else crosses_down
        plain = jnp.logical_and(has_above if upward else has_below, jnp.logical_not(crosses))

        pl.when(plain)(lambda: depth_copy(turn, upward, TX).start())

        @pl.when(crosses)
        def _():
            for part in (1, 0, 2) if not upward else (1, 2, 0):
                part_copy(turn, upward, part).start()
            depth_copy(turn, upward, DIRECT).start()

    late_up = start == 0

    def relay_depth(turn, late):
        for upward in (True, False):
            if late and not upward:
                continue
            for part in range(PARTS):
                now = relays(upward, part)
                if upward:
                    now = jnp.logical_and(now, late_up if late else jnp.logical_not(late_up))

                @pl.when(now)
                def _():
                    part_copy(turn, upward, part).wait_recv()
                    relay_copy(turn, upward, part).start()

    def wait_depth(turn):
        for upward, crosses in ((True, crosses_down), (False, crosses_up)):
            plain = jnp.logical_and(has_below if upward else has_above, jnp.logical_not(crosses))
            pl.when(plain)(lambda: depth_copy(turn, upward, TX).wait_recv())

            @pl.when(crosses)
            def _():
                depth_copy(turn, upward, DIRECT).wait_recv()
                for part in range(PARTS):
                    relay_copy(turn, upward, part).wait_recv()

    def finish_depth(turn):
        for upward, crosses in ((True, crosses_up), (False, crosses_down)):
            plain = jnp.logical_and(has_above if upward else has_below, jnp.logical_not(crosses))
            pl.when(plain)(lambda: depth_copy(turn, upward, TX).wait_send())

            @pl.when(crosses)
            def _():
                for part in range(PARTS):
                    part_copy(turn, upward, part).wait_send()
                depth_copy(turn, upward, DIRECT).wait_send()

            for part in range(PARTS):
                pl.when(relays(upward, part))(lambda: relay_copy(turn, upward, part).wait_send())

    def band_copy(kind, group, toward_next):
        first, count = GROUPS[group]
        source, target = ((yc_out, yc_in), (xn_out, xn_in), (yn_out, yn_in), (xc_out, xc_in))[kind]
        direction = int(toward_next)
        if kind in (0, 2):
            other = y_next if toward_next else y_prev
        else:
            other = x_next if toward_next else x_prev
        slot = (kind * 2 + group) * 2 + direction
        part = slice(first, first + count)
        return pltpu.make_async_remote_copy(
            source.at[direction, part], target.at[direction, part],
            band_send.at[slot], band_recv.at[slot],
            device_id=(other, sub), device_id_type=MESH)

    def send_band(kind, group):
        for toward_next in (False, True):
            band_copy(kind, group, toward_next).start()

    def wait_band(kind, group):
        for toward_next in (False, True):
            band_copy(kind, group, toward_next).wait_recv()

    for number in (3, 4, 0, 1):
        loads[number].wait()
    d0, d1, d2, d3 = (decay[i] for i in range(4))
    c0, c1, c2, c3 = (coupling[i] for i in range(4))

    def scale(row):
        for plane in range(2):
            label = mat[plane, pl.ds(row, ROWS), :]
            is0, is1, is2 = label == 0, label == 1, label == 2
            couple = jnp.where(is0, c0, jnp.where(is1, c1, jnp.where(is2, c2, c3)))
            decays = jnp.where(is0, d0, jnp.where(is1, d1, jnp.where(is2, d2, d3)))
            cb[plane, pl.ds(row, ROWS), :] = couple
            ca[plane, pl.ds(row, ROWS), :] = decays
            (down_out, up_out)[plane][1][2, pl.ds(row, ROWS), :] = couple
            scaled = [couple * at(field, comp, plane, row) for comp in range(3)]
            for comp in range(3):
                put(s0, comp, plane, row, scaled[comp])
            if plane == 0:
                for comp in range(2):
                    down_out[0][comp, pl.ds(row, ROWS), :] = scaled[comp]
            else:
                put(decayed, 0, 0, row, decays * scaled[2])

    row_tiles(scale)
    count = lambda flag, number: jnp.where(flag, number, 0)
    crosses_any = jnp.logical_or(crosses_up, crosses_down)
    pl.semaphore_wait(barrier, 3 + count(jnp.logical_and(in_line > 0, in_line < LINE - 1), 1) + count(has_below, 1) + count(has_above, 1) + count(crosses_any, PARTS))
    def pass_word(step):
        for onward in range(2):
            place = step if onward else LINE - 1 - step

            @pl.when(in_line == place)
            def _():
                if step > 0:
                    pl.semaphore_wait(word_sem.at[onward], 1)
                if step < LINE - 1:
                    pl.semaphore_signal(
                        word_sem.at[onward], inc=1, device_id=(x_next if onward else x_prev, sub), device_id_type=MESH)

    send_depth(0, False)
    pass_word(0)
    loads[2].wait()

    def without_above(hbuf, offset, sbuf, row):
        s_x, s_y, s_z = (at(sbuf, comp, 1, row) for comp in range(3))
        part_x = at(hbuf, offset, 1, row) + plus_y(s_z) + s_y
        part_y = at(hbuf, offset + 1, 1, row) - s_x - plus_x(sbuf, 2, 1, row)
        return part_x, part_y

    def first_partial(row):
        up_out[0][0, pl.ds(row, ROWS), :], up_out[0][1, pl.ds(row, ROWS), :] = without_above(field, HX, s0, row)

    row_tiles(first_partial)
    send_depth(0, True)

    def magnetic_local(hbuf, offset, sbuf, row):
        s_x0, s_y0, s_z0 = (at(sbuf, comp, 0, row) for comp in range(3))
        new_x = at(hbuf, offset, 0, row) + plus_y(s_z0) - (at(sbuf, 1, 1, row) - s_y0)
        new_y = at(hbuf, offset + 1, 0, row) + (at(sbuf, 0, 1, row) - s_x0) - plus_x(sbuf, 2, 0, row)
        new_z = at(hbuf, offset + 2, 0, row) + curl_z(sbuf, 0, row)
        new_z1 = at(hbuf, offset + 2, 1, row) + curl_z(sbuf, 1, row)
        return new_x, new_y, new_z, new_z1

    def first_local(row):
        new_x, new_y, new_z, new_z1 = magnetic_local(field, HX, s0, row)
        put(h1, 0, 0, row, new_x)
        put(h1, 1, 0, row, new_y)
        put(h1, 2, 0, row, new_z)
        put(h1, 2, 1, row, new_z1)

    row_tiles(first_local)

    def second_terms(row):
        h_x, h_y = at(h1, 0, 0, row), at(h1, 1, 0, row)
        decays, couple = rows_of(ca, 1, row), rows_of(cb, 1, row)
        part_x = decays * at(field, EX, 1, row) - MAGNETIC * (minus_y(at(h1, 2, 1, row)) + h_y)
        part_y = decays * at(field, EY, 1, row) + MAGNETIC * (h_x + minus_x(h1, 2, 1, row))
        up_out[1][0, pl.ds(row, ROWS), :] = plus_y(at(decayed, 0, 0, row)) + couple * part_y
        up_out[1][1, pl.ds(row, ROWS), :] = -couple * part_x - plus_x(decayed, 0, 0, row)
        decays, couple = rows_of(ca, 0, row), rows_of(cb, 0, row)
        down_out[1][0, pl.ds(row, ROWS), :] = couple * (
            decays * at(field, EX, 0, row) - MAGNETIC * (minus_y(at(h1, 2, 0, row)) - h_y))
        down_out[1][1, pl.ds(row, ROWS), :] = couple * (
            decays * at(field, EY, 0, row) - MAGNETIC * (h_x - minus_x(h1, 2, 0, row)))

    row_tiles(second_terms)
    send_depth(1, False)
    send_depth(1, True)

    @pl.when(jnp.logical_not(has_above))
    def _():
        def clear(row):
            for buf in down_in:
                for comp in range(buf.shape[0]):
                    buf[comp, pl.ds(row, ROWS), :] = jnp.zeros((ROWS, TY), jnp.float32)

        row_tiles(clear)

    @pl.when(jnp.logical_not(has_below))
    def _():
        def cancel(row):
            up_in[0][0, pl.ds(row, ROWS), :] = at(s0, 1, 0, row)
            up_in[0][1, pl.ds(row, ROWS), :] = -at(s0, 0, 0, row)
            for comp in range(3):
                up_in[1][comp, pl.ds(row, ROWS), :] = jnp.zeros((ROWS, TY), jnp.float32)

        row_tiles(cancel)

    def electric_xy(ebuf, hbuf, plane, row, h_x, h_y, under_x, under_y):
        h_z = at(hbuf, 2, plane, row)
        decays = rows_of(ca, plane, row)
        new_x = decays * at(ebuf, 0, plane, row) - MAGNETIC * (minus_y(h_z) - (h_y - under_y))
        new_y = decays * at(ebuf, 1, plane, row) - MAGNETIC * ((h_x - under_x) - minus_x(hbuf, 2, plane, row))
        return new_x, new_y

    def electric_z(ebuf, hbuf, plane, row, h_x):
        decays = rows_of(ca, plane, row)
        return decays * at(ebuf, 2, plane, row) - MAGNETIC * (minus_x(hbuf, 1, plane, row) - minus_y(h_x))

    pass_word(1)
    relay_depth(0, False)
    wait_depth(0)
    relay_depth(1, False)
    pass_word(2)

    def first_rest(row):
        x1 = rows_of(up_out[0], 0, row) - rows_of(down_in[0], 1, row)
        y1 = rows_of(up_out[0], 1, row) + rows_of(down_in[0], 0, row)
        under_x = rows_of(up_in[0], 0, row) - at(s0, 1, 0, row)
        under_y = rows_of(up_in[0], 1, row) + at(s0, 0, 0, row)
        put(h1, 0, 1, row, x1)
        put(h1, 1, 1, row, y1)
        put(under, 0, 0, row, under_x)
        put(under, 1, 0, row, under_y)
        x0, y0 = at(h1, 0, 0, row), at(h1, 1, 0, row)
        for plane, (h_x, h_y, b_x, b_y) in enumerate(((x0, y0, under_x, under_y), (x1, y1, x0, y0))):
            new = (*electric_xy(field, h1, plane, row, h_x, h_y, b_x, b_y), electric_z(field, h1, plane, row, h_x))
            couple = rows_of(cb, plane, row)
            for comp in range(3):
                put(e1, comp, plane, row, new[comp])
                put(s1, comp, plane, row, couple * new[comp])

    row_tiles(first_rest)

    def keep(name, row, value, weights):
        w[ORDER.index(name), pl.ds(row, ROWS), :] = value * weights

    def second_local(row):
        new_x, new_y, new_z, new_z1 = magnetic_local(h1, 0, s1, row)
        put(h2, 0, 0, row, new_x)
        put(h2, 1, 0, row, new_y)
        put(h2, 2, 0, row, new_z)
        put(h2, 2, 1, row, new_z1)
        weights = weight(row)
        keep((HX, 0), row, new_x, weights)
        keep((HY, 0), row, new_y, weights)
        keep((HZ, 0), row, new_z, weights)
        keep((HZ, 1), row, new_z1, weights)
        keep((EZ, 0), row, electric_z(e1, h2, 0, row, new_x), weights)

    row_tiles(second_local)

    def slot_of(rows):
        return lax.broadcasted_iota(jnp.int32, (rows, TY), 1) // BAND

    def pack_lanes(values):
        slot = slot_of(values[0].shape[0])
        turned = [values[0]] + [pltpu.roll(values[k], BAND * k, 1) for k in (1, 2, 3)]
        low, high = turned[3], turned[0]
        for k in (2, 1, 0):
            low = jnp.where(slot == k, turned[k], low)
            high = jnp.where(slot == k, turned[k + 1], high)
        return low, high

    def unpack_lanes(low_side, high_side):
        slot = slot_of(low_side.shape[0])
        turned = []
        for k in range(4):
            mixed = jnp.where(slot == (k + 3) % 4, low_side, high_side)
            shift = (TY - BAND * (k - 1)) % TY
            turned.append(pltpu.roll(mixed, shift, 1) if shift else mixed)
        return [jnp.where(slot == 0, turned[k], jnp.where(slot == 3, turned[(k + 2) % 4], 0.0)) for k in range(4)]

    corner_rows = (0, 16, TX - 32, TX - 16)
    middle_rows = (32, 80, 128, 176)

    def middle_lanes():
        slot = slot_of(16)
        return jnp.logical_or(slot == 1, slot == 2)

    def pack_corners(index):
        values = [w[index, first : first + 16, :] for first in corner_rows]
        low, high = pack_lanes(values)
        yc_out[0, index], yc_out[1, index] = low, high
        middle = middle_lanes()
        for direction in range(2):
            xn_out[direction, index] = jnp.where(
                middle, values[2 * direction], pltpu.roll(values[2 * direction + 1], TY // 2, 1))

    def pack_middle(index):
        low, high = pack_lanes([w[index, first : first + 48, :] for first in middle_rows])
        yn_out[0, index], yn_out[1, index] = low, high

    def add_corners(index):
        added = unpack_lanes(yc_in[1, index], yc_in[0, index])
        values = []
        for first, more in zip(corner_rows, added):
            total = w[index, first : first + 16, :] + more
            w[index, first : first + 16, :] = total
            values.append(total)
        middle = middle_lanes()
        for direction in range(2):
            xc_out[direction, index] = jnp.where(
                middle, pltpu.roll(values[2 * direction + 1], TY // 2, 1), values[2 * direction])

    def add_middle(index):
        added = unpack_lanes(yn_in[1, index], yn_in[0, index])
        for first, more in zip(middle_rows, added):
            w[index, first : first + 48, :] += more

    def add_x_bands(index):
        middle = middle_lanes()
        for side_of, first in ((1, 0), (0, TX - 32)):
            plain, summed = xn_in[side_of, index], xc_in[side_of, index]
            w[index, first : first + 16, :] += jnp.where(middle, plain, summed)
            w[index, first + 16 : first + 32, :] += pltpu.roll(jnp.where(middle, summed, plain), TY // 2, 1)

    def send_group(group):
        planes_of(group, pack_corners)
        send_band(0, group)
        send_band(1, group)
        planes_of(group, pack_middle)
        send_band(2, group)

    pass_word(LINE - 1)
    send_group(0)
    relay_depth(0, True)
    relay_depth(1, True)
    wait_depth(1)

    def mix(row):
        turn_z = minus_x(under, 1, 0, row) - minus_y(at(under, 0, 0, row))
        put(mixed, 0, 0, row, MAGNETIC * rows_of(up_in[1], 2, row) * turn_z)

    row_tiles(mix)

    def second_rest(row):
        x1, y1 = without_above(h1, 0, s1, row)
        couple = MAGNETIC * rows_of(down_in[1], 2, row)
        x1 -= rows_of(down_in[1], 1, row) + couple * at(h1, 0, 1, row)
        y1 += rows_of(down_in[1], 0, row) - couple * at(h1, 1, 1, row)
        couple = MAGNETIC * rows_of(up_in[1], 2, row)
        under_x, under_y = at(under, 0, 0, row), at(under, 1, 0, row)
        under_x += rows_of(up_in[1], 0, row) - couple * under_x - plus_y(at(mixed, 0, 0, row)) - at(s1, 1, 0, row)
        under_y += rows_of(up_in[1], 1, row) - couple * under_y + plus_x(mixed, 0, 0, row) + at(s1, 0, 0, row)
        under_x = jnp.where(has_below, under_x, 0.0)
        under_y = jnp.where(has_below, under_y, 0.0)
        put(h2, 0, 1, row, x1)
        put(h2, 1, 1, row, y1)
        x0, y0 = at(h2, 0, 0, row), at(h2, 1, 0, row)
        weights = weight(row)
        keep((HX, 1), row, x1, weights)
        keep((HY, 1), row, y1, weights)
        for plane, (h_x, h_y, b_x, b_y) in enumerate(((x0, y0, under_x, under_y), (x1, y1, x0, y0))):
            new_x, new_y = electric_xy(e1, h2, plane, row, h_x, h_y, b_x, b_y)
            keep((EX, plane), row, new_x, weights)
            keep((EY, plane), row, new_y, weights)
        keep((EZ, 1), row, electric_z(e1, h2, 1, row, x1), weights)

    row_tiles(second_rest)
    send_group(1)

    for group in range(2):
        wait_band(0, group)
        planes_of(group, add_corners)
        send_band(3, group)

    for group in range(2):
        wait_band(2, group)
        planes_of(group, add_middle)
        wait_band(1, group)
        wait_band(3, group)
        planes_of(group, add_x_bands)

    for turn in range(2):
        finish_depth(turn)
    for group in range(2):
        for kind in range(4):
            for toward_next in (False, True):
                band_copy(kind, group, toward_next).wait_send()


def place(planes, out, sems):
    copies = [
        pltpu.make_async_copy(planes.at[index], out.at[0, comp, plane], sems.at[index])
        for index, (comp, plane) in enumerate(ORDER)
    ]
    for copy in copies:
        copy.start()
    for copy in copies:
        copy.wait()


def on_device(tiles, subs, seeds, material, decay, coupling):
    f32 = jnp.float32
    padded = (3, 2, PAD + TX + PAD, TY)
    planes = len(ORDER)
    narrow, wide = pltpu.VMEM((2, planes, 16, TY), f32), pltpu.VMEM((2, planes, 48, TY), f32)
    hbm = pl.BlockSpec(memory_space=pltpu.HBM)
    done = pl.pallas_call(
        functools.partial(kernel, tiles, subs),
        out_shape=jax.ShapeDtypeStruct((planes, TX, TY), f32),
        in_specs=[hbm] * 4,
        out_specs=pl.BlockSpec(memory_space=pltpu.VMEM),
        scratch_shapes=[
            pltpu.SMEM(decay.shape, f32),
            pltpu.SMEM(coupling.shape, f32),
            pltpu.VMEM((6, *padded[1:]), f32),
            pltpu.VMEM((2, TX, TY), jnp.int32),
            pltpu.VMEM((2, TX, TY), f32),
            pltpu.VMEM((2, TX, TY), f32),
            *[pltpu.VMEM(padded, f32)] * 5,
            *[pltpu.VMEM((count, 1, *padded[2:]), f32) for count in (1, 2, 1)],
            *[pltpu.VMEM((count, TX, TY), f32) for count in (2, 3)] * 4,
            *[pltpu.VMEM((count, MOST, TY), f32) for count in (2, 3)],
            narrow, wide, narrow, narrow,
            narrow, wide, narrow, narrow,
            pltpu.SemaphoreType.DMA((5,)),
            pltpu.SemaphoreType.DMA((4,)),
            pltpu.SemaphoreType.DMA((4,)),
            pltpu.SemaphoreType.DMA((2 * PARTS,)),
            pltpu.SemaphoreType.DMA((2 * PARTS,)),
            pltpu.SemaphoreType.DMA((2,)),
            pltpu.SemaphoreType.DMA((2,)),
            pltpu.SemaphoreType.DMA((16,)),
            pltpu.SemaphoreType.DMA((16,)),
            pltpu.SemaphoreType.REGULAR((2,)),
        ],
        compiler_params=pltpu.CompilerParams(
            collective_id=0, has_side_effects=True, vmem_limit_bytes=20 * 2**20),
    )(*(pltpu.with_memory_space_constraint(array, pltpu.HBM) for array in (decay, coupling, seeds, material)))
    return pl.pallas_call(
        place,
        out_shape=jax.ShapeDtypeStruct(seeds.shape, f32),
        in_specs=[pl.BlockSpec(memory_space=pltpu.VMEM)],
        out_specs=hbm,
        scratch_shapes=[pltpu.SemaphoreType.DMA((planes,))],
        compiler_params=pltpu.CompilerParams(vmem_limit_bytes=4 * 2**20),
    )(done)


def solution(mesh):
    placed = (P("tile", None, "sub", None, None), P("tile", "sub", None, None), P(), P())
    return jax.shard_map(
        functools.partial(on_device, mesh.shape["tile"], mesh.shape["sub"]),
        mesh=mesh,
        in_specs=placed,
        out_specs=P("tile", None, "sub", None, None),
        check_vma=False,
    )
```

```python
import functools
import math

import jax
import jax.numpy as jnp
from jax import lax
from jax.experimental import pallas as pl
from jax.experimental.pallas import tpu as pltpu
from jax.sharding import PartitionSpec as P

BAND = 32
MESH = pl.DeviceIdType.MESH
MAGNETIC = 0.5
TX = 256
TY = 128
PAD = 8
ROWS = 32
EX, EY, EZ, HX, HY, HZ = range(6)

EARLY = ((HX, 0), (HY, 0), (HZ, 0), (HZ, 1), (EZ, 0))
LATE = ((HX, 1), (HY, 1), (EX, 0), (EY, 0), (EX, 1), (EY, 1), (EZ, 1))
ORDER = EARLY + LATE
GROUPS = ((0, len(EARLY)), (len(EARLY), len(LATE)))

RUN = 8
PARTS = 3
LINE = 4
DIRECT = 104
PIECES = (((104, 40), (144, 40), (184, 72)), ((104, 72), (176, 40), (216, 40)))
MOST = 72


def row_tiles(body):
    def step(index, carry):
        body(pl.multiple_of(index * ROWS, ROWS))
        return carry

    lax.fori_loop(0, TX // ROWS, step, 0, unroll=2)


def planes_of(group, body):
    first, count = GROUPS[group]

    def step(index, carry):
        body(index)
        return carry

    lax.fori_loop(first, first + count, step, 0, unroll=True)


def kernel(
    tiles, subs, decay_in, coupling_in, seeds, material, w,
    decay, coupling, field, mat, ca, cb, s0, s1, h1, h2, e1, decayed, under, mixed,
    up_out0, up_out1, down_out0, down_out1, up_in0, up_in1, down_in0, down_in1, relay_in0, relay_in1,
    yc_out, yn_out, xn_out, xc_out, yc_in, yn_in, xn_in, xc_in,
    load_sem, depth_send, depth_recv, part_send, part_recv, relay_recv, relay_send, band_send, band_recv, word_sem,
):
    tile = lax.axis_index("tile")
    sub = lax.axis_index("sub")
    side = math.isqrt(tiles)
    has_below = sub > 0
    has_above = sub < subs - 1
    below = jnp.maximum(sub - 1, 0)
    above = jnp.minimum(sub + 1, subs - 1)
    x_prev = lax.rem(tile + tiles - 1, tiles)
    x_next = lax.rem(tile + 1, tiles)
    y_prev = lax.rem(tile + tiles - side, tiles)
    y_next = lax.rem(tile + side, tiles)

    loads = [
        pltpu.make_async_copy(material.at[0], mat, load_sem.at[0]),
        pltpu.make_async_copy(seeds.at[0, 0:3], field.at[0:3, :, PAD : PAD + TX], load_sem.at[1]),
        pltpu.make_async_copy(seeds.at[0, 3:6], field.at[3:6, :, PAD : PAD + TX], load_sem.at[2]),
        pltpu.make_async_copy(decay_in, decay, load_sem.at[3]),
        pltpu.make_async_copy(coupling_in, coupling, load_sem.at[4]),
    ]
    barrier = pltpu.get_barrier_semaphore()

    def greet(other_tile, other_sub):
        pl.semaphore_signal(barrier, inc=1, device_id=(other_tile, other_sub), device_id_type=MESH)

    pl.when(has_below)(lambda: greet(tile, below))
    pl.when(has_above)(lambda: greet(tile, above))
    for load in loads:
        load.start()
    in_line = lax.rem(tile, LINE)
    for other in (y_prev, y_next):
        greet(other, sub)
    pl.when(in_line > 0)(lambda: greet(x_prev, sub))
    pl.when(in_line < LINE - 1)(lambda: greet(x_next, sub))
    place_in_run = lax.rem(sub, RUN)
    start = sub - place_in_run
    run_above = start + RUN < subs
    run_below = start > 0
    crosses_up = jnp.logical_and(place_in_run == RUN - 1, run_above)
    crosses_down = jnp.logical_and(place_in_run == 0, run_below)

    def relays(upward, part):
        return jnp.logical_and(place_in_run == 2 * part + (1 if upward else 2), run_above if upward else run_below)

    last_here = start + RUN - 1
    first_above = jnp.minimum(start + RUN, subs - 1)
    last_below = jnp.maximum(start - 1, 0)

    def up_relay(part):
        return start + 2 * part + 1

    def down_relay(part):
        return start + 2 * part + 2

    for part in range(PARTS):
        pl.when(relays(True, part))(lambda: greet(tile, last_here))
        pl.when(relays(False, part))(lambda: greet(tile, start))

    lane = lax.broadcasted_iota(jnp.int32, (ROWS, TY), 1)
    not_last = lane < TY - 1
    not_first = lane > 0
    zeros_pad = jnp.zeros((PAD, TY), jnp.float32)
    for comp in range(3):
        for plane in range(2):
            for buf in (s0, s1):
                buf[comp, plane, PAD + TX : PAD + TX + PAD, :] = zeros_pad
            for buf in (h1, h2):
                buf[comp, plane, 0:PAD, :] = zeros_pad
    for buf in (decayed, mixed):
        buf[0, 0, PAD + TX : PAD + TX + PAD, :] = zeros_pad
    under[1, 0, 0:PAD, :] = zeros_pad
    up_out, down_out = (up_out0, up_out1), (down_out0, down_out1)
    up_in, down_in, relay_in = (up_in0, up_in1), (down_in0, down_in1), (relay_in0, relay_in1)

    def at(buf, comp, plane, row):
        return buf[comp, plane, pl.ds(PAD + row, ROWS), :]

    def put(buf, comp, plane, row, value):
        buf[comp, plane, pl.ds(PAD + row, ROWS), :] = value

    def plus_x(buf, comp, plane, row):
        return buf[comp, plane, pl.ds(PAD + row + 1, ROWS), :] - at(buf, comp, plane, row)

    def minus_x(buf, comp, plane, row):
        return at(buf, comp, plane, row) - buf[comp, plane, pl.ds(PAD + row - 1, ROWS), :]

    def plus_y(value):
        return jnp.where(not_last, pltpu.roll(value, TY - 1, 1), 0.0) - value

    def minus_y(value):
        return value - jnp.where(not_first, pltpu.roll(value, 1, 1), 0.0)

    def curl_z(buf, plane, row):
        return plus_x(buf, 1, plane, row) - plus_y(at(buf, 0, plane, row))

    ramp_lane = lane.astype(jnp.float32) + 0.5
    ramp_y = jnp.minimum(jnp.minimum(ramp_lane, TY - ramp_lane) * (1.0 / BAND), 1.0)
    row_iota = lax.broadcasted_iota(jnp.int32, (ROWS, TY), 0)

    def weight(row):
        position = (row_iota + row).astype(jnp.float32) + 0.5
        return jnp.minimum(jnp.minimum(position, TX - position) * (1.0 / BAND), 1.0) * ramp_y

    def rows_of(buf, index, row):
        return buf[index, pl.ds(row, ROWS), :]

    def depth_rows(turn, upward, first, count):
        return (up_out if upward else down_out)[turn].at[:, first : first + count]

    def depth_copy(turn, upward, count):
        slot = turn * 2 + int(upward)
        return pltpu.make_async_remote_copy(
            depth_rows(turn, upward, 0, count), (up_in if upward else down_in)[turn].at[:, 0:count],
            depth_send.at[slot], depth_recv.at[slot],
            device_id=(tile, above if upward else below), device_id_type=MESH)

    def part_copy(turn, upward, part):
        relay = up_relay(part) if upward else down_relay(part)
        first, count = PIECES[int(upward)][part]
        return pltpu.make_async_remote_copy(
            depth_rows(turn, upward, first, count), relay_in[turn].at[:, 0:count],
            part_send.at[turn * PARTS + part], relay_recv.at[turn],
            device_id=(tile, relay), device_id_type=MESH)

    def relay_copy(turn, upward, part):
        first, count = PIECES[int(upward)][part]
        return pltpu.make_async_remote_copy(
            relay_in[turn].at[:, 0:count], (up_in if upward else down_in)[turn].at[:, first : first + count],
            relay_send.at[turn], part_recv.at[turn * PARTS + part],
            device_id=(tile, first_above if upward else last_below), device_id_type=MESH)

    def send_depth(turn, upward):
        crosses = crosses_up if upward else crosses_down
        plain = jnp.logical_and(has_above if upward else has_below, jnp.logical_not(crosses))

        pl.when(plain)(lambda: depth_copy(turn, upward, TX).start())

        @pl.when(crosses)
        def _():
            for part in (1, 0, 2) if not upward else (1, 2, 0):
                part_copy(turn, upward, part).start()
            depth_copy(turn, upward, DIRECT).start()

    late_up = start + 2 * RUN < subs

    def relay_depth(turn, late):
        for upward in (True, False):
            if late and not upward:
                continue
            for part in range(PARTS):
                now = relays(upward, part)
                if upward:
                    now = jnp.logical_and(now, late_up if late else jnp.logical_not(late_up))

                @pl.when(now)
                def _():
                    part_copy(turn, upward, part).wait_recv()
                    relay_copy(turn, upward, part).start()

    def wait_depth(turn):
        for upward, crosses in ((True, crosses_down), (False, crosses_up)):
            plain = jnp.logical_and(has_below if upward else has_above, jnp.logical_not(crosses))
            pl.when(plain)(lambda: depth_copy(turn, upward, TX).wait_recv())

            @pl.when(crosses)
            def _():
                depth_copy(turn, upward, DIRECT).wait_recv()
                for part in range(PARTS):
                    relay_copy(turn, upward, part).wait_recv()

    def finish_depth(turn):
        for upward, crosses in ((True, crosses_up), (False, crosses_down)):
            plain = jnp.logical_and(has_above if upward else has_below, jnp.logical_not(crosses))
            pl.when(plain)(lambda: depth_copy(turn, upward, TX).wait_send())

            @pl.when(crosses)
            def _():
                for part in range(PARTS):
                    part_copy(turn, upward, part).wait_send()
                depth_copy(turn, upward, DIRECT).wait_send()

            for part in range(PARTS):
                pl.when(relays(upward, part))(lambda: relay_copy(turn, upward, part).wait_send())

    def band_copy(kind, group, toward_next):
        first, count = GROUPS[group]
        source, target = ((yc_out, yc_in), (xn_out, xn_in), (yn_out, yn_in), (xc_out, xc_in))[kind]
        direction = int(toward_next)
        if kind in (0, 2):
            other = y_next if toward_next else y_prev
        else:
            other = x_next if toward_next else x_prev
        slot = (kind * 2 + group) * 2 + direction
        part = slice(first, first + count)
        return pltpu.make_async_remote_copy(
            source.at[direction, part], target.at[direction, part],
            band_send.at[slot], band_recv.at[slot],
            device_id=(other, sub), device_id_type=MESH)

    def send_band(kind, group):
        for toward_next in (False, True):
            band_copy(kind, group, toward_next).start()

    def wait_band(kind, group):
        for toward_next in (False, True):
            band_copy(kind, group, toward_next).wait_recv()

    for number in (3, 4, 0, 1):
        loads[number].wait()
    d0, d1, d2, d3 = (decay[i] for i in range(4))
    c0, c1, c2, c3 = (coupling[i] for i in range(4))

    def scale(row):
        for plane in range(2):
            label = mat[plane, pl.ds(row, ROWS), :]
            is0, is1, is2 = label == 0, label == 1, label == 2
            couple = jnp.where(is0, c0, jnp.where(is1, c1, jnp.where(is2, c2, c3)))
            decays = jnp.where(is0, d0, jnp.where(is1, d1, jnp.where(is2, d2, d3)))
            cb[plane, pl.ds(row, ROWS), :] = couple
            ca[plane, pl.ds(row, ROWS), :] = decays
            (down_out, up_out)[plane][1][2, pl.ds(row, ROWS), :] = couple
            scaled = [couple * at(field, comp, plane, row) for comp in range(3)]
            for comp in range(3):
                put(s0, comp, plane, row, scaled[comp])
            if plane == 0:
                for comp in range(2):
                    down_out[0][comp, pl.ds(row, ROWS), :] = scaled[comp]
            else:
                put(decayed, 0, 0, row, decays * scaled[2])

    row_tiles(scale)
    count = lambda flag, number: jnp.where(flag, number, 0)
    crosses_any = jnp.logical_or(crosses_up, crosses_down)
    pl.semaphore_wait(barrier, 3 + count(jnp.logical_and(in_line > 0, in_line < LINE - 1), 1) + count(has_below, 1) + count(has_above, 1) + count(crosses_any, PARTS))
    def pass_word(step):
        for onward in range(2):
            place = step if onward else LINE - 1 - step

            @pl.when(in_line == place)
            def _():
                if step > 0:
                    pl.semaphore_wait(word_sem.at[onward], 1)
                if step < LINE - 1:
                    pl.semaphore_signal(
                        word_sem.at[onward], inc=1, device_id=(x_next if onward else x_prev, sub), device_id_type=MESH)

    send_depth(0, False)
    pass_word(0)
    loads[2].wait()

    def without_above(hbuf, offset, sbuf, row):
        s_x, s_y, s_z = (at(sbuf, comp, 1, row) for comp in range(3))
        part_x = at(hbuf, offset, 1, row) + plus_y(s_z) + s_y
        part_y = at(hbuf, offset + 1, 1, row) - s_x - plus_x(sbuf, 2, 1, row)
        return part_x, part_y

    def first_partial(row):
        up_out[0][0, pl.ds(row, ROWS), :], up_out[0][1, pl.ds(row, ROWS), :] = without_above(field, HX, s0, row)

    row_tiles(first_partial)
    send_depth(0, True)

    def magnetic_local(hbuf, offset, sbuf, row):
        s_x0, s_y0, s_z0 = (at(sbuf, comp, 0, row) for comp in range(3))
        new_x = at(hbuf, offset, 0, row) + plus_y(s_z0) - (at(sbuf, 1, 1, row) - s_y0)
        new_y = at(hbuf, offset + 1, 0, row) + (at(sbuf, 0, 1, row) - s_x0) - plus_x(sbuf, 2, 0, row)
        new_z = at(hbuf, offset + 2, 0, row) + curl_z(sbuf, 0, row)
        new_z1 = at(hbuf, offset + 2, 1, row) + curl_z(sbuf, 1, row)
        return new_x, new_y, new_z, new_z1

    def first_local(row):
        new_x, new_y, new_z, new_z1 = magnetic_local(field, HX, s0, row)
        put(h1, 0, 0, row, new_x)
        put(h1, 1, 0, row, new_y)
        put(h1, 2, 0, row, new_z)
        put(h1, 2, 1, row, new_z1)

    row_tiles(first_local)

    def second_terms(row):
        h_x, h_y = at(h1, 0, 0, row), at(h1, 1, 0, row)
        decays, couple = rows_of(ca, 1, row), rows_of(cb, 1, row)
        part_x = decays * at(field, EX, 1, row) - MAGNETIC * (minus_y(at(h1, 2, 1, row)) + h_y)
        part_y = decays * at(field, EY, 1, row) + MAGNETIC * (h_x + minus_x(h1, 2, 1, row))
        up_out[1][0, pl.ds(row, ROWS), :] = plus_y(at(decayed, 0, 0, row)) + couple * part_y
        up_out[1][1, pl.ds(row, ROWS), :] = -couple * part_x - plus_x(decayed, 0, 0, row)
        decays, couple = rows_of(ca, 0, row), rows_of(cb, 0, row)
        down_out[1][0, pl.ds(row, ROWS), :] = couple * (
            decays * at(field, EX, 0, row) - MAGNETIC * (minus_y(at(h1, 2, 0, row)) - h_y))
        down_out[1][1, pl.ds(row, ROWS), :] = couple * (
            decays * at(field, EY, 0, row) - MAGNETIC * (h_x - minus_x(h1, 2, 0, row)))

    row_tiles(second_terms)
    send_depth(1, False)
    send_depth(1, True)

    @pl.when(jnp.logical_not(has_above))
    def _():
        def clear(row):
            for buf in down_in:
                for comp in range(buf.shape[0]):
                    buf[comp, pl.ds(row, ROWS), :] = jnp.zeros((ROWS, TY), jnp.float32)

        row_tiles(clear)

    @pl.when(jnp.logical_not(has_below))
    def _():
        def cancel(row):
            up_in[0][0, pl.ds(row, ROWS), :] = at(s0, 1, 0, row)
            up_in[0][1, pl.ds(row, ROWS), :] = -at(s0, 0, 0, row)
            for comp in range(3):
                up_in[1][comp, pl.ds(row, ROWS), :] = jnp.zeros((ROWS, TY), jnp.float32)

        row_tiles(cancel)

    def electric_xy(ebuf, hbuf, plane, row, h_x, h_y, under_x, under_y):
        h_z = at(hbuf, 2, plane, row)
        decays = rows_of(ca, plane, row)
        new_x = decays * at(ebuf, 0, plane, row) - MAGNETIC * (minus_y(h_z) - (h_y - under_y))
        new_y = decays * at(ebuf, 1, plane, row) - MAGNETIC * ((h_x - under_x) - minus_x(hbuf, 2, plane, row))
        return new_x, new_y

    def electric_z(ebuf, hbuf, plane, row, h_x):
        decays = rows_of(ca, plane, row)
        return decays * at(ebuf, 2, plane, row) - MAGNETIC * (minus_x(hbuf, 1, plane, row) - minus_y(h_x))

    for step in range(1, LINE - 1):
        pass_word(step)
    relay_depth(0, False)
    wait_depth(0)
    relay_depth(1, False)

    def first_rest(row):
        x1 = rows_of(up_out[0], 0, row) - rows_of(down_in[0], 1, row)
        y1 = rows_of(up_out[0], 1, row) + rows_of(down_in[0], 0, row)
        under_x = rows_of(up_in[0], 0, row) - at(s0, 1, 0, row)
        under_y = rows_of(up_in[0], 1, row) + at(s0, 0, 0, row)
        put(h1, 0, 1, row, x1)
        put(h1, 1, 1, row, y1)
        put(under, 0, 0, row, under_x)
        put(under, 1, 0, row, under_y)
        x0, y0 = at(h1, 0, 0, row), at(h1, 1, 0, row)
        for plane, (h_x, h_y, b_x, b_y) in enumerate(((x0, y0, under_x, under_y), (x1, y1, x0, y0))):
            new = (*electric_xy(field, h1, plane, row, h_x, h_y, b_x, b_y), electric_z(field, h1, plane, row, h_x))
            couple = rows_of(cb, plane, row)
            for comp in range(3):
                put(e1, comp, plane, row, new[comp])
                put(s1, comp, plane, row, couple * new[comp])

    row_tiles(first_rest)

    def keep(name, row, value, weights):
        w[ORDER.index(name), pl.ds(row, ROWS), :] = value * weights

    def second_local(row):
        new_x, new_y, new_z, new_z1 = magnetic_local(h1, 0, s1, row)
        put(h2, 0, 0, row, new_x)
        put(h2, 1, 0, row, new_y)
        put(h2, 2, 0, row, new_z)
        put(h2, 2, 1, row, new_z1)
        weights = weight(row)
        keep((HX, 0), row, new_x, weights)
        keep((HY, 0), row, new_y, weights)
        keep((HZ, 0), row, new_z, weights)
        keep((HZ, 1), row, new_z1, weights)
        keep((EZ, 0), row, electric_z(e1, h2, 0, row, new_x), weights)

    row_tiles(second_local)

    def slot_of(rows):
        return lax.broadcasted_iota(jnp.int32, (rows, TY), 1) // BAND

    def pack_lanes(values):
        slot = slot_of(values[0].shape[0])
        turned = [values[0]] + [pltpu.roll(values[k], BAND * k, 1) for k in (1, 2, 3)]
        low, high = turned[3], turned[0]
        for k in (2, 1, 0):
            low = jnp.where(slot == k, turned[k], low)
            high = jnp.where(slot == k, turned[k + 1], high)
        return low, high

    def unpack_lanes(low_side, high_side):
        slot = slot_of(low_side.shape[0])
        turned = []
        for k in range(4):
            mixed = jnp.where(slot == (k + 3) % 4, low_side, high_side)
            shift = (TY - BAND * (k - 1)) % TY
            turned.append(pltpu.roll(mixed, shift, 1) if shift else mixed)
        return [jnp.where(slot == 0, turned[k], jnp.where(slot == 3, turned[(k + 2) % 4], 0.0)) for k in range(4)]

    corner_rows = (0, 16, TX - 32, TX - 16)
    middle_rows = (32, 80, 128, 176)

    def middle_lanes():
        slot = slot_of(16)
        return jnp.logical_or(slot == 1, slot == 2)

    def pack_corners(index):
        values = [w[index, first : first + 16, :] for first in corner_rows]
        low, high = pack_lanes(values)
        yc_out[0, index], yc_out[1, index] = low, high
        middle = middle_lanes()
        for direction in range(2):
            xn_out[direction, index] = jnp.where(
                middle, values[2 * direction], pltpu.roll(values[2 * direction + 1], TY // 2, 1))

    def pack_middle(index):
        low, high = pack_lanes([w[index, first : first + 48, :] for first in middle_rows])
        yn_out[0, index], yn_out[1, index] = low, high

    def add_corners(index):
        added = unpack_lanes(yc_in[1, index], yc_in[0, index])
        values = []
        for first, more in zip(corner_rows, added):
            total = w[index, first : first + 16, :] + more
            w[index, first : first + 16, :] = total
            values.append(total)
        middle = middle_lanes()
        for direction in range(2):
            xc_out[direction, index] = jnp.where(
                middle, pltpu.roll(values[2 * direction + 1], TY // 2, 1), values[2 * direction])

    def add_middle(index):
        added = unpack_lanes(yn_in[1, index], yn_in[0, index])
        for first, more in zip(middle_rows, added):
            w[index, first : first + 48, :] += more

    def add_x_bands(index):
        middle = middle_lanes()
        for side_of, first in ((1, 0), (0, TX - 32)):
            plain, summed = xn_in[side_of, index], xc_in[side_of, index]
            w[index, first : first + 16, :] += jnp.where(middle, plain, summed)
            w[index, first + 16 : first + 32, :] += pltpu.roll(jnp.where(middle, summed, plain), TY // 2, 1)

    def send_group(group):
        planes_of(group, pack_corners)
        send_band(0, group)
        send_band(1, group)
        planes_of(group, pack_middle)
        send_band(2, group)

    pass_word(LINE - 1)
    send_group(0)
    relay_depth(0, True)
    relay_depth(1, True)
    wait_depth(1)

    def mix(row):
        turn_z = minus_x(under, 1, 0, row) - minus_y(at(under, 0, 0, row))
        put(mixed, 0, 0, row, MAGNETIC * rows_of(up_in[1], 2, row) * turn_z)

    row_tiles(mix)

    def second_rest(row):
        x1, y1 = without_above(h1, 0, s1, row)
        couple = MAGNETIC * rows_of(down_in[1], 2, row)
        x1 -= rows_of(down_in[1], 1, row) + couple * at(h1, 0, 1, row)
        y1 += rows_of(down_in[1], 0, row) - couple * at(h1, 1, 1, row)
        couple = MAGNETIC * rows_of(up_in[1], 2, row)
        under_x, under_y = at(under, 0, 0, row), at(under, 1, 0, row)
        under_x += rows_of(up_in[1], 0, row) - couple * under_x - plus_y(at(mixed, 0, 0, row)) - at(s1, 1, 0, row)
        under_y += rows_of(up_in[1], 1, row) - couple * under_y + plus_x(mixed, 0, 0, row) + at(s1, 0, 0, row)
        under_x = jnp.where(has_below, under_x, 0.0)
        under_y = jnp.where(has_below, under_y, 0.0)
        put(h2, 0, 1, row, x1)
        put(h2, 1, 1, row, y1)
        x0, y0 = at(h2, 0, 0, row), at(h2, 1, 0, row)
        weights = weight(row)
        keep((HX, 1), row, x1, weights)
        keep((HY, 1), row, y1, weights)
        for plane, (h_x, h_y, b_x, b_y) in enumerate(((x0, y0, under_x, under_y), (x1, y1, x0, y0))):
            new_x, new_y = electric_xy(e1, h2, plane, row, h_x, h_y, b_x, b_y)
            keep((EX, plane), row, new_x, weights)
            keep((EY, plane), row, new_y, weights)
        keep((EZ, 1), row, electric_z(e1, h2, 1, row, x1), weights)

    row_tiles(second_rest)
    send_group(1)

    for group in range(2):
        wait_band(0, group)
        planes_of(group, add_corners)
        send_band(3, group)

    for group in range(2):
        wait_band(2, group)
        planes_of(group, add_middle)
        wait_band(1, group)
        wait_band(3, group)
        planes_of(group, add_x_bands)

    for turn in range(2):
        finish_depth(turn)
    for group in range(2):
        for kind in range(4):
            for toward_next in (False, True):
                band_copy(kind, group, toward_next).wait_send()


def place(planes, out, sems):
    copies = [
        pltpu.make_async_copy(planes.at[index], out.at[0, comp, plane], sems.at[index])
        for index, (comp, plane) in enumerate(ORDER)
    ]
    for copy in copies:
        copy.start()
    for copy in copies:
        copy.wait()


def on_device(tiles, subs, seeds, material, decay, coupling):
    f32 = jnp.float32
    padded = (3, 2, PAD + TX + PAD, TY)
    planes = len(ORDER)
    narrow, wide = pltpu.VMEM((2, planes, 16, TY), f32), pltpu.VMEM((2, planes, 48, TY), f32)
    hbm = pl.BlockSpec(memory_space=pltpu.HBM)
    done = pl.pallas_call(
        functools.partial(kernel, tiles, subs),
        out_shape=jax.ShapeDtypeStruct((planes, TX, TY), f32),
        in_specs=[hbm] * 4,
        out_specs=pl.BlockSpec(memory_space=pltpu.VMEM),
        scratch_shapes=[
            pltpu.SMEM(decay.shape, f32),
            pltpu.SMEM(coupling.shape, f32),
            pltpu.VMEM((6, *padded[1:]), f32),
            pltpu.VMEM((2, TX, TY), jnp.int32),
            pltpu.VMEM((2, TX, TY), f32),
            pltpu.VMEM((2, TX, TY), f32),
            *[pltpu.VMEM(padded, f32)] * 5,
            *[pltpu.VMEM((count, 1, *padded[2:]), f32) for count in (1, 2, 1)],
            *[pltpu.VMEM((count, TX, TY), f32) for count in (2, 3)] * 4,
            *[pltpu.VMEM((count, MOST, TY), f32) for count in (2, 3)],
            narrow, wide, narrow, narrow,
            narrow, wide, narrow, narrow,
            pltpu.SemaphoreType.DMA((5,)),
            pltpu.SemaphoreType.DMA((4,)),
            pltpu.SemaphoreType.DMA((4,)),
            pltpu.SemaphoreType.DMA((2 * PARTS,)),
            pltpu.SemaphoreType.DMA((2 * PARTS,)),
            pltpu.SemaphoreType.DMA((2,)),
            pltpu.SemaphoreType.DMA((2,)),
            pltpu.SemaphoreType.DMA((16,)),
            pltpu.SemaphoreType.DMA((16,)),
            pltpu.SemaphoreType.REGULAR((2,)),
        ],
        compiler_params=pltpu.CompilerParams(
            collective_id=0, has_side_effects=True, vmem_limit_bytes=20 * 2**20),
    )(*(pltpu.with_memory_space_constraint(array, pltpu.HBM) for array in (decay, coupling, seeds, material)))
    return pl.pallas_call(
        place,
        out_shape=jax.ShapeDtypeStruct(seeds.shape, f32),
        in_specs=[pl.BlockSpec(memory_space=pltpu.VMEM)],
        out_specs=hbm,
        scratch_shapes=[pltpu.SemaphoreType.DMA((planes,))],
        compiler_params=pltpu.CompilerParams(vmem_limit_bytes=4 * 2**20),
    )(done)


def solution(mesh):
    placed = (P("tile", None, "sub", None, None), P("tile", "sub", None, None), P(), P())
    return jax.shard_map(
        functools.partial(on_device, mesh.shape["tile"], mesh.shape["sub"]),
        mesh=mesh,
        in_specs=placed,
        out_specs=P("tile", None, "sub", None, None),
        check_vma=False,
    )
```

```python
import functools
import math

import jax
import jax.numpy as jnp
from jax import lax
from jax.experimental import pallas as pl
from jax.experimental.pallas import tpu as pltpu
from jax.sharding import PartitionSpec as P

BAND = 32
MESH = pl.DeviceIdType.MESH
MAGNETIC = 0.5
TX = 256
TY = 128
PAD = 8
ROWS = 32
EX, EY, EZ, HX, HY, HZ = range(6)

EARLY = ((HX, 0), (HY, 0), (HZ, 0), (HZ, 1), (EZ, 0))
LATE = ((HX, 1), (HY, 1), (EX, 0), (EY, 0), (EX, 1), (EY, 1), (EZ, 1))
ORDER = EARLY + LATE
GROUPS = ((0, len(EARLY)), (len(EARLY), len(LATE)))

RUN = 8
PARTS = 3
LINE = 4
DIRECT = 104
PIECES = (((104, 40), (144, 40), (184, 72)), ((104, 72), (176, 40), (216, 40)))
MOST = 72


def row_tiles(body):
    def step(index, carry):
        body(pl.multiple_of(index * ROWS, ROWS))
        return carry

    lax.fori_loop(0, TX // ROWS, step, 0, unroll=2)


def planes_of(group, body):
    first, count = GROUPS[group]

    def step(index, carry):
        body(index)
        return carry

    lax.fori_loop(first, first + count, step, 0, unroll=True)


def kernel(
    tiles, subs, decay_in, coupling_in, seeds, material, w,
    decay, coupling, field, mat, ca, cb, s0, s1, h1, h2, e1, decayed, under, mixed,
    up_out0, up_out1, down_out0, down_out1, up_in0, up_in1, down_in0, down_in1, relay_in0, relay_in1,
    yc_out, yn_out, xn_out, xc_out, yc_in, yn_in, xn_in, xc_in,
    load_sem, depth_send, depth_recv, part_send, part_recv, relay_recv, relay_send, band_send, band_recv, word_sem,
):
    tile = lax.axis_index("tile")
    sub = lax.axis_index("sub")
    side = math.isqrt(tiles)
    has_below = sub > 0
    has_above = sub < subs - 1
    below = jnp.maximum(sub - 1, 0)
    above = jnp.minimum(sub + 1, subs - 1)
    x_prev = lax.rem(tile + tiles - 1, tiles)
    x_next = lax.rem(tile + 1, tiles)
    y_prev = lax.rem(tile + tiles - side, tiles)
    y_next = lax.rem(tile + side, tiles)

    loads = [
        pltpu.make_async_copy(material.at[0], mat, load_sem.at[0]),
        pltpu.make_async_copy(seeds.at[0, 0:3], field.at[0:3, :, PAD : PAD + TX], load_sem.at[1]),
        pltpu.make_async_copy(seeds.at[0, 3:6], field.at[3:6, :, PAD : PAD + TX], load_sem.at[2]),
        pltpu.make_async_copy(decay_in, decay, load_sem.at[3]),
        pltpu.make_async_copy(coupling_in, coupling, load_sem.at[4]),
    ]
    barrier = pltpu.get_barrier_semaphore()

    def greet(other_tile, other_sub):
        pl.semaphore_signal(barrier, inc=1, device_id=(other_tile, other_sub), device_id_type=MESH)

    pl.when(has_below)(lambda: greet(tile, below))
    pl.when(has_above)(lambda: greet(tile, above))
    for load in loads:
        load.start()
    in_line = lax.rem(tile, LINE)
    for other in (y_prev, y_next):
        greet(other, sub)
    pl.when(in_line > 0)(lambda: greet(x_prev, sub))
    pl.when(in_line < LINE - 1)(lambda: greet(x_next, sub))
    place_in_run = lax.rem(sub, RUN)
    start = sub - place_in_run
    run_above = start + RUN < subs
    run_below = start > 0
    crosses_up = jnp.logical_and(place_in_run == RUN - 1, run_above)
    crosses_down = jnp.logical_and(place_in_run == 0, run_below)

    def relays(upward, part):
        return jnp.logical_and(place_in_run == 2 * part + (1 if upward else 2), run_above if upward else run_below)

    last_here = start + RUN - 1
    first_above = jnp.minimum(start + RUN, subs - 1)
    last_below = jnp.maximum(start - 1, 0)

    def up_relay(part):
        return start + 2 * part + 1

    def down_relay(part):
        return start + 2 * part + 2

    for part in range(PARTS):
        pl.when(relays(True, part))(lambda: greet(tile, last_here))
        pl.when(relays(False, part))(lambda: greet(tile, start))

    lane = lax.broadcasted_iota(jnp.int32, (ROWS, TY), 1)
    not_last = lane < TY - 1
    not_first = lane > 0
    zeros_pad = jnp.zeros((PAD, TY), jnp.float32)
    for comp in range(3):
        for plane in range(2):
            for buf in (s0, s1):
                buf[comp, plane, PAD + TX : PAD + TX + PAD, :] = zeros_pad
            for buf in (h1, h2):
                buf[comp, plane, 0:PAD, :] = zeros_pad
    for buf in (decayed, mixed):
        buf[0, 0, PAD + TX : PAD + TX + PAD, :] = zeros_pad
    under[1, 0, 0:PAD, :] = zeros_pad
    up_out, down_out = (up_out0, up_out1), (down_out0, down_out1)
    up_in, down_in, relay_in = (up_in0, up_in1), (down_in0, down_in1), (relay_in0, relay_in1)

    def at(buf, comp, plane, row):
        return buf[comp, plane, pl.ds(PAD + row, ROWS), :]

    def put(buf, comp, plane, row, value):
        buf[comp, plane, pl.ds(PAD + row, ROWS), :] = value

    def plus_x(buf, comp, plane, row):
        return buf[comp, plane, pl.ds(PAD + row + 1, ROWS), :] - at(buf, comp, plane, row)

    def minus_x(buf, comp, plane, row):
        return at(buf, comp, plane, row) - buf[comp, plane, pl.ds(PAD + row - 1, ROWS), :]

    def plus_y(value):
        return jnp.where(not_last, pltpu.roll(value, TY - 1, 1), 0.0) - value

    def minus_y(value):
        return value - jnp.where(not_first, pltpu.roll(value, 1, 1), 0.0)

    def curl_z(buf, plane, row):
        return plus_x(buf, 1, plane, row) - plus_y(at(buf, 0, plane, row))

    ramp_lane = lane.astype(jnp.float32) + 0.5
    ramp_y = jnp.minimum(jnp.minimum(ramp_lane, TY - ramp_lane) * (1.0 / BAND), 1.0)
    row_iota = lax.broadcasted_iota(jnp.int32, (ROWS, TY), 0)

    def weight(row):
        position = (row_iota + row).astype(jnp.float32) + 0.5
        return jnp.minimum(jnp.minimum(position, TX - position) * (1.0 / BAND), 1.0) * ramp_y

    def rows_of(buf, index, row):
        return buf[index, pl.ds(row, ROWS), :]

    def depth_rows(turn, upward, first, count):
        return (up_out if upward else down_out)[turn].at[:, first : first + count]

    def depth_copy(turn, upward, count):
        slot = turn * 2 + int(upward)
        return pltpu.make_async_remote_copy(
            depth_rows(turn, upward, 0, count), (up_in if upward else down_in)[turn].at[:, 0:count],
            depth_send.at[slot], depth_recv.at[slot],
            device_id=(tile, above if upward else below), device_id_type=MESH)

    def part_copy(turn, upward, part):
        relay = up_relay(part) if upward else down_relay(part)
        first, count = PIECES[int(upward)][part]
        return pltpu.make_async_remote_copy(
            depth_rows(turn, upward, first, count), relay_in[turn].at[:, 0:count],
            part_send.at[turn * PARTS + part], relay_recv.at[turn],
            device_id=(tile, relay), device_id_type=MESH)

    def relay_copy(turn, upward, part):
        first, count = PIECES[int(upward)][part]
        return pltpu.make_async_remote_copy(
            relay_in[turn].at[:, 0:count], (up_in if upward else down_in)[turn].at[:, first : first + count],
            relay_send.at[turn], part_recv.at[turn * PARTS + part],
            device_id=(tile, first_above if upward else last_below), device_id_type=MESH)

    def send_depth(turn, upward):
        crosses = crosses_up if upward else crosses_down
        plain = jnp.logical_and(has_above if upward else has_below, jnp.logical_not(crosses))

        pl.when(plain)(lambda: depth_copy(turn, upward, TX).start())

        @pl.when(crosses)
        def _():
            for part in (1, 0, 2) if not upward else (1, 2, 0):
                part_copy(turn, upward, part).start()
            depth_copy(turn, upward, DIRECT).start()

    late_up = start + 2 * RUN < subs

    def relay_depth(turn, late):
        for upward in (True, False):
            if late and not upward:
                continue
            for part in range(PARTS):
                now = relays(upward, part)
                if upward:
                    now = jnp.logical_and(now, late_up if late else jnp.logical_not(late_up))

                @pl.when(now)
                def _():
                    part_copy(turn, upward, part).wait_recv()
                    relay_copy(turn, upward, part).start()

    def wait_depth(turn):
        for upward, crosses in ((True, crosses_down), (False, crosses_up)):
            plain = jnp.logical_and(has_below if upward else has_above, jnp.logical_not(crosses))
            pl.when(plain)(lambda: depth_copy(turn, upward, TX).wait_recv())

            @pl.when(crosses)
            def _():
                depth_copy(turn, upward, DIRECT).wait_recv()
                for part in range(PARTS):
                    relay_copy(turn, upward, part).wait_recv()

    def finish_depth(turn):
        for upward, crosses in ((True, crosses_up), (False, crosses_down)):
            plain = jnp.logical_and(has_above if upward else has_below, jnp.logical_not(crosses))
            pl.when(plain)(lambda: depth_copy(turn, upward, TX).wait_send())

            @pl.when(crosses)
            def _():
                for part in range(PARTS):
                    part_copy(turn, upward, part).wait_send()
                depth_copy(turn, upward, DIRECT).wait_send()

            for part in range(PARTS):
                pl.when(relays(upward, part))(lambda: relay_copy(turn, upward, part).wait_send())

    def band_copy(kind, group, toward_next):
        first, count = GROUPS[group]
        source, target = ((yc_out, yc_in), (xn_out, xn_in), (yn_out, yn_in), (xc_out, xc_in))[kind]
        direction = int(toward_next)
        if kind in (0, 2):
            other = y_next if toward_next else y_prev
        else:
            other = x_next if toward_next else x_prev
        slot = (kind * 2 + group) * 2 + direction
        part = slice(first, first + count)
        return pltpu.make_async_remote_copy(
            source.at[direction, part], target.at[direction, part],
            band_send.at[slot], band_recv.at[slot],
            device_id=(other, sub), device_id_type=MESH)

    def send_band(kind, group):
        for toward_next in (False, True):
            band_copy(kind, group, toward_next).start()

    def wait_band(kind, group):
        for toward_next in (False, True):
            band_copy(kind, group, toward_next).wait_recv()

    for number in (3, 4, 0, 1):
        loads[number].wait()
    d0, d1, d2, d3 = (decay[i] for i in range(4))
    c0, c1, c2, c3 = (coupling[i] for i in range(4))

    def scale(row):
        for plane in range(2):
            label = mat[plane, pl.ds(row, ROWS), :]
            is0, is1, is2 = label == 0, label == 1, label == 2
            couple = jnp.where(is0, c0, jnp.where(is1, c1, jnp.where(is2, c2, c3)))
            decays = jnp.where(is0, d0, jnp.where(is1, d1, jnp.where(is2, d2, d3)))
            cb[plane, pl.ds(row, ROWS), :] = couple
            ca[plane, pl.ds(row, ROWS), :] = decays
            (down_out, up_out)[plane][1][2, pl.ds(row, ROWS), :] = couple
            scaled = [couple * at(field, comp, plane, row) for comp in range(3)]
            for comp in range(3):
                put(s0, comp, plane, row, scaled[comp])
            if plane == 0:
                for comp in range(2):
                    down_out[0][comp, pl.ds(row, ROWS), :] = scaled[comp]
            else:
                put(decayed, 0, 0, row, decays * scaled[2])

    row_tiles(scale)
    count = lambda flag, number: jnp.where(flag, number, 0)
    crosses_any = jnp.logical_or(crosses_up, crosses_down)
    pl.semaphore_wait(barrier, 3 + count(jnp.logical_and(in_line > 0, in_line < LINE - 1), 1) + count(has_below, 1) + count(has_above, 1) + count(crosses_any, PARTS))
    def pass_word(step):
        for onward in range(2):
            place = step if onward else LINE - 1 - step

            @pl.when(in_line == place)
            def _():
                if step > 0:
                    pl.semaphore_wait(word_sem.at[onward], 1)
                if step < LINE - 1:
                    pl.semaphore_signal(
                        word_sem.at[onward], inc=1, device_id=(x_next if onward else x_prev, sub), device_id_type=MESH)

    send_depth(0, False)
    pass_word(0)
    loads[2].wait()

    def without_above(hbuf, offset, sbuf, row):
        s_x, s_y, s_z = (at(sbuf, comp, 1, row) for comp in range(3))
        part_x = at(hbuf, offset, 1, row) + plus_y(s_z) + s_y
        part_y = at(hbuf, offset + 1, 1, row) - s_x - plus_x(sbuf, 2, 1, row)
        return part_x, part_y

    def first_partial(row):
        up_out[0][0, pl.ds(row, ROWS), :], up_out[0][1, pl.ds(row, ROWS), :] = without_above(field, HX, s0, row)

    row_tiles(first_partial)
    send_depth(0, True)

    def magnetic_local(hbuf, offset, sbuf, row):
        s_x0, s_y0, s_z0 = (at(sbuf, comp, 0, row) for comp in range(3))
        new_x = at(hbuf, offset, 0, row) + plus_y(s_z0) - (at(sbuf, 1, 1, row) - s_y0)
        new_y = at(hbuf, offset + 1, 0, row) + (at(sbuf, 0, 1, row) - s_x0) - plus_x(sbuf, 2, 0, row)
        new_z = at(hbuf, offset + 2, 0, row) + curl_z(sbuf, 0, row)
        new_z1 = at(hbuf, offset + 2, 1, row) + curl_z(sbuf, 1, row)
        return new_x, new_y, new_z, new_z1

    def first_local(row):
        new_x, new_y, new_z, new_z1 = magnetic_local(field, HX, s0, row)
        put(h1, 0, 0, row, new_x)
        put(h1, 1, 0, row, new_y)
        put(h1, 2, 0, row, new_z)
        put(h1, 2, 1, row, new_z1)

    row_tiles(first_local)

    def second_terms(row):
        h_x, h_y = at(h1, 0, 0, row), at(h1, 1, 0, row)
        decays, couple = rows_of(ca, 1, row), rows_of(cb, 1, row)
        part_x = decays * at(field, EX, 1, row) - MAGNETIC * (minus_y(at(h1, 2, 1, row)) + h_y)
        part_y = decays * at(field, EY, 1, row) + MAGNETIC * (h_x + minus_x(h1, 2, 1, row))
        up_out[1][0, pl.ds(row, ROWS), :] = plus_y(at(decayed, 0, 0, row)) + couple * part_y
        up_out[1][1, pl.ds(row, ROWS), :] = -couple * part_x - plus_x(decayed, 0, 0, row)
        decays, couple = rows_of(ca, 0, row), rows_of(cb, 0, row)
        down_out[1][0, pl.ds(row, ROWS), :] = couple * (
            decays * at(field, EX, 0, row) - MAGNETIC * (minus_y(at(h1, 2, 0, row)) - h_y))
        down_out[1][1, pl.ds(row, ROWS), :] = couple * (
            decays * at(field, EY, 0, row) - MAGNETIC * (h_x - minus_x(h1, 2, 0, row)))

    row_tiles(second_terms)
    send_depth(1, False)
    send_depth(1, True)

    @pl.when(jnp.logical_not(has_above))
    def _():
        def clear(row):
            for buf in down_in:
                for comp in range(buf.shape[0]):
                    buf[comp, pl.ds(row, ROWS), :] = jnp.zeros((ROWS, TY), jnp.float32)

        row_tiles(clear)

    @pl.when(jnp.logical_not(has_below))
    def _():
        def cancel(row):
            up_in[0][0, pl.ds(row, ROWS), :] = at(s0, 1, 0, row)
            up_in[0][1, pl.ds(row, ROWS), :] = -at(s0, 0, 0, row)
            for comp in range(3):
                up_in[1][comp, pl.ds(row, ROWS), :] = jnp.zeros((ROWS, TY), jnp.float32)

        row_tiles(cancel)

    def electric_xy(ebuf, hbuf, plane, row, h_x, h_y, under_x, under_y):
        h_z = at(hbuf, 2, plane, row)
        decays = rows_of(ca, plane, row)
        new_x = decays * at(ebuf, 0, plane, row) - MAGNETIC * (minus_y(h_z) - (h_y - under_y))
        new_y = decays * at(ebuf, 1, plane, row) - MAGNETIC * ((h_x - under_x) - minus_x(hbuf, 2, plane, row))
        return new_x, new_y

    def electric_z(ebuf, hbuf, plane, row, h_x):
        decays = rows_of(ca, plane, row)
        return decays * at(ebuf, 2, plane, row) - MAGNETIC * (minus_x(hbuf, 1, plane, row) - minus_y(h_x))

    for step in range(1, LINE - 1):
        pass_word(step)
    relay_depth(0, False)
    wait_depth(0)
    relay_depth(1, False)

    def first_rest(row):
        x1 = rows_of(up_out[0], 0, row) - rows_of(down_in[0], 1, row)
        y1 = rows_of(up_out[0], 1, row) + rows_of(down_in[0], 0, row)
        under_x = rows_of(up_in[0], 0, row) - at(s0, 1, 0, row)
        under_y = rows_of(up_in[0], 1, row) + at(s0, 0, 0, row)
        put(h1, 0, 1, row, x1)
        put(h1, 1, 1, row, y1)
        put(under, 0, 0, row, under_x)
        put(under, 1, 0, row, under_y)
        x0, y0 = at(h1, 0, 0, row), at(h1, 1, 0, row)
        for plane, (h_x, h_y, b_x, b_y) in enumerate(((x0, y0, under_x, under_y), (x1, y1, x0, y0))):
            new = (*electric_xy(field, h1, plane, row, h_x, h_y, b_x, b_y), electric_z(field, h1, plane, row, h_x))
            couple = rows_of(cb, plane, row)
            for comp in range(3):
                put(e1, comp, plane, row, new[comp])
                put(s1, comp, plane, row, couple * new[comp])

    row_tiles(first_rest)

    def keep(name, row, value, weights):
        w[ORDER.index(name), pl.ds(row, ROWS), :] = value * weights

    def second_local(row):
        new_x, new_y, new_z, new_z1 = magnetic_local(h1, 0, s1, row)
        put(h2, 0, 0, row, new_x)
        put(h2, 1, 0, row, new_y)
        put(h2, 2, 0, row, new_z)
        put(h2, 2, 1, row, new_z1)
        weights = weight(row)
        keep((HX, 0), row, new_x, weights)
        keep((HY, 0), row, new_y, weights)
        keep((HZ, 0), row, new_z, weights)
        keep((HZ, 1), row, new_z1, weights)
        keep((EZ, 0), row, electric_z(e1, h2, 0, row, new_x), weights)

    row_tiles(second_local)

    def slot_of(rows):
        return lax.broadcasted_iota(jnp.int32, (rows, TY), 1) // BAND

    def pack_lanes(values):
        slot = slot_of(values[0].shape[0])
        turned = [values[0]] + [pltpu.roll(values[k], BAND * k, 1) for k in (1, 2, 3)]
        low, high = turned[3], turned[0]
        for k in (2, 1, 0):
            low = jnp.where(slot == k, turned[k], low)
            high = jnp.where(slot == k, turned[k + 1], high)
        return low, high

    def unpack_lanes(low_side, high_side):
        slot = slot_of(low_side.shape[0])
        turned = []
        for k in range(4):
            mixed = jnp.where(slot == (k + 3) % 4, low_side, high_side)
            shift = (TY - BAND * (k - 1)) % TY
            turned.append(pltpu.roll(mixed, shift, 1) if shift else mixed)
        return [jnp.where(slot == 0, turned[k], jnp.where(slot == 3, turned[(k + 2) % 4], 0.0)) for k in range(4)]

    corner_rows = (0, 16, TX - 32, TX - 16)
    middle_rows = (32, 80, 128, 176)

    def middle_lanes():
        slot = slot_of(16)
        return jnp.logical_or(slot == 1, slot == 2)

    def corners(index):
        return [w[index, first : first + 16, :] for first in corner_rows]

    def put_corners(index, values):
        for first, value in zip(corner_rows, values):
            w[index, first : first + 16, :] = value

    def swapped(value):
        return pltpu.roll(value, TY // 2, 1)

    def pack_x(index):
        values = corners(index)
        middle = middle_lanes()
        for direction in range(2):
            upper, lower = values[2 * direction], swapped(values[2 * direction + 1])
            xn_out[direction, index] = jnp.where(middle, upper, lower)
            xc_out[direction, index] = jnp.where(middle, lower, upper)

    def pack_middle(index):
        low, high = pack_lanes([w[index, first : first + 48, :] for first in middle_rows])
        yn_out[0, index], yn_out[1, index] = low, high

    def add_x_corners(index):
        values = corners(index)
        middle = middle_lanes()
        for side_of in range(2):
            corner, first = xc_in[side_of, index], 2 - 2 * side_of
            values[first] += jnp.where(middle, 0.0, corner)
            values[first + 1] += swapped(jnp.where(middle, corner, 0.0))
        put_corners(index, values)
        yc_out[0, index], yc_out[1, index] = pack_lanes(values)

    def add_y_corners(index):
        added = unpack_lanes(yc_in[1, index], yc_in[0, index])
        put_corners(index, [value + more for value, more in zip(corners(index), added)])

    def add_middle(index):
        added = unpack_lanes(yn_in[1, index], yn_in[0, index])
        for first, more in zip(middle_rows, added):
            w[index, first : first + 48, :] += more

    def add_x_middle(index):
        values = corners(index)
        middle = middle_lanes()
        for side_of in range(2):
            plain, first = xn_in[side_of, index], 2 - 2 * side_of
            values[first] += jnp.where(middle, plain, 0.0)
            values[first + 1] += swapped(jnp.where(middle, 0.0, plain))
        put_corners(index, values)

    def send_group(group):
        planes_of(group, pack_x)
        send_band(3, group)
        send_band(1, group)
        planes_of(group, pack_middle)
        send_band(2, group)

    pass_word(LINE - 1)
    send_group(0)
    relay_depth(0, True)
    relay_depth(1, True)
    wait_depth(1)

    def mix(row):
        turn_z = minus_x(under, 1, 0, row) - minus_y(at(under, 0, 0, row))
        put(mixed, 0, 0, row, MAGNETIC * rows_of(up_in[1], 2, row) * turn_z)

    row_tiles(mix)

    def second_rest(row):
        x1, y1 = without_above(h1, 0, s1, row)
        couple = MAGNETIC * rows_of(down_in[1], 2, row)
        x1 -= rows_of(down_in[1], 1, row) + couple * at(h1, 0, 1, row)
        y1 += rows_of(down_in[1], 0, row) - couple * at(h1, 1, 1, row)
        couple = MAGNETIC * rows_of(up_in[1], 2, row)
        under_x, under_y = at(under, 0, 0, row), at(under, 1, 0, row)
        under_x += rows_of(up_in[1], 0, row) - couple * under_x - plus_y(at(mixed, 0, 0, row)) - at(s1, 1, 0, row)
        under_y += rows_of(up_in[1], 1, row) - couple * under_y + plus_x(mixed, 0, 0, row) + at(s1, 0, 0, row)
        under_x = jnp.where(has_below, under_x, 0.0)
        under_y = jnp.where(has_below, under_y, 0.0)
        put(h2, 0, 1, row, x1)
        put(h2, 1, 1, row, y1)
        x0, y0 = at(h2, 0, 0, row), at(h2, 1, 0, row)
        weights = weight(row)
        keep((HX, 1), row, x1, weights)
        keep((HY, 1), row, y1, weights)
        for plane, (h_x, h_y, b_x, b_y) in enumerate(((x0, y0, under_x, under_y), (x1, y1, x0, y0))):
            new_x, new_y = electric_xy(e1, h2, plane, row, h_x, h_y, b_x, b_y)
            keep((EX, plane), row, new_x, weights)
            keep((EY, plane), row, new_y, weights)
        keep((EZ, 1), row, electric_z(e1, h2, 1, row, x1), weights)

    row_tiles(second_rest)
    send_group(1)

    for group in range(2):
        wait_band(3, group)
        planes_of(group, add_x_corners)
        send_band(0, group)

    for group in range(2):
        wait_band(2, group)
        planes_of(group, add_middle)
        wait_band(1, group)
        planes_of(group, add_x_middle)
        wait_band(0, group)
        planes_of(group, add_y_corners)

    for turn in range(2):
        finish_depth(turn)
    for group in range(2):
        for kind in range(4):
            for toward_next in (False, True):
                band_copy(kind, group, toward_next).wait_send()


def place(planes, out, sems):
    copies = [
        pltpu.make_async_copy(planes.at[index], out.at[0, comp, plane], sems.at[index])
        for index, (comp, plane) in enumerate(ORDER)
    ]
    for copy in copies:
        copy.start()
    for copy in copies:
        copy.wait()


def on_device(tiles, subs, seeds, material, decay, coupling):
    f32 = jnp.float32
    padded = (3, 2, PAD + TX + PAD, TY)
    planes = len(ORDER)
    narrow, wide = pltpu.VMEM((2, planes, 16, TY), f32), pltpu.VMEM((2, planes, 48, TY), f32)
    hbm = pl.BlockSpec(memory_space=pltpu.HBM)
    done = pl.pallas_call(
        functools.partial(kernel, tiles, subs),
        out_shape=jax.ShapeDtypeStruct((planes, TX, TY), f32),
        in_specs=[hbm] * 4,
        out_specs=pl.BlockSpec(memory_space=pltpu.VMEM),
        scratch_shapes=[
            pltpu.SMEM(decay.shape, f32),
            pltpu.SMEM(coupling.shape, f32),
            pltpu.VMEM((6, *padded[1:]), f32),
            pltpu.VMEM((2, TX, TY), jnp.int32),
            pltpu.VMEM((2, TX, TY), f32),
            pltpu.VMEM((2, TX, TY), f32),
            *[pltpu.VMEM(padded, f32)] * 5,
            *[pltpu.VMEM((count, 1, *padded[2:]), f32) for count in (1, 2, 1)],
            *[pltpu.VMEM((count, TX, TY), f32) for count in (2, 3)] * 4,
            *[pltpu.VMEM((count, MOST, TY), f32) for count in (2, 3)],
            narrow, wide, narrow, narrow,
            narrow, wide, narrow, narrow,
            pltpu.SemaphoreType.DMA((5,)),
            pltpu.SemaphoreType.DMA((4,)),
            pltpu.SemaphoreType.DMA((4,)),
            pltpu.SemaphoreType.DMA((2 * PARTS,)),
            pltpu.SemaphoreType.DMA((2 * PARTS,)),
            pltpu.SemaphoreType.DMA((2,)),
            pltpu.SemaphoreType.DMA((2,)),
            pltpu.SemaphoreType.DMA((16,)),
            pltpu.SemaphoreType.DMA((16,)),
            pltpu.SemaphoreType.REGULAR((2,)),
        ],
        compiler_params=pltpu.CompilerParams(
            collective_id=0, has_side_effects=True, vmem_limit_bytes=20 * 2**20),
    )(*(pltpu.with_memory_space_constraint(array, pltpu.HBM) for array in (decay, coupling, seeds, material)))
    return pl.pallas_call(
        place,
        out_shape=jax.ShapeDtypeStruct(seeds.shape, f32),
        in_specs=[pl.BlockSpec(memory_space=pltpu.VMEM)],
        out_specs=hbm,
        scratch_shapes=[pltpu.SemaphoreType.DMA((planes,))],
        compiler_params=pltpu.CompilerParams(vmem_limit_bytes=4 * 2**20),
    )(done)


def solution(mesh):
    placed = (P("tile", None, "sub", None, None), P("tile", "sub", None, None), P(), P())
    return jax.shard_map(
        functools.partial(on_device, mesh.shape["tile"], mesh.shape["sub"]),
        mesh=mesh,
        in_specs=placed,
        out_specs=P("tile", None, "sub", None, None),
        check_vma=False,
    )
```

```python
import functools
import math

import jax
import jax.numpy as jnp
from jax import lax
from jax.experimental import pallas as pl
from jax.experimental.pallas import tpu as pltpu
from jax.sharding import PartitionSpec as P

BAND = 32
MESH = pl.DeviceIdType.MESH
MAGNETIC = 0.5
TX = 256
TY = 128
PAD = 8
ROWS = 32
EX, EY, EZ, HX, HY, HZ = range(6)

EARLY = ((HX, 0), (HY, 0), (HZ, 0), (HZ, 1), (EZ, 0))
LATE = ((HX, 1), (HY, 1), (EX, 0), (EY, 0), (EX, 1), (EY, 1), (EZ, 1))
ORDER = EARLY + LATE
GROUPS = ((0, len(EARLY)), (len(EARLY), len(LATE)))

RUN = 8
PARTS = 3
LINE = 4
DIRECT = (104, 88)
PIECES = (((104, 40), (144, 40), (184, 72)), ((88, 64), (152, 56), (208, 48)))
MOST = 72


def row_tiles(body):
    def step(index, carry):
        body(pl.multiple_of(index * ROWS, ROWS))
        return carry

    lax.fori_loop(0, TX // ROWS, step, 0, unroll=2)


def planes_of(group, body):
    first, count = GROUPS[group]

    def step(index, carry):
        body(index)
        return carry

    lax.fori_loop(first, first + count, step, 0, unroll=True)


def kernel(
    tiles, subs, decay_in, coupling_in, seeds, material, w,
    decay, coupling, field, mat, ca, cb, s0, s1, h1, h2, e1, decayed, under, mixed,
    up_out0, up_out1, down_out0, down_out1, up_in0, up_in1, down_in0, down_in1, relay_in0, relay_in1,
    yc_out, yn_out, xn_out, xc_out, yc_in, yn_in, xn_in, xc_in,
    load_sem, depth_send, depth_recv, part_send, part_recv, relay_recv, relay_send, band_send, band_recv, word_sem,
):
    tile = lax.axis_index("tile")
    sub = lax.axis_index("sub")
    side = math.isqrt(tiles)
    has_below = sub > 0
    has_above = sub < subs - 1
    below = jnp.maximum(sub - 1, 0)
    above = jnp.minimum(sub + 1, subs - 1)
    x_prev = lax.rem(tile + tiles - 1, tiles)
    x_next = lax.rem(tile + 1, tiles)
    y_prev = lax.rem(tile + tiles - side, tiles)
    y_next = lax.rem(tile + side, tiles)

    loads = [
        pltpu.make_async_copy(material.at[0], mat, load_sem.at[0]),
        pltpu.make_async_copy(seeds.at[0, 0:3], field.at[0:3, :, PAD : PAD + TX], load_sem.at[1]),
        pltpu.make_async_copy(seeds.at[0, 3:6], field.at[3:6, :, PAD : PAD + TX], load_sem.at[2]),
        pltpu.make_async_copy(decay_in, decay, load_sem.at[3]),
        pltpu.make_async_copy(coupling_in, coupling, load_sem.at[4]),
    ]
    barrier = pltpu.get_barrier_semaphore()

    def greet(other_tile, other_sub):
        pl.semaphore_signal(barrier, inc=1, device_id=(other_tile, other_sub), device_id_type=MESH)

    pl.when(has_below)(lambda: greet(tile, below))
    pl.when(has_above)(lambda: greet(tile, above))
    for load in loads:
        load.start()
    in_line = lax.rem(tile, LINE)
    for other in (y_prev, y_next):
        greet(other, sub)
    pl.when(in_line > 0)(lambda: greet(x_prev, sub))
    pl.when(in_line < LINE - 1)(lambda: greet(x_next, sub))
    place_in_run = lax.rem(sub, RUN)
    start = sub - place_in_run
    run_above = start + RUN < subs
    run_below = start > 0
    crosses_up = jnp.logical_and(place_in_run == RUN - 1, run_above)
    crosses_down = jnp.logical_and(place_in_run == 0, run_below)

    def relays(upward, part):
        return jnp.logical_and(place_in_run == 2 * part + (1 if upward else 2), run_above if upward else run_below)

    last_here = start + RUN - 1
    first_above = jnp.minimum(start + RUN, subs - 1)
    last_below = jnp.maximum(start - 1, 0)

    def up_relay(part):
        return start + 2 * part + 1

    def down_relay(part):
        return start + 2 * part + 2

    for part in range(PARTS):
        pl.when(relays(True, part))(lambda: greet(tile, last_here))
        pl.when(relays(False, part))(lambda: greet(tile, start))

    lane = lax.broadcasted_iota(jnp.int32, (ROWS, TY), 1)
    not_last = lane < TY - 1
    not_first = lane > 0
    zeros_pad = jnp.zeros((PAD, TY), jnp.float32)
    for comp in range(3):
        for plane in range(2):
            for buf in (s0, s1):
                buf[comp, plane, PAD + TX : PAD + TX + PAD, :] = zeros_pad
            for buf in (h1, h2):
                buf[comp, plane, 0:PAD, :] = zeros_pad
    for buf in (decayed, mixed):
        buf[0, 0, PAD + TX : PAD + TX + PAD, :] = zeros_pad
    under[1, 0, 0:PAD, :] = zeros_pad
    up_out, down_out = (up_out0, up_out1), (down_out0, down_out1)
    up_in, down_in, relay_in = (up_in0, up_in1), (down_in0, down_in1), (relay_in0, relay_in1)

    def at(buf, comp, plane, row):
        return buf[comp, plane, pl.ds(PAD + row, ROWS), :]

    def put(buf, comp, plane, row, value):
        buf[comp, plane, pl.ds(PAD + row, ROWS), :] = value

    def plus_x(buf, comp, plane, row):
        return buf[comp, plane, pl.ds(PAD + row + 1, ROWS), :] - at(buf, comp, plane, row)

    def minus_x(buf, comp, plane, row):
        return at(buf, comp, plane, row) - buf[comp, plane, pl.ds(PAD + row - 1, ROWS), :]

    def plus_y(value):
        return jnp.where(not_last, pltpu.roll(value, TY - 1, 1), 0.0) - value

    def minus_y(value):
        return value - jnp.where(not_first, pltpu.roll(value, 1, 1), 0.0)

    def curl_z(buf, plane, row):
        return plus_x(buf, 1, plane, row) - plus_y(at(buf, 0, plane, row))

    ramp_lane = lane.astype(jnp.float32) + 0.5
    ramp_y = jnp.minimum(jnp.minimum(ramp_lane, TY - ramp_lane) * (1.0 / BAND), 1.0)
    row_iota = lax.broadcasted_iota(jnp.int32, (ROWS, TY), 0)

    def weight(row):
        position = (row_iota + row).astype(jnp.float32) + 0.5
        return jnp.minimum(jnp.minimum(position, TX - position) * (1.0 / BAND), 1.0) * ramp_y

    def rows_of(buf, index, row):
        return buf[index, pl.ds(row, ROWS), :]

    def depth_rows(turn, upward, first, count):
        return (up_out if upward else down_out)[turn].at[:, first : first + count]

    def depth_copy(turn, upward, count):
        slot = turn * 2 + int(upward)
        return pltpu.make_async_remote_copy(
            depth_rows(turn, upward, 0, count), (up_in if upward else down_in)[turn].at[:, 0:count],
            depth_send.at[slot], depth_recv.at[slot],
            device_id=(tile, above if upward else below), device_id_type=MESH)

    def part_copy(turn, upward, part):
        relay = up_relay(part) if upward else down_relay(part)
        first, count = PIECES[int(upward)][part]
        return pltpu.make_async_remote_copy(
            depth_rows(turn, upward, first, count), relay_in[turn].at[:, 0:count],
            part_send.at[turn * PARTS + part], relay_recv.at[turn],
            device_id=(tile, relay), device_id_type=MESH)

    def relay_copy(turn, upward, part):
        first, count = PIECES[int(upward)][part]
        return pltpu.make_async_remote_copy(
            relay_in[turn].at[:, 0:count], (up_in if upward else down_in)[turn].at[:, first : first + count],
            relay_send.at[turn], part_recv.at[turn * PARTS + part],
            device_id=(tile, first_above if upward else last_below), device_id_type=MESH)

    def send_depth(turn, upward):
        crosses = crosses_up if upward else crosses_down
        plain = jnp.logical_and(has_above if upward else has_below, jnp.logical_not(crosses))

        pl.when(plain)(lambda: depth_copy(turn, upward, TX).start())

        @pl.when(crosses)
        def _():
            for part in (1, 0, 2) if not upward else (1, 2, 0):
                part_copy(turn, upward, part).start()
            depth_copy(turn, upward, DIRECT[int(upward)]).start()

    late_up = start + 2 * RUN < subs

    def relay_depth(turn, late):
        for upward in (True, False):
            if late and not upward:
                continue
            for part in range(PARTS):
                now = relays(upward, part)
                if upward:
                    now = jnp.logical_and(now, late_up if late else jnp.logical_not(late_up))

                @pl.when(now)
                def _():
                    part_copy(turn, upward, part).wait_recv()
                    relay_copy(turn, upward, part).start()

    def wait_depth(turn):
        for upward, crosses in ((True, crosses_down), (False, crosses_up)):
            plain = jnp.logical_and(has_below if upward else has_above, jnp.logical_not(crosses))
            pl.when(plain)(lambda: depth_copy(turn, upward, TX).wait_recv())

            @pl.when(crosses)
            def _():
                depth_copy(turn, upward, DIRECT[int(upward)]).wait_recv()
                for part in range(PARTS):
                    relay_copy(turn, upward, part).wait_recv()

    def finish_depth(turn):
        for upward, crosses in ((True, crosses_up), (False, crosses_down)):
            plain = jnp.logical_and(has_above if upward else has_below, jnp.logical_not(crosses))
            pl.when(plain)(lambda: depth_copy(turn, upward, TX).wait_send())

            @pl.when(crosses)
            def _():
                for part in range(PARTS):
                    part_copy(turn, upward, part).wait_send()
                depth_copy(turn, upward, DIRECT[int(upward)]).wait_send()

            for part in range(PARTS):
                pl.when(relays(upward, part))(lambda: relay_copy(turn, upward, part).wait_send())

    def band_copy(kind, group, toward_next):
        first, count = GROUPS[group]
        source, target = ((yc_out, yc_in), (xn_out, xn_in), (yn_out, yn_in), (xc_out, xc_in))[kind]
        direction = int(toward_next)
        if kind in (0, 2):
            other = y_next if toward_next else y_prev
        else:
            other = x_next if toward_next else x_prev
        slot = (kind * 2 + group) * 2 + direction
        part = slice(first, first + count)
        return pltpu.make_async_remote_copy(
            source.at[direction, part], target.at[direction, part],
            band_send.at[slot], band_recv.at[slot],
            device_id=(other, sub), device_id_type=MESH)

    def send_band(kind, group):
        for toward_next in (False, True):
            band_copy(kind, group, toward_next).start()

    def wait_band(kind, group):
        for toward_next in (False, True):
            band_copy(kind, group, toward_next).wait_recv()

    for number in (3, 4, 0, 1):
        loads[number].wait()
    d0, d1, d2, d3 = (decay[i] for i in range(4))
    c0, c1, c2, c3 = (coupling[i] for i in range(4))

    def scale(row):
        for plane in range(2):
            label = mat[plane, pl.ds(row, ROWS), :]
            is0, is1, is2 = label == 0, label == 1, label == 2
            couple = jnp.where(is0, c0, jnp.where(is1, c1, jnp.where(is2, c2, c3)))
            decays = jnp.where(is0, d0, jnp.where(is1, d1, jnp.where(is2, d2, d3)))
            cb[plane, pl.ds(row, ROWS), :] = couple
            ca[plane, pl.ds(row, ROWS), :] = decays
            (down_out, up_out)[plane][1][2, pl.ds(row, ROWS), :] = couple
            scaled = [couple * at(field, comp, plane, row) for comp in range(3)]
            for comp in range(3):
                put(s0, comp, plane, row, scaled[comp])
            if plane == 0:
                for comp in range(2):
                    down_out[0][comp, pl.ds(row, ROWS), :] = scaled[comp]
            else:
                put(decayed, 0, 0, row, decays * scaled[2])

    row_tiles(scale)
    count = lambda flag, number: jnp.where(flag, number, 0)
    crosses_any = jnp.logical_or(crosses_up, crosses_down)
    pl.semaphore_wait(barrier, 3 + count(jnp.logical_and(in_line > 0, in_line < LINE - 1), 1) + count(has_below, 1) + count(has_above, 1) + count(crosses_any, PARTS))
    def pass_word(step):
        for onward in range(2):
            place = step if onward else LINE - 1 - step

            @pl.when(in_line == place)
            def _():
                if step > 0:
                    pl.semaphore_wait(word_sem.at[onward], 1)
                if step < LINE - 1:
                    pl.semaphore_signal(
                        word_sem.at[onward], inc=1, device_id=(x_next if onward else x_prev, sub), device_id_type=MESH)

    send_depth(0, False)
    pass_word(0)
    loads[2].wait()

    def without_above(hbuf, offset, sbuf, row):
        s_x, s_y, s_z = (at(sbuf, comp, 1, row) for comp in range(3))
        part_x = at(hbuf, offset, 1, row) + plus_y(s_z) + s_y
        part_y = at(hbuf, offset + 1, 1, row) - s_x - plus_x(sbuf, 2, 1, row)
        return part_x, part_y

    def first_partial(row):
        up_out[0][0, pl.ds(row, ROWS), :], up_out[0][1, pl.ds(row, ROWS), :] = without_above(field, HX, s0, row)

    row_tiles(first_partial)
    send_depth(0, True)

    def magnetic_local(hbuf, offset, sbuf, row):
        s_x0, s_y0, s_z0 = (at(sbuf, comp, 0, row) for comp in range(3))
        new_x = at(hbuf, offset, 0, row) + plus_y(s_z0) - (at(sbuf, 1, 1, row) - s_y0)
        new_y = at(hbuf, offset + 1, 0, row) + (at(sbuf, 0, 1, row) - s_x0) - plus_x(sbuf, 2, 0, row)
        new_z = at(hbuf, offset + 2, 0, row) + curl_z(sbuf, 0, row)
        new_z1 = at(hbuf, offset + 2, 1, row) + curl_z(sbuf, 1, row)
        return new_x, new_y, new_z, new_z1

    def first_local(row):
        new_x, new_y, new_z, new_z1 = magnetic_local(field, HX, s0, row)
        put(h1, 0, 0, row, new_x)
        put(h1, 1, 0, row, new_y)
        put(h1, 2, 0, row, new_z)
        put(h1, 2, 1, row, new_z1)

    row_tiles(first_local)

    def second_terms(row):
        h_x, h_y = at(h1, 0, 0, row), at(h1, 1, 0, row)
        decays, couple = rows_of(ca, 1, row), rows_of(cb, 1, row)
        part_x = decays * at(field, EX, 1, row) - MAGNETIC * (minus_y(at(h1, 2, 1, row)) + h_y)
        part_y = decays * at(field, EY, 1, row) + MAGNETIC * (h_x + minus_x(h1, 2, 1, row))
        up_out[1][0, pl.ds(row, ROWS), :] = plus_y(at(decayed, 0, 0, row)) + couple * part_y
        up_out[1][1, pl.ds(row, ROWS), :] = -couple * part_x - plus_x(decayed, 0, 0, row)
        decays, couple = rows_of(ca, 0, row), rows_of(cb, 0, row)
        down_out[1][0, pl.ds(row, ROWS), :] = couple * (
            decays * at(field, EX, 0, row) - MAGNETIC * (minus_y(at(h1, 2, 0, row)) - h_y))
        down_out[1][1, pl.ds(row, ROWS), :] = couple * (
            decays * at(field, EY, 0, row) - MAGNETIC * (h_x - minus_x(h1, 2, 0, row)))

    row_tiles(second_terms)
    send_depth(1, False)
    send_depth(1, True)

    @pl.when(jnp.logical_not(has_above))
    def _():
        def clear(row):
            for buf in down_in:
                for comp in range(buf.shape[0]):
                    buf[comp, pl.ds(row, ROWS), :] = jnp.zeros((ROWS, TY), jnp.float32)

        row_tiles(clear)

    @pl.when(jnp.logical_not(has_below))
    def _():
        def cancel(row):
            up_in[0][0, pl.ds(row, ROWS), :] = at(s0, 1, 0, row)
            up_in[0][1, pl.ds(row, ROWS), :] = -at(s0, 0, 0, row)
            for comp in range(3):
                up_in[1][comp, pl.ds(row, ROWS), :] = jnp.zeros((ROWS, TY), jnp.float32)

        row_tiles(cancel)

    def electric_xy(ebuf, hbuf, plane, row, h_x, h_y, under_x, under_y):
        h_z = at(hbuf, 2, plane, row)
        decays = rows_of(ca, plane, row)
        new_x = decays * at(ebuf, 0, plane, row) - MAGNETIC * (minus_y(h_z) - (h_y - under_y))
        new_y = decays * at(ebuf, 1, plane, row) - MAGNETIC * ((h_x - under_x) - minus_x(hbuf, 2, plane, row))
        return new_x, new_y

    def electric_z(ebuf, hbuf, plane, row, h_x):
        decays = rows_of(ca, plane, row)
        return decays * at(ebuf, 2, plane, row) - MAGNETIC * (minus_x(hbuf, 1, plane, row) - minus_y(h_x))

    for step in range(1, LINE - 1):
        pass_word(step)
    relay_depth(0, False)
    wait_depth(0)
    relay_depth(1, False)

    def first_rest(row):
        x1 = rows_of(up_out[0], 0, row) - rows_of(down_in[0], 1, row)
        y1 = rows_of(up_out[0], 1, row) + rows_of(down_in[0], 0, row)
        under_x = rows_of(up_in[0], 0, row) - at(s0, 1, 0, row)
        under_y = rows_of(up_in[0], 1, row) + at(s0, 0, 0, row)
        put(h1, 0, 1, row, x1)
        put(h1, 1, 1, row, y1)
        put(under, 0, 0, row, under_x)
        put(under, 1, 0, row, under_y)
        x0, y0 = at(h1, 0, 0, row), at(h1, 1, 0, row)
        for plane, (h_x, h_y, b_x, b_y) in enumerate(((x0, y0, under_x, under_y), (x1, y1, x0, y0))):
            new = (*electric_xy(field, h1, plane, row, h_x, h_y, b_x, b_y), electric_z(field, h1, plane, row, h_x))
            couple = rows_of(cb, plane, row)
            for comp in range(3):
                put(e1, comp, plane, row, new[comp])
                put(s1, comp, plane, row, couple * new[comp])

    row_tiles(first_rest)

    def keep(name, row, value, weights):
        w[ORDER.index(name), pl.ds(row, ROWS), :] = value * weights

    def second_local(row):
        new_x, new_y, new_z, new_z1 = magnetic_local(h1, 0, s1, row)
        put(h2, 0, 0, row, new_x)
        put(h2, 1, 0, row, new_y)
        put(h2, 2, 0, row, new_z)
        put(h2, 2, 1, row, new_z1)
        weights = weight(row)
        keep((HX, 0), row, new_x, weights)
        keep((HY, 0), row, new_y, weights)
        keep((HZ, 0), row, new_z, weights)
        keep((HZ, 1), row, new_z1, weights)
        keep((EZ, 0), row, electric_z(e1, h2, 0, row, new_x), weights)

    row_tiles(second_local)

    def slot_of(rows):
        return lax.broadcasted_iota(jnp.int32, (rows, TY), 1) // BAND

    def pack_lanes(values):
        slot = slot_of(values[0].shape[0])
        turned = [values[0]] + [pltpu.roll(values[k], BAND * k, 1) for k in (1, 2, 3)]
        low, high = turned[3], turned[0]
        for k in (2, 1, 0):
            low = jnp.where(slot == k, turned[k], low)
            high = jnp.where(slot == k, turned[k + 1], high)
        return low, high

    def unpack_lanes(low_side, high_side):
        slot = slot_of(low_side.shape[0])
        turned = []
        for k in range(4):
            mixed = jnp.where(slot == (k + 3) % 4, low_side, high_side)
            shift = (TY - BAND * (k - 1)) % TY
            turned.append(pltpu.roll(mixed, shift, 1) if shift else mixed)
        return [jnp.where(slot == 0, turned[k], jnp.where(slot == 3, turned[(k + 2) % 4], 0.0)) for k in range(4)]

    corner_rows = (0, 16, TX - 32, TX - 16)
    middle_rows = (32, 80, 128, 176)

    def middle_lanes():
        slot = slot_of(16)
        return jnp.logical_or(slot == 1, slot == 2)

    def pack_corners(index):
        values = [w[index, first : first + 16, :] for first in corner_rows]
        low, high = pack_lanes(values)
        yc_out[0, index], yc_out[1, index] = low, high
        middle = middle_lanes()
        for direction in range(2):
            xn_out[direction, index] = jnp.where(
                middle, values[2 * direction], pltpu.roll(values[2 * direction + 1], TY // 2, 1))

    def pack_middle(index):
        low, high = pack_lanes([w[index, first : first + 48, :] for first in middle_rows])
        yn_out[0, index], yn_out[1, index] = low, high

    def add_corners(index):
        added = unpack_lanes(yc_in[1, index], yc_in[0, index])
        values = []
        for first, more in zip(corner_rows, added):
            total = w[index, first : first + 16, :] + more
            w[index, first : first + 16, :] = total
            values.append(total)
        middle = middle_lanes()
        for direction in range(2):
            xc_out[direction, index] = jnp.where(
                middle, pltpu.roll(values[2 * direction + 1], TY // 2, 1), values[2 * direction])

    def add_middle(index):
        added = unpack_lanes(yn_in[1, index], yn_in[0, index])
        for first, more in zip(middle_rows, added):
            w[index, first : first + 48, :] += more

    def add_x_bands(index):
        middle = middle_lanes()
        for side_of, first in ((1, 0), (0, TX - 32)):
            plain, summed = xn_in[side_of, index], xc_in[side_of, index]
            w[index, first : first + 16, :] += jnp.where(middle, plain, summed)
            w[index, first + 16 : first + 32, :] += pltpu.roll(jnp.where(middle, summed, plain), TY // 2, 1)

    def send_group(group):
        planes_of(group, pack_corners)
        send_band(0, group)
        send_band(1, group)
        planes_of(group, pack_middle)
        send_band(2, group)

    pass_word(LINE - 1)
    send_group(0)
    relay_depth(0, True)
    relay_depth(1, True)
    wait_depth(1)

    def mix(row):
        turn_z = minus_x(under, 1, 0, row) - minus_y(at(under, 0, 0, row))
        put(mixed, 0, 0, row, MAGNETIC * rows_of(up_in[1], 2, row) * turn_z)

    row_tiles(mix)

    def second_rest(row):
        x1, y1 = without_above(h1, 0, s1, row)
        couple = MAGNETIC * rows_of(down_in[1], 2, row)
        x1 -= rows_of(down_in[1], 1, row) + couple * at(h1, 0, 1, row)
        y1 += rows_of(down_in[1], 0, row) - couple * at(h1, 1, 1, row)
        couple = MAGNETIC * rows_of(up_in[1], 2, row)
        under_x, under_y = at(under, 0, 0, row), at(under, 1, 0, row)
        under_x += rows_of(up_in[1], 0, row) - couple * under_x - plus_y(at(mixed, 0, 0, row)) - at(s1, 1, 0, row)
        under_y += rows_of(up_in[1], 1, row) - couple * under_y + plus_x(mixed, 0, 0, row) + at(s1, 0, 0, row)
        under_x = jnp.where(has_below, under_x, 0.0)
        under_y = jnp.where(has_below, under_y, 0.0)
        put(h2, 0, 1, row, x1)
        put(h2, 1, 1, row, y1)
        x0, y0 = at(h2, 0, 0, row), at(h2, 1, 0, row)
        weights = weight(row)
        keep((HX, 1), row, x1, weights)
        keep((HY, 1), row, y1, weights)
        for plane, (h_x, h_y, b_x, b_y) in enumerate(((x0, y0, under_x, under_y), (x1, y1, x0, y0))):
            new_x, new_y = electric_xy(e1, h2, plane, row, h_x, h_y, b_x, b_y)
            keep((EX, plane), row, new_x, weights)
            keep((EY, plane), row, new_y, weights)
        keep((EZ, 1), row, electric_z(e1, h2, 1, row, x1), weights)

    row_tiles(second_rest)
    send_group(1)

    for group in range(2):
        wait_band(0, group)
        planes_of(group, add_corners)
        send_band(3, group)

    for group in range(2):
        wait_band(2, group)
        planes_of(group, add_middle)
        wait_band(1, group)
        wait_band(3, group)
        planes_of(group, add_x_bands)

    for turn in range(2):
        finish_depth(turn)
    for group in range(2):
        for kind in range(4):
            for toward_next in (False, True):
                band_copy(kind, group, toward_next).wait_send()


def place(planes, out, sems):
    copies = [
        pltpu.make_async_copy(planes.at[index], out.at[0, comp, plane], sems.at[index])
        for index, (comp, plane) in enumerate(ORDER)
    ]
    for copy in copies:
        copy.start()
    for copy in copies:
        copy.wait()


def on_device(tiles, subs, seeds, material, decay, coupling):
    f32 = jnp.float32
    padded = (3, 2, PAD + TX + PAD, TY)
    planes = len(ORDER)
    narrow, wide = pltpu.VMEM((2, planes, 16, TY), f32), pltpu.VMEM((2, planes, 48, TY), f32)
    hbm = pl.BlockSpec(memory_space=pltpu.HBM)
    done = pl.pallas_call(
        functools.partial(kernel, tiles, subs),
        out_shape=jax.ShapeDtypeStruct((planes, TX, TY), f32),
        in_specs=[hbm] * 4,
        out_specs=pl.BlockSpec(memory_space=pltpu.VMEM),
        scratch_shapes=[
            pltpu.SMEM(decay.shape, f32),
            pltpu.SMEM(coupling.shape, f32),
            pltpu.VMEM((6, *padded[1:]), f32),
            pltpu.VMEM((2, TX, TY), jnp.int32),
            pltpu.VMEM((2, TX, TY), f32),
            pltpu.VMEM((2, TX, TY), f32),
            *[pltpu.VMEM(padded, f32)] * 5,
            *[pltpu.VMEM((count, 1, *padded[2:]), f32) for count in (1, 2, 1)],
            *[pltpu.VMEM((count, TX, TY), f32) for count in (2, 3)] * 4,
            *[pltpu.VMEM((count, MOST, TY), f32) for count in (2, 3)],
            narrow, wide, narrow, narrow,
            narrow, wide, narrow, narrow,
            pltpu.SemaphoreType.DMA((5,)),
            pltpu.SemaphoreType.DMA((4,)),
            pltpu.SemaphoreType.DMA((4,)),
            pltpu.SemaphoreType.DMA((2 * PARTS,)),
            pltpu.SemaphoreType.DMA((2 * PARTS,)),
            pltpu.SemaphoreType.DMA((2,)),
            pltpu.SemaphoreType.DMA((2,)),
            pltpu.SemaphoreType.DMA((16,)),
            pltpu.SemaphoreType.DMA((16,)),
            pltpu.SemaphoreType.REGULAR((2,)),
        ],
        compiler_params=pltpu.CompilerParams(
            collective_id=0, has_side_effects=True, vmem_limit_bytes=20 * 2**20),
    )(*(pltpu.with_memory_space_constraint(array, pltpu.HBM) for array in (decay, coupling, seeds, material)))
    return pl.pallas_call(
        place,
        out_shape=jax.ShapeDtypeStruct(seeds.shape, f32),
        in_specs=[pl.BlockSpec(memory_space=pltpu.VMEM)],
        out_specs=hbm,
        scratch_shapes=[pltpu.SemaphoreType.DMA((planes,))],
        compiler_params=pltpu.CompilerParams(vmem_limit_bytes=4 * 2**20),
    )(done)


def solution(mesh):
    placed = (P("tile", None, "sub", None, None), P("tile", "sub", None, None), P(), P())
    return jax.shard_map(
        functools.partial(on_device, mesh.shape["tile"], mesh.shape["sub"]),
        mesh=mesh,
        in_specs=placed,
        out_specs=P("tile", None, "sub", None, None),
        check_vma=False,
    )
```

```python
import functools
import math

import jax
import jax.numpy as jnp
from jax import lax
from jax.experimental import pallas as pl
from jax.experimental.pallas import tpu as pltpu
from jax.sharding import PartitionSpec as P

BAND = 32
MESH = pl.DeviceIdType.MESH
MAGNETIC = 0.5
TX = 256
TY = 128
PAD = 8
ROWS = 32
EX, EY, EZ, HX, HY, HZ = range(6)

EARLY = ((HX, 0), (HY, 0), (HZ, 0), (HZ, 1), (EZ, 0))
LATE = ((HX, 1), (HY, 1), (EX, 0), (EY, 0), (EX, 1), (EY, 1), (EZ, 1))
ORDER = EARLY + LATE
GROUPS = ((0, len(EARLY)), (len(EARLY), len(LATE)))
PLACE = tuple(2 * comp + plane for comp, plane in ORDER)

RUN = 8
PARTS = 3
LINE = 4
DIRECT = (104, 88)
PIECES = (((104, 40), (144, 40), (184, 72)), ((88, 64), (152, 56), (208, 48)))
MOST = 72


def row_tiles(body):
    def step(index, carry):
        body(pl.multiple_of(index * ROWS, ROWS))
        return carry

    lax.fori_loop(0, TX // ROWS, step, 0, unroll=2)


def planes_of(group, body):
    first, count = GROUPS[group]
    for index in range(first, first + count):
        body(index)


def kernel(
    tiles, subs, decay_in, coupling_in, seeds, material, w,
    decay, coupling, field, mat, ca, cb, s0, s1, h1, h2, e1, decayed, under, mixed,
    up_out0, up_out1, down_out0, down_out1, up_in0, up_in1, down_in0, down_in1, relay_in0, relay_in1,
    yc_out, yn_out, xn_out, xc_out, yc_in, yn_in, xn_in, xc_in,
    load_sem, depth_send, depth_recv, part_send, part_recv, relay_recv, relay_send, band_send, band_recv, word_sem,
):
    tile = lax.axis_index("tile")
    sub = lax.axis_index("sub")
    side = math.isqrt(tiles)
    has_below = sub > 0
    has_above = sub < subs - 1
    below = jnp.maximum(sub - 1, 0)
    above = jnp.minimum(sub + 1, subs - 1)
    x_prev = lax.rem(tile + tiles - 1, tiles)
    x_next = lax.rem(tile + 1, tiles)
    y_prev = lax.rem(tile + tiles - side, tiles)
    y_next = lax.rem(tile + side, tiles)

    loads = [
        pltpu.make_async_copy(material.at[0], mat, load_sem.at[0]),
        pltpu.make_async_copy(seeds.at[0, 0:3], field.at[0:3, :, PAD : PAD + TX], load_sem.at[1]),
        pltpu.make_async_copy(seeds.at[0, 3:6], field.at[3:6, :, PAD : PAD + TX], load_sem.at[2]),
        pltpu.make_async_copy(decay_in, decay, load_sem.at[3]),
        pltpu.make_async_copy(coupling_in, coupling, load_sem.at[4]),
    ]
    barrier = pltpu.get_barrier_semaphore()

    def greet(other_tile, other_sub):
        pl.semaphore_signal(barrier, inc=1, device_id=(other_tile, other_sub), device_id_type=MESH)

    pl.when(has_below)(lambda: greet(tile, below))
    pl.when(has_above)(lambda: greet(tile, above))
    for load in loads:
        load.start()
    in_line = lax.rem(tile, LINE)
    for other in (y_prev, y_next):
        greet(other, sub)
    pl.when(in_line > 0)(lambda: greet(x_prev, sub))
    pl.when(in_line < LINE - 1)(lambda: greet(x_next, sub))
    place_in_run = lax.rem(sub, RUN)
    start = sub - place_in_run
    run_above = start + RUN < subs
    run_below = start > 0
    crosses_up = jnp.logical_and(place_in_run == RUN - 1, run_above)
    crosses_down = jnp.logical_and(place_in_run == 0, run_below)

    def relays(upward, part):
        return jnp.logical_and(place_in_run == 2 * part + (1 if upward else 2), run_above if upward else run_below)

    last_here = start + RUN - 1
    first_above = jnp.minimum(start + RUN, subs - 1)
    last_below = jnp.maximum(start - 1, 0)

    def up_relay(part):
        return start + 2 * part + 1

    def down_relay(part):
        return start + 2 * part + 2

    for part in range(PARTS):
        pl.when(relays(True, part))(lambda: greet(tile, last_here))
        pl.when(relays(False, part))(lambda: greet(tile, start))

    lane = lax.broadcasted_iota(jnp.int32, (ROWS, TY), 1)
    not_last = lane < TY - 1
    not_first = lane > 0
    zeros_pad = jnp.zeros((PAD, TY), jnp.float32)
    for comp in range(3):
        for plane in range(2):
            for buf in (s0, s1):
                buf[comp, plane, PAD + TX : PAD + TX + PAD, :] = zeros_pad
            for buf in (h1, h2):
                buf[comp, plane, 0:PAD, :] = zeros_pad
    for buf in (decayed, mixed):
        buf[0, 0, PAD + TX : PAD + TX + PAD, :] = zeros_pad
    under[1, 0, 0:PAD, :] = zeros_pad
    up_out, down_out = (up_out0, up_out1), (down_out0, down_out1)
    up_in, down_in, relay_in = (up_in0, up_in1), (down_in0, down_in1), (relay_in0, relay_in1)

    def at(buf, comp, plane, row):
        return buf[comp, plane, pl.ds(PAD + row, ROWS), :]

    def put(buf, comp, plane, row, value):
        buf[comp, plane, pl.ds(PAD + row, ROWS), :] = value

    def plus_x(buf, comp, plane, row):
        return buf[comp, plane, pl.ds(PAD + row + 1, ROWS), :] - at(buf, comp, plane, row)

    def minus_x(buf, comp, plane, row):
        return at(buf, comp, plane, row) - buf[comp, plane, pl.ds(PAD + row - 1, ROWS), :]

    def plus_y(value):
        return jnp.where(not_last, pltpu.roll(value, TY - 1, 1), 0.0) - value

    def minus_y(value):
        return value - jnp.where(not_first, pltpu.roll(value, 1, 1), 0.0)

    def curl_z(buf, plane, row):
        return plus_x(buf, 1, plane, row) - plus_y(at(buf, 0, plane, row))

    ramp_lane = lane.astype(jnp.float32) + 0.5
    ramp_y = jnp.minimum(jnp.minimum(ramp_lane, TY - ramp_lane) * (1.0 / BAND), 1.0)
    row_iota = lax.broadcasted_iota(jnp.int32, (ROWS, TY), 0)

    def weight(row):
        position = (row_iota + row).astype(jnp.float32) + 0.5
        return jnp.minimum(jnp.minimum(position, TX - position) * (1.0 / BAND), 1.0) * ramp_y

    def rows_of(buf, index, row):
        return buf[index, pl.ds(row, ROWS), :]

    def depth_rows(turn, upward, first, count):
        return (up_out if upward else down_out)[turn].at[:, first : first + count]

    def depth_copy(turn, upward, count):
        slot = turn * 2 + int(upward)
        return pltpu.make_async_remote_copy(
            depth_rows(turn, upward, 0, count), (up_in if upward else down_in)[turn].at[:, 0:count],
            depth_send.at[slot], depth_recv.at[slot],
            device_id=(tile, above if upward else below), device_id_type=MESH)

    def part_copy(turn, upward, part):
        relay = up_relay(part) if upward else down_relay(part)
        first, count = PIECES[int(upward)][part]
        return pltpu.make_async_remote_copy(
            depth_rows(turn, upward, first, count), relay_in[turn].at[:, 0:count],
            part_send.at[turn * PARTS + part], relay_recv.at[turn],
            device_id=(tile, relay), device_id_type=MESH)

    def relay_copy(turn, upward, part):
        first, count = PIECES[int(upward)][part]
        return pltpu.make_async_remote_copy(
            relay_in[turn].at[:, 0:count], (up_in if upward else down_in)[turn].at[:, first : first + count],
            relay_send.at[turn], part_recv.at[turn * PARTS + part],
            device_id=(tile, first_above if upward else last_below), device_id_type=MESH)

    def send_depth(turn, upward):
        crosses = crosses_up if upward else crosses_down
        plain = jnp.logical_and(has_above if upward else has_below, jnp.logical_not(crosses))

        pl.when(plain)(lambda: depth_copy(turn, upward, TX).start())

        @pl.when(crosses)
        def _():
            for part in (1, 0, 2) if not upward else (1, 2, 0):
                part_copy(turn, upward, part).start()
            depth_copy(turn, upward, DIRECT[int(upward)]).start()

    late_up = start + 2 * RUN < subs

    def relay_depth(turn, late):
        for upward in (True, False):
            if late and not upward:
                continue
            for part in range(PARTS):
                now = relays(upward, part)
                if upward:
                    now = jnp.logical_and(now, late_up if late else jnp.logical_not(late_up))

                @pl.when(now)
                def _():
                    part_copy(turn, upward, part).wait_recv()
                    relay_copy(turn, upward, part).start()

    def wait_depth(turn):
        for upward, crosses in ((True, crosses_down), (False, crosses_up)):
            plain = jnp.logical_and(has_below if upward else has_above, jnp.logical_not(crosses))
            pl.when(plain)(lambda: depth_copy(turn, upward, TX).wait_recv())

            @pl.when(crosses)
            def _():
                depth_copy(turn, upward, DIRECT[int(upward)]).wait_recv()
                for part in range(PARTS):
                    relay_copy(turn, upward, part).wait_recv()

    def finish_depth(turn):
        for upward, crosses in ((True, crosses_up), (False, crosses_down)):
            plain = jnp.logical_and(has_above if upward else has_below, jnp.logical_not(crosses))
            pl.when(plain)(lambda: depth_copy(turn, upward, TX).wait_send())

            @pl.when(crosses)
            def _():
                for part in range(PARTS):
                    part_copy(turn, upward, part).wait_send()
                depth_copy(turn, upward, DIRECT[int(upward)]).wait_send()

            for part in range(PARTS):
                pl.when(relays(upward, part))(lambda: relay_copy(turn, upward, part).wait_send())

    def band_copy(kind, group, toward_next):
        first, count = GROUPS[group]
        source, target = ((yc_out, yc_in), (xn_out, xn_in), (yn_out, yn_in), (xc_out, xc_in))[kind]
        direction = int(toward_next)
        if kind in (0, 2):
            other = y_next if toward_next else y_prev
        else:
            other = x_next if toward_next else x_prev
        slot = (kind * 2 + group) * 2 + direction
        part = slice(first, first + count)
        return pltpu.make_async_remote_copy(
            source.at[direction, part], target.at[direction, part],
            band_send.at[slot], band_recv.at[slot],
            device_id=(other, sub), device_id_type=MESH)

    def send_band(kind, group):
        for toward_next in (False, True):
            band_copy(kind, group, toward_next).start()

    def wait_band(kind, group):
        for toward_next in (False, True):
            band_copy(kind, group, toward_next).wait_recv()

    for number in (3, 4, 0, 1):
        loads[number].wait()
    d0, d1, d2, d3 = (decay[i] for i in range(4))
    c0, c1, c2, c3 = (coupling[i] for i in range(4))

    def scale(row):
        for plane in range(2):
            label = mat[plane, pl.ds(row, ROWS), :]
            is0, is1, is2 = label == 0, label == 1, label == 2
            couple = jnp.where(is0, c0, jnp.where(is1, c1, jnp.where(is2, c2, c3)))
            decays = jnp.where(is0, d0, jnp.where(is1, d1, jnp.where(is2, d2, d3)))
            cb[plane, pl.ds(row, ROWS), :] = couple
            ca[plane, pl.ds(row, ROWS), :] = decays
            (down_out, up_out)[plane][1][2, pl.ds(row, ROWS), :] = couple
            scaled = [couple * at(field, comp, plane, row) for comp in range(3)]
            for comp in range(3):
                put(s0, comp, plane, row, scaled[comp])
            if plane == 0:
                for comp in range(2):
                    down_out[0][comp, pl.ds(row, ROWS), :] = scaled[comp]
            else:
                put(decayed, 0, 0, row, decays * scaled[2])

    row_tiles(scale)
    count = lambda flag, number: jnp.where(flag, number, 0)
    crosses_any = jnp.logical_or(crosses_up, crosses_down)
    pl.semaphore_wait(barrier, 3 + count(jnp.logical_and(in_line > 0, in_line < LINE - 1), 1) + count(has_below, 1) + count(has_above, 1) + count(crosses_any, PARTS))
    def pass_word(step):
        for onward in range(2):
            place = step if onward else LINE - 1 - step

            @pl.when(in_line == place)
            def _():
                if step > 0:
                    pl.semaphore_wait(word_sem.at[onward], 1)
                if step < LINE - 1:
                    pl.semaphore_signal(
                        word_sem.at[onward], inc=1, device_id=(x_next if onward else x_prev, sub), device_id_type=MESH)

    send_depth(0, False)
    pass_word(0)
    loads[2].wait()

    def without_above(hbuf, offset, sbuf, row):
        s_x, s_y, s_z = (at(sbuf, comp, 1, row) for comp in range(3))
        part_x = at(hbuf, offset, 1, row) + plus_y(s_z) + s_y
        part_y = at(hbuf, offset + 1, 1, row) - s_x - plus_x(sbuf, 2, 1, row)
        return part_x, part_y

    def first_partial(row):
        up_out[0][0, pl.ds(row, ROWS), :], up_out[0][1, pl.ds(row, ROWS), :] = without_above(field, HX, s0, row)

    row_tiles(first_partial)
    send_depth(0, True)

    def magnetic_local(hbuf, offset, sbuf, row):
        s_x0, s_y0, s_z0 = (at(sbuf, comp, 0, row) for comp in range(3))
        new_x = at(hbuf, offset, 0, row) + plus_y(s_z0) - (at(sbuf, 1, 1, row) - s_y0)
        new_y = at(hbuf, offset + 1, 0, row) + (at(sbuf, 0, 1, row) - s_x0) - plus_x(sbuf, 2, 0, row)
        new_z = at(hbuf, offset + 2, 0, row) + curl_z(sbuf, 0, row)
        new_z1 = at(hbuf, offset + 2, 1, row) + curl_z(sbuf, 1, row)
        return new_x, new_y, new_z, new_z1

    def first_local(row):
        new_x, new_y, new_z, new_z1 = magnetic_local(field, HX, s0, row)
        put(h1, 0, 0, row, new_x)
        put(h1, 1, 0, row, new_y)
        put(h1, 2, 0, row, new_z)
        put(h1, 2, 1, row, new_z1)

    row_tiles(first_local)

    def second_terms(row):
        h_x, h_y = at(h1, 0, 0, row), at(h1, 1, 0, row)
        decays, couple = rows_of(ca, 1, row), rows_of(cb, 1, row)
        part_x = decays * at(field, EX, 1, row) - MAGNETIC * (minus_y(at(h1, 2, 1, row)) + h_y)
        part_y = decays * at(field, EY, 1, row) + MAGNETIC * (h_x + minus_x(h1, 2, 1, row))
        up_out[1][0, pl.ds(row, ROWS), :] = plus_y(at(decayed, 0, 0, row)) + couple * part_y
        up_out[1][1, pl.ds(row, ROWS), :] = -couple * part_x - plus_x(decayed, 0, 0, row)
        decays, couple = rows_of(ca, 0, row), rows_of(cb, 0, row)
        down_out[1][0, pl.ds(row, ROWS), :] = couple * (
            decays * at(field, EX, 0, row) - MAGNETIC * (minus_y(at(h1, 2, 0, row)) - h_y))
        down_out[1][1, pl.ds(row, ROWS), :] = couple * (
            decays * at(field, EY, 0, row) - MAGNETIC * (h_x - minus_x(h1, 2, 0, row)))

    row_tiles(second_terms)
    send_depth(1, False)
    send_depth(1, True)

    @pl.when(jnp.logical_not(has_above))
    def _():
        def clear(row):
            for buf in down_in:
                for comp in range(buf.shape[0]):
                    buf[comp, pl.ds(row, ROWS), :] = jnp.zeros((ROWS, TY), jnp.float32)

        row_tiles(clear)

    @pl.when(jnp.logical_not(has_below))
    def _():
        def cancel(row):
            up_in[0][0, pl.ds(row, ROWS), :] = at(s0, 1, 0, row)
            up_in[0][1, pl.ds(row, ROWS), :] = -at(s0, 0, 0, row)
            for comp in range(3):
                up_in[1][comp, pl.ds(row, ROWS), :] = jnp.zeros((ROWS, TY), jnp.float32)

        row_tiles(cancel)

    def electric_xy(ebuf, hbuf, plane, row, h_x, h_y, under_x, under_y):
        h_z = at(hbuf, 2, plane, row)
        decays = rows_of(ca, plane, row)
        new_x = decays * at(ebuf, 0, plane, row) - MAGNETIC * (minus_y(h_z) - (h_y - under_y))
        new_y = decays * at(ebuf, 1, plane, row) - MAGNETIC * ((h_x - under_x) - minus_x(hbuf, 2, plane, row))
        return new_x, new_y

    def electric_z(ebuf, hbuf, plane, row, h_x):
        decays = rows_of(ca, plane, row)
        return decays * at(ebuf, 2, plane, row) - MAGNETIC * (minus_x(hbuf, 1, plane, row) - minus_y(h_x))

    for step in range(1, LINE - 1):
        pass_word(step)
    relay_depth(0, False)
    wait_depth(0)
    relay_depth(1, False)

    def first_rest(row):
        x1 = rows_of(up_out[0], 0, row) - rows_of(down_in[0], 1, row)
        y1 = rows_of(up_out[0], 1, row) + rows_of(down_in[0], 0, row)
        under_x = rows_of(up_in[0], 0, row) - at(s0, 1, 0, row)
        under_y = rows_of(up_in[0], 1, row) + at(s0, 0, 0, row)
        put(h1, 0, 1, row, x1)
        put(h1, 1, 1, row, y1)
        put(under, 0, 0, row, under_x)
        put(under, 1, 0, row, under_y)
        x0, y0 = at(h1, 0, 0, row), at(h1, 1, 0, row)
        for plane, (h_x, h_y, b_x, b_y) in enumerate(((x0, y0, under_x, under_y), (x1, y1, x0, y0))):
            new = (*electric_xy(field, h1, plane, row, h_x, h_y, b_x, b_y), electric_z(field, h1, plane, row, h_x))
            couple = rows_of(cb, plane, row)
            for comp in range(3):
                put(e1, comp, plane, row, new[comp])
                put(s1, comp, plane, row, couple * new[comp])

    row_tiles(first_rest)

    def keep(name, row, value, weights):
        w[2 * name[0] + name[1], pl.ds(row, ROWS), :] = value * weights

    def second_local(row):
        new_x, new_y, new_z, new_z1 = magnetic_local(h1, 0, s1, row)
        put(h2, 0, 0, row, new_x)
        put(h2, 1, 0, row, new_y)
        put(h2, 2, 0, row, new_z)
        put(h2, 2, 1, row, new_z1)
        weights = weight(row)
        keep((HX, 0), row, new_x, weights)
        keep((HY, 0), row, new_y, weights)
        keep((HZ, 0), row, new_z, weights)
        keep((HZ, 1), row, new_z1, weights)
        keep((EZ, 0), row, electric_z(e1, h2, 0, row, new_x), weights)

    row_tiles(second_local)

    def slot_of(rows):
        return lax.broadcasted_iota(jnp.int32, (rows, TY), 1) // BAND

    def pack_lanes(values):
        slot = slot_of(values[0].shape[0])
        turned = [values[0]] + [pltpu.roll(values[k], BAND * k, 1) for k in (1, 2, 3)]
        low, high = turned[3], turned[0]
        for k in (2, 1, 0):
            low = jnp.where(slot == k, turned[k], low)
            high = jnp.where(slot == k, turned[k + 1], high)
        return low, high

    def unpack_lanes(low_side, high_side):
        slot = slot_of(low_side.shape[0])
        turned = []
        for k in range(4):
            mixed = jnp.where(slot == (k + 3) % 4, low_side, high_side)
            shift = (TY - BAND * (k - 1)) % TY
            turned.append(pltpu.roll(mixed, shift, 1) if shift else mixed)
        return [jnp.where(slot == 0, turned[k], jnp.where(slot == 3, turned[(k + 2) % 4], 0.0)) for k in range(4)]

    corner_rows = (0, 16, TX - 32, TX - 16)
    middle_rows = (32, 80, 128, 176)

    def middle_lanes():
        slot = slot_of(16)
        return jnp.logical_or(slot == 1, slot == 2)

    def pack_corners(index):
        values = [w[PLACE[index], first : first + 16, :] for first in corner_rows]
        low, high = pack_lanes(values)
        yc_out[0, index], yc_out[1, index] = low, high
        middle = middle_lanes()
        for direction in range(2):
            xn_out[direction, index] = jnp.where(
                middle, values[2 * direction], pltpu.roll(values[2 * direction + 1], TY // 2, 1))

    def pack_middle(index):
        low, high = pack_lanes([w[PLACE[index], first : first + 48, :] for first in middle_rows])
        yn_out[0, index], yn_out[1, index] = low, high

    def add_corners(index):
        added = unpack_lanes(yc_in[1, index], yc_in[0, index])
        values = []
        for first, more in zip(corner_rows, added):
            total = w[PLACE[index], first : first + 16, :] + more
            w[PLACE[index], first : first + 16, :] = total
            values.append(total)
        middle = middle_lanes()
        for direction in range(2):
            xc_out[direction, index] = jnp.where(
                middle, pltpu.roll(values[2 * direction + 1], TY // 2, 1), values[2 * direction])

    def add_middle(index):
        added = unpack_lanes(yn_in[1, index], yn_in[0, index])
        for first, more in zip(middle_rows, added):
            w[PLACE[index], first : first + 48, :] += more

    def add_x_bands(index):
        middle = middle_lanes()
        for side_of, first in ((1, 0), (0, TX - 32)):
            plain, summed = xn_in[side_of, index], xc_in[side_of, index]
            w[PLACE[index], first : first + 16, :] += jnp.where(middle, plain, summed)
            w[PLACE[index], first + 16 : first + 32, :] += pltpu.roll(jnp.where(middle, summed, plain), TY // 2, 1)

    def send_group(group):
        planes_of(group, pack_corners)
        send_band(0, group)
        send_band(1, group)
        planes_of(group, pack_middle)
        send_band(2, group)

    pass_word(LINE - 1)
    send_group(0)
    relay_depth(0, True)
    relay_depth(1, True)
    wait_depth(1)

    def mix(row):
        turn_z = minus_x(under, 1, 0, row) - minus_y(at(under, 0, 0, row))
        put(mixed, 0, 0, row, MAGNETIC * rows_of(up_in[1], 2, row) * turn_z)

    row_tiles(mix)

    def second_rest(row):
        x1, y1 = without_above(h1, 0, s1, row)
        couple = MAGNETIC * rows_of(down_in[1], 2, row)
        x1 -= rows_of(down_in[1], 1, row) + couple * at(h1, 0, 1, row)
        y1 += rows_of(down_in[1], 0, row) - couple * at(h1, 1, 1, row)
        couple = MAGNETIC * rows_of(up_in[1], 2, row)
        under_x, under_y = at(under, 0, 0, row), at(under, 1, 0, row)
        under_x += rows_of(up_in[1], 0, row) - couple * under_x - plus_y(at(mixed, 0, 0, row)) - at(s1, 1, 0, row)
        under_y += rows_of(up_in[1], 1, row) - couple * under_y + plus_x(mixed, 0, 0, row) + at(s1, 0, 0, row)
        under_x = jnp.where(has_below, under_x, 0.0)
        under_y = jnp.where(has_below, under_y, 0.0)
        put(h2, 0, 1, row, x1)
        put(h2, 1, 1, row, y1)
        x0, y0 = at(h2, 0, 0, row), at(h2, 1, 0, row)
        weights = weight(row)
        keep((HX, 1), row, x1, weights)
        keep((HY, 1), row, y1, weights)
        for plane, (h_x, h_y, b_x, b_y) in enumerate(((x0, y0, under_x, under_y), (x1, y1, x0, y0))):
            new_x, new_y = electric_xy(e1, h2, plane, row, h_x, h_y, b_x, b_y)
            keep((EX, plane), row, new_x, weights)
            keep((EY, plane), row, new_y, weights)
        keep((EZ, 1), row, electric_z(e1, h2, 1, row, x1), weights)

    row_tiles(second_rest)
    send_group(1)

    for group in range(2):
        wait_band(0, group)
        planes_of(group, add_corners)
        send_band(3, group)

    for group in range(2):
        wait_band(2, group)
        planes_of(group, add_middle)
        wait_band(1, group)
        wait_band(3, group)
        planes_of(group, add_x_bands)

    for turn in range(2):
        finish_depth(turn)
    for group in range(2):
        for kind in range(4):
            for toward_next in (False, True):
                band_copy(kind, group, toward_next).wait_send()


def on_device(tiles, subs, seeds, material, decay, coupling):
    f32 = jnp.float32
    padded = (3, 2, PAD + TX + PAD, TY)
    planes = len(ORDER)
    narrow, wide = pltpu.VMEM((2, planes, 16, TY), f32), pltpu.VMEM((2, planes, 48, TY), f32)
    hbm = pl.BlockSpec(memory_space=pltpu.HBM)
    done = pl.pallas_call(
        functools.partial(kernel, tiles, subs),
        out_shape=jax.ShapeDtypeStruct((planes, TX, TY), f32),
        in_specs=[hbm] * 4,
        out_specs=pl.BlockSpec(memory_space=pltpu.VMEM),
        scratch_shapes=[
            pltpu.SMEM(decay.shape, f32),
            pltpu.SMEM(coupling.shape, f32),
            pltpu.VMEM((6, *padded[1:]), f32),
            pltpu.VMEM((2, TX, TY), jnp.int32),
            pltpu.VMEM((2, TX, TY), f32),
            pltpu.VMEM((2, TX, TY), f32),
            *[pltpu.VMEM(padded, f32)] * 5,
            *[pltpu.VMEM((count, 1, *padded[2:]), f32) for count in (1, 2, 1)],
            *[pltpu.VMEM((count, TX, TY), f32) for count in (2, 3)] * 4,
            *[pltpu.VMEM((count, MOST, TY), f32) for count in (2, 3)],
            narrow, wide, narrow, narrow,
            narrow, wide, narrow, narrow,
            pltpu.SemaphoreType.DMA((5,)),
            pltpu.SemaphoreType.DMA((4,)),
            pltpu.SemaphoreType.DMA((4,)),
            pltpu.SemaphoreType.DMA((2 * PARTS,)),
            pltpu.SemaphoreType.DMA((2 * PARTS,)),
            pltpu.SemaphoreType.DMA((2,)),
            pltpu.SemaphoreType.DMA((2,)),
            pltpu.SemaphoreType.DMA((16,)),
            pltpu.SemaphoreType.DMA((16,)),
            pltpu.SemaphoreType.REGULAR((2,)),
        ],
        compiler_params=pltpu.CompilerParams(
            collective_id=0, has_side_effects=True, vmem_limit_bytes=20 * 2**20),
    )(*(pltpu.with_memory_space_constraint(array, pltpu.HBM) for array in (decay, coupling, seeds, material)))
    return done.reshape(seeds.shape)


def solution(mesh):
    placed = (P("tile", None, "sub", None, None), P("tile", "sub", None, None), P(), P())
    return jax.shard_map(
        functools.partial(on_device, mesh.shape["tile"], mesh.shape["sub"]),
        mesh=mesh,
        in_specs=placed,
        out_specs=P("tile", None, "sub", None, None),
        check_vma=False,
    )
```

```python
import functools
import math

import jax
import jax.numpy as jnp
from jax import lax
from jax.experimental import pallas as pl
from jax.experimental.pallas import tpu as pltpu
from jax.sharding import PartitionSpec as P

BAND = 32
MESH = pl.DeviceIdType.MESH
MAGNETIC = 0.5
TX = 256
TY = 128
PAD = 8
ROWS = 32
EX, EY, EZ, HX, HY, HZ = range(6)

EARLY = ((HX, 0), (HY, 0), (HZ, 0), (HZ, 1), (EZ, 0))
LATE = ((HX, 1), (HY, 1), (EX, 0), (EY, 0), (EX, 1), (EY, 1), (EZ, 1))
ORDER = EARLY + LATE
GROUPS = ((0, len(EARLY)), (len(EARLY), len(LATE)))
PLACE = tuple(2 * comp + plane for comp, plane in ORDER)

RUN = 8
PARTS = 3
LINE = 4
DIRECT = (104, 88)
PIECES = (((104, 40), (144, 40), (184, 72)), ((88, 64), (152, 56), (208, 48)))
MOST = 72


def row_tiles(body):
    def step(index, carry):
        body(pl.multiple_of(index * ROWS, ROWS))
        return carry

    lax.fori_loop(0, TX // ROWS, step, 0, unroll=4)


def planes_of(group, body):
    first, count = GROUPS[group]
    for index in range(first, first + count):
        body(index)


def kernel(
    tiles, subs, decay_in, coupling_in, seeds, material, w,
    decay, coupling, field, mat, ca, cb, s0, s1, h1, h2, e1, decayed, under, mixed,
    up_out0, up_out1, down_out0, down_out1, up_in0, up_in1, down_in0, down_in1, relay_in0, relay_in1,
    yc_out, yn_out, xn_out, xc_out, yc_in, yn_in, xn_in, xc_in,
    load_sem, depth_send, depth_recv, part_send, part_recv, relay_recv, relay_send, band_send, band_recv, word_sem,
):
    tile = lax.axis_index("tile")
    sub = lax.axis_index("sub")
    side = math.isqrt(tiles)
    has_below = sub > 0
    has_above = sub < subs - 1
    below = jnp.maximum(sub - 1, 0)
    above = jnp.minimum(sub + 1, subs - 1)
    x_prev = lax.rem(tile + tiles - 1, tiles)
    x_next = lax.rem(tile + 1, tiles)
    y_prev = lax.rem(tile + tiles - side, tiles)
    y_next = lax.rem(tile + side, tiles)

    loads = [
        pltpu.make_async_copy(material.at[0], mat, load_sem.at[0]),
        pltpu.make_async_copy(seeds.at[0, 0:3], field.at[0:3, :, PAD : PAD + TX], load_sem.at[1]),
        pltpu.make_async_copy(seeds.at[0, 3:6], field.at[3:6, :, PAD : PAD + TX], load_sem.at[2]),
        pltpu.make_async_copy(decay_in, decay, load_sem.at[3]),
        pltpu.make_async_copy(coupling_in, coupling, load_sem.at[4]),
    ]
    barrier = pltpu.get_barrier_semaphore()

    def greet(other_tile, other_sub):
        pl.semaphore_signal(barrier, inc=1, device_id=(other_tile, other_sub), device_id_type=MESH)

    pl.when(has_below)(lambda: greet(tile, below))
    pl.when(has_above)(lambda: greet(tile, above))
    for load in loads:
        load.start()
    in_line = lax.rem(tile, LINE)
    for other in (y_prev, y_next):
        greet(other, sub)
    pl.when(in_line > 0)(lambda: greet(x_prev, sub))
    pl.when(in_line < LINE - 1)(lambda: greet(x_next, sub))
    place_in_run = lax.rem(sub, RUN)
    start = sub - place_in_run
    run_above = start + RUN < subs
    run_below = start > 0
    crosses_up = jnp.logical_and(place_in_run == RUN - 1, run_above)
    crosses_down = jnp.logical_and(place_in_run == 0, run_below)

    def relays(upward, part):
        return jnp.logical_and(place_in_run == 2 * part + (1 if upward else 2), run_above if upward else run_below)

    last_here = start + RUN - 1
    first_above = jnp.minimum(start + RUN, subs - 1)
    last_below = jnp.maximum(start - 1, 0)

    def up_relay(part):
        return start + 2 * part + 1

    def down_relay(part):
        return start + 2 * part + 2

    for part in range(PARTS):
        pl.when(relays(True, part))(lambda: greet(tile, last_here))
        pl.when(relays(False, part))(lambda: greet(tile, start))

    lane = lax.broadcasted_iota(jnp.int32, (ROWS, TY), 1)
    not_last = lane < TY - 1
    not_first = lane > 0
    zeros_pad = jnp.zeros((PAD, TY), jnp.float32)
    for comp in range(3):
        for plane in range(2):
            for buf in (s0, s1):
                buf[comp, plane, PAD + TX : PAD + TX + PAD, :] = zeros_pad
            for buf in (h1, h2):
                buf[comp, plane, 0:PAD, :] = zeros_pad
    for buf in (decayed, mixed):
        buf[0, 0, PAD + TX : PAD + TX + PAD, :] = zeros_pad
    under[1, 0, 0:PAD, :] = zeros_pad
    up_out, down_out = (up_out0, up_out1), (down_out0, down_out1)
    up_in, down_in, relay_in = (up_in0, up_in1), (down_in0, down_in1), (relay_in0, relay_in1)

    def at(buf, comp, plane, row):
        return buf[comp, plane, pl.ds(PAD + row, ROWS), :]

    def put(buf, comp, plane, row, value):
        buf[comp, plane, pl.ds(PAD + row, ROWS), :] = value

    def plus_x(buf, comp, plane, row):
        return buf[comp, plane, pl.ds(PAD + row + 1, ROWS), :] - at(buf, comp, plane, row)

    def minus_x(buf, comp, plane, row):
        return at(buf, comp, plane, row) - buf[comp, plane, pl.ds(PAD + row - 1, ROWS), :]

    def plus_y(value):
        return jnp.where(not_last, pltpu.roll(value, TY - 1, 1), 0.0) - value

    def minus_y(value):
        return value - jnp.where(not_first, pltpu.roll(value, 1, 1), 0.0)

    def curl_z(buf, plane, row):
        return plus_x(buf, 1, plane, row) - plus_y(at(buf, 0, plane, row))

    ramp_lane = lane.astype(jnp.float32) + 0.5
    ramp_y = jnp.minimum(jnp.minimum(ramp_lane, TY - ramp_lane) * (1.0 / BAND), 1.0)
    row_iota = lax.broadcasted_iota(jnp.int32, (ROWS, TY), 0)

    def weight(row):
        position = (row_iota + row).astype(jnp.float32) + 0.5
        return jnp.minimum(jnp.minimum(position, TX - position) * (1.0 / BAND), 1.0) * ramp_y

    def rows_of(buf, index, row):
        return buf[index, pl.ds(row, ROWS), :]

    def depth_rows(turn, upward, first, count):
        return (up_out if upward else down_out)[turn].at[:, first : first + count]

    def depth_copy(turn, upward, count):
        slot = turn * 2 + int(upward)
        return pltpu.make_async_remote_copy(
            depth_rows(turn, upward, 0, count), (up_in if upward else down_in)[turn].at[:, 0:count],
            depth_send.at[slot], depth_recv.at[slot],
            device_id=(tile, above if upward else below), device_id_type=MESH)

    def part_copy(turn, upward, part):
        relay = up_relay(part) if upward else down_relay(part)
        first, count = PIECES[int(upward)][part]
        return pltpu.make_async_remote_copy(
            depth_rows(turn, upward, first, count), relay_in[turn].at[:, 0:count],
            part_send.at[turn * PARTS + part], relay_recv.at[turn],
            device_id=(tile, relay), device_id_type=MESH)

    def relay_copy(turn, upward, part):
        first, count = PIECES[int(upward)][part]
        return pltpu.make_async_remote_copy(
            relay_in[turn].at[:, 0:count], (up_in if upward else down_in)[turn].at[:, first : first + count],
            relay_send.at[turn], part_recv.at[turn * PARTS + part],
            device_id=(tile, first_above if upward else last_below), device_id_type=MESH)

    def send_depth(turn, upward):
        crosses = crosses_up if upward else crosses_down
        plain = jnp.logical_and(has_above if upward else has_below, jnp.logical_not(crosses))

        pl.when(plain)(lambda: depth_copy(turn, upward, TX).start())

        @pl.when(crosses)
        def _():
            for part in (1, 0, 2) if not upward else (1, 2, 0):
                part_copy(turn, upward, part).start()
            depth_copy(turn, upward, DIRECT[int(upward)]).start()

    late_up = start + 2 * RUN < subs

    def relay_depth(turn, late):
        for upward in (True, False):
            if late and not upward:
                continue
            for part in range(PARTS):
                now = relays(upward, part)
                if upward:
                    now = jnp.logical_and(now, late_up if late else jnp.logical_not(late_up))

                @pl.when(now)
                def _():
                    part_copy(turn, upward, part).wait_recv()
                    relay_copy(turn, upward, part).start()

    def wait_depth(turn):
        for upward, crosses in ((True, crosses_down), (False, crosses_up)):
            plain = jnp.logical_and(has_below if upward else has_above, jnp.logical_not(crosses))
            pl.when(plain)(lambda: depth_copy(turn, upward, TX).wait_recv())

            @pl.when(crosses)
            def _():
                depth_copy(turn, upward, DIRECT[int(upward)]).wait_recv()
                for part in range(PARTS):
                    relay_copy(turn, upward, part).wait_recv()

    def finish_depth(turn):
        for upward, crosses in ((True, crosses_up), (False, crosses_down)):
            plain = jnp.logical_and(has_above if upward else has_below, jnp.logical_not(crosses))
            pl.when(plain)(lambda: depth_copy(turn, upward, TX).wait_send())

            @pl.when(crosses)
            def _():
                for part in range(PARTS):
                    part_copy(turn, upward, part).wait_send()
                depth_copy(turn, upward, DIRECT[int(upward)]).wait_send()

            for part in range(PARTS):
                pl.when(relays(upward, part))(lambda: relay_copy(turn, upward, part).wait_send())

    def band_copy(kind, group, toward_next):
        first, count = GROUPS[group]
        source, target = ((yc_out, yc_in), (xn_out, xn_in), (yn_out, yn_in), (xc_out, xc_in))[kind]
        direction = int(toward_next)
        if kind in (0, 2):
            other = y_next if toward_next else y_prev
        else:
            other = x_next if toward_next else x_prev
        slot = (kind * 2 + group) * 2 + direction
        part = slice(first, first + count)
        return pltpu.make_async_remote_copy(
            source.at[direction, part], target.at[direction, part],
            band_send.at[slot], band_recv.at[slot],
            device_id=(other, sub), device_id_type=MESH)

    def send_band(kind, group):
        for toward_next in (False, True):
            band_copy(kind, group, toward_next).start()

    def wait_band(kind, group):
        for toward_next in (False, True):
            band_copy(kind, group, toward_next).wait_recv()

    for number in (3, 4, 0, 1):
        loads[number].wait()
    d0, d1, d2, d3 = (decay[i] for i in range(4))
    c0, c1, c2, c3 = (coupling[i] for i in range(4))

    def scale(row):
        for plane in range(2):
            label = mat[plane, pl.ds(row, ROWS), :]
            is0, is1, is2 = label == 0, label == 1, label == 2
            couple = jnp.where(is0, c0, jnp.where(is1, c1, jnp.where(is2, c2, c3)))
            decays = jnp.where(is0, d0, jnp.where(is1, d1, jnp.where(is2, d2, d3)))
            cb[plane, pl.ds(row, ROWS), :] = couple
            ca[plane, pl.ds(row, ROWS), :] = decays
            (down_out, up_out)[plane][1][2, pl.ds(row, ROWS), :] = couple
            scaled = [couple * at(field, comp, plane, row) for comp in range(3)]
            for comp in range(3):
                put(s0, comp, plane, row, scaled[comp])
            if plane == 0:
                for comp in range(2):
                    down_out[0][comp, pl.ds(row, ROWS), :] = scaled[comp]
            else:
                put(decayed, 0, 0, row, decays * scaled[2])

    row_tiles(scale)
    count = lambda flag, number: jnp.where(flag, number, 0)
    crosses_any = jnp.logical_or(crosses_up, crosses_down)
    pl.semaphore_wait(barrier, 3 + count(jnp.logical_and(in_line > 0, in_line < LINE - 1), 1) + count(has_below, 1) + count(has_above, 1) + count(crosses_any, PARTS))
    def pass_word(step):
        for onward in range(2):
            place = step if onward else LINE - 1 - step

            @pl.when(in_line == place)
            def _():
                if step > 0:
                    pl.semaphore_wait(word_sem.at[onward], 1)
                if step < LINE - 1:
                    pl.semaphore_signal(
                        word_sem.at[onward], inc=1, device_id=(x_next if onward else x_prev, sub), device_id_type=MESH)

    send_depth(0, False)
    pass_word(0)
    loads[2].wait()

    def without_above(hbuf, offset, sbuf, row):
        s_x, s_y, s_z = (at(sbuf, comp, 1, row) for comp in range(3))
        part_x = at(hbuf, offset, 1, row) + plus_y(s_z) + s_y
        part_y = at(hbuf, offset + 1, 1, row) - s_x - plus_x(sbuf, 2, 1, row)
        return part_x, part_y

    def first_partial(row):
        up_out[0][0, pl.ds(row, ROWS), :], up_out[0][1, pl.ds(row, ROWS), :] = without_above(field, HX, s0, row)

    row_tiles(first_partial)
    send_depth(0, True)

    def magnetic_local(hbuf, offset, sbuf, row):
        s_x0, s_y0, s_z0 = (at(sbuf, comp, 0, row) for comp in range(3))
        new_x = at(hbuf, offset, 0, row) + plus_y(s_z0) - (at(sbuf, 1, 1, row) - s_y0)
        new_y = at(hbuf, offset + 1, 0, row) + (at(sbuf, 0, 1, row) - s_x0) - plus_x(sbuf, 2, 0, row)
        new_z = at(hbuf, offset + 2, 0, row) + curl_z(sbuf, 0, row)
        new_z1 = at(hbuf, offset + 2, 1, row) + curl_z(sbuf, 1, row)
        return new_x, new_y, new_z, new_z1

    def first_local(row):
        new_x, new_y, new_z, new_z1 = magnetic_local(field, HX, s0, row)
        put(h1, 0, 0, row, new_x)
        put(h1, 1, 0, row, new_y)
        put(h1, 2, 0, row, new_z)
        put(h1, 2, 1, row, new_z1)

    row_tiles(first_local)

    def second_terms(row):
        h_x, h_y = at(h1, 0, 0, row), at(h1, 1, 0, row)
        decays, couple = rows_of(ca, 1, row), rows_of(cb, 1, row)
        part_x = decays * at(field, EX, 1, row) - MAGNETIC * (minus_y(at(h1, 2, 1, row)) + h_y)
        part_y = decays * at(field, EY, 1, row) + MAGNETIC * (h_x + minus_x(h1, 2, 1, row))
        up_out[1][0, pl.ds(row, ROWS), :] = plus_y(at(decayed, 0, 0, row)) + couple * part_y
        up_out[1][1, pl.ds(row, ROWS), :] = -couple * part_x - plus_x(decayed, 0, 0, row)
        decays, couple = rows_of(ca, 0, row), rows_of(cb, 0, row)
        down_out[1][0, pl.ds(row, ROWS), :] = couple * (
            decays * at(field, EX, 0, row) - MAGNETIC * (minus_y(at(h1, 2, 0, row)) - h_y))
        down_out[1][1, pl.ds(row, ROWS), :] = couple * (
            decays * at(field, EY, 0, row) - MAGNETIC * (h_x - minus_x(h1, 2, 0, row)))

    row_tiles(second_terms)
    send_depth(1, False)
    send_depth(1, True)

    @pl.when(jnp.logical_not(has_above))
    def _():
        def clear(row):
            for buf in down_in:
                for comp in range(buf.shape[0]):
                    buf[comp, pl.ds(row, ROWS), :] = jnp.zeros((ROWS, TY), jnp.float32)

        row_tiles(clear)

    @pl.when(jnp.logical_not(has_below))
    def _():
        def cancel(row):
            up_in[0][0, pl.ds(row, ROWS), :] = at(s0, 1, 0, row)
            up_in[0][1, pl.ds(row, ROWS), :] = -at(s0, 0, 0, row)
            for comp in range(3):
                up_in[1][comp, pl.ds(row, ROWS), :] = jnp.zeros((ROWS, TY), jnp.float32)

        row_tiles(cancel)

    def electric_xy(ebuf, hbuf, plane, row, h_x, h_y, under_x, under_y):
        h_z = at(hbuf, 2, plane, row)
        decays = rows_of(ca, plane, row)
        new_x = decays * at(ebuf, 0, plane, row) - MAGNETIC * (minus_y(h_z) - (h_y - under_y))
        new_y = decays * at(ebuf, 1, plane, row) - MAGNETIC * ((h_x - under_x) - minus_x(hbuf, 2, plane, row))
        return new_x, new_y

    def electric_z(ebuf, hbuf, plane, row, h_x):
        decays = rows_of(ca, plane, row)
        return decays * at(ebuf, 2, plane, row) - MAGNETIC * (minus_x(hbuf, 1, plane, row) - minus_y(h_x))

    for step in range(1, LINE - 1):
        pass_word(step)
    relay_depth(0, False)
    wait_depth(0)
    relay_depth(1, False)

    def first_rest(row):
        x1 = rows_of(up_out[0], 0, row) - rows_of(down_in[0], 1, row)
        y1 = rows_of(up_out[0], 1, row) + rows_of(down_in[0], 0, row)
        under_x = rows_of(up_in[0], 0, row) - at(s0, 1, 0, row)
        under_y = rows_of(up_in[0], 1, row) + at(s0, 0, 0, row)
        put(h1, 0, 1, row, x1)
        put(h1, 1, 1, row, y1)
        put(under, 0, 0, row, under_x)
        put(under, 1, 0, row, under_y)
        x0, y0 = at(h1, 0, 0, row), at(h1, 1, 0, row)
        for plane, (h_x, h_y, b_x, b_y) in enumerate(((x0, y0, under_x, under_y), (x1, y1, x0, y0))):
            new = (*electric_xy(field, h1, plane, row, h_x, h_y, b_x, b_y), electric_z(field, h1, plane, row, h_x))
            couple = rows_of(cb, plane, row)
            for comp in range(3):
                put(e1, comp, plane, row, new[comp])
                put(s1, comp, plane, row, couple * new[comp])

    row_tiles(first_rest)

    def keep(name, row, value, weights):
        w[2 * name[0] + name[1], pl.ds(row, ROWS), :] = value * weights

    def second_local(row):
        new_x, new_y, new_z, new_z1 = magnetic_local(h1, 0, s1, row)
        put(h2, 0, 0, row, new_x)
        put(h2, 1, 0, row, new_y)
        put(h2, 2, 0, row, new_z)
        put(h2, 2, 1, row, new_z1)
        weights = weight(row)
        keep((HX, 0), row, new_x, weights)
        keep((HY, 0), row, new_y, weights)
        keep((HZ, 0), row, new_z, weights)
        keep((HZ, 1), row, new_z1, weights)
        keep((EZ, 0), row, electric_z(e1, h2, 0, row, new_x), weights)

    row_tiles(second_local)

    def slot_of(rows):
        return lax.broadcasted_iota(jnp.int32, (rows, TY), 1) // BAND

    def pack_lanes(values):
        slot = slot_of(values[0].shape[0])
        turned = [values[0]] + [pltpu.roll(values[k], BAND * k, 1) for k in (1, 2, 3)]
        low, high = turned[3], turned[0]
        for k in (2, 1, 0):
            low = jnp.where(slot == k, turned[k], low)
            high = jnp.where(slot == k, turned[k + 1], high)
        return low, high

    def unpack_lanes(low_side, high_side):
        slot = slot_of(low_side.shape[0])
        turned = []
        for k in range(4):
            mixed = jnp.where(slot == (k + 3) % 4, low_side, high_side)
            shift = (TY - BAND * (k - 1)) % TY
            turned.append(pltpu.roll(mixed, shift, 1) if shift else mixed)
        return [jnp.where(slot == 0, turned[k], jnp.where(slot == 3, turned[(k + 2) % 4], 0.0)) for k in range(4)]

    corner_rows = (0, 16, TX - 32, TX - 16)
    middle_rows = (32, 80, 128, 176)

    def middle_lanes():
        slot = slot_of(16)
        return jnp.logical_or(slot == 1, slot == 2)

    def pack_corners(index):
        values = [w[PLACE[index], first : first + 16, :] for first in corner_rows]
        low, high = pack_lanes(values)
        yc_out[0, index], yc_out[1, index] = low, high
        middle = middle_lanes()
        for direction in range(2):
            xn_out[direction, index] = jnp.where(
                middle, values[2 * direction], pltpu.roll(values[2 * direction + 1], TY // 2, 1))

    def pack_middle(index):
        low, high = pack_lanes([w[PLACE[index], first : first + 48, :] for first in middle_rows])
        yn_out[0, index], yn_out[1, index] = low, high

    def add_corners(index):
        added = unpack_lanes(yc_in[1, index], yc_in[0, index])
        values = []
        for first, more in zip(corner_rows, added):
            total = w[PLACE[index], first : first + 16, :] + more
            w[PLACE[index], first : first + 16, :] = total
            values.append(total)
        middle = middle_lanes()
        for direction in range(2):
            xc_out[direction, index] = jnp.where(
                middle, pltpu.roll(values[2 * direction + 1], TY // 2, 1), values[2 * direction])

    def add_middle(index):
        added = unpack_lanes(yn_in[1, index], yn_in[0, index])
        for first, more in zip(middle_rows, added):
            w[PLACE[index], first : first + 48, :] += more

    def add_x_bands(index):
        middle = middle_lanes()
        for side_of, first in ((1, 0), (0, TX - 32)):
            plain, summed = xn_in[side_of, index], xc_in[side_of, index]
            w[PLACE[index], first : first + 16, :] += jnp.where(middle, plain, summed)
            w[PLACE[index], first + 16 : first + 32, :] += pltpu.roll(jnp.where(middle, summed, plain), TY // 2, 1)

    def send_group(group):
        planes_of(group, pack_corners)
        send_band(0, group)
        send_band(1, group)
        planes_of(group, pack_middle)
        send_band(2, group)

    pass_word(LINE - 1)
    send_group(0)
    relay_depth(0, True)
    relay_depth(1, True)
    wait_depth(1)

    def mix(row):
        turn_z = minus_x(under, 1, 0, row) - minus_y(at(under, 0, 0, row))
        put(mixed, 0, 0, row, MAGNETIC * rows_of(up_in[1], 2, row) * turn_z)

    row_tiles(mix)

    def second_rest(row):
        x1, y1 = without_above(h1, 0, s1, row)
        couple = MAGNETIC * rows_of(down_in[1], 2, row)
        x1 -= rows_of(down_in[1], 1, row) + couple * at(h1, 0, 1, row)
        y1 += rows_of(down_in[1], 0, row) - couple * at(h1, 1, 1, row)
        couple = MAGNETIC * rows_of(up_in[1], 2, row)
        under_x, under_y = at(under, 0, 0, row), at(under, 1, 0, row)
        under_x += rows_of(up_in[1], 0, row) - couple * under_x - plus_y(at(mixed, 0, 0, row)) - at(s1, 1, 0, row)
        under_y += rows_of(up_in[1], 1, row) - couple * under_y + plus_x(mixed, 0, 0, row) + at(s1, 0, 0, row)
        under_x = jnp.where(has_below, under_x, 0.0)
        under_y = jnp.where(has_below, under_y, 0.0)
        put(h2, 0, 1, row, x1)
        put(h2, 1, 1, row, y1)
        x0, y0 = at(h2, 0, 0, row), at(h2, 1, 0, row)
        weights = weight(row)
        keep((HX, 1), row, x1, weights)
        keep((HY, 1), row, y1, weights)
        for plane, (h_x, h_y, b_x, b_y) in enumerate(((x0, y0, under_x, under_y), (x1, y1, x0, y0))):
            new_x, new_y = electric_xy(e1, h2, plane, row, h_x, h_y, b_x, b_y)
            keep((EX, plane), row, new_x, weights)
            keep((EY, plane), row, new_y, weights)
        keep((EZ, 1), row, electric_z(e1, h2, 1, row, x1), weights)

    row_tiles(second_rest)
    send_group(1)

    for group in range(2):
        wait_band(0, group)
        planes_of(group, add_corners)
        send_band(3, group)

    for group in range(2):
        wait_band(2, group)
        planes_of(group, add_middle)
        wait_band(1, group)
        wait_band(3, group)
        planes_of(group, add_x_bands)

    for turn in range(2):
        finish_depth(turn)
    for group in range(2):
        for kind in range(4):
            for toward_next in (False, True):
                band_copy(kind, group, toward_next).wait_send()


def on_device(tiles, subs, seeds, material, decay, coupling):
    f32 = jnp.float32
    padded = (3, 2, PAD + TX + PAD, TY)
    planes = len(ORDER)
    narrow, wide = pltpu.VMEM((2, planes, 16, TY), f32), pltpu.VMEM((2, planes, 48, TY), f32)
    hbm = pl.BlockSpec(memory_space=pltpu.HBM)
    done = pl.pallas_call(
        functools.partial(kernel, tiles, subs),
        out_shape=jax.ShapeDtypeStruct((planes, TX, TY), f32),
        in_specs=[hbm] * 4,
        out_specs=pl.BlockSpec(memory_space=pltpu.VMEM),
        scratch_shapes=[
            pltpu.SMEM(decay.shape, f32),
            pltpu.SMEM(coupling.shape, f32),
            pltpu.VMEM((6, *padded[1:]), f32),
            pltpu.VMEM((2, TX, TY), jnp.int32),
            pltpu.VMEM((2, TX, TY), f32),
            pltpu.VMEM((2, TX, TY), f32),
            *[pltpu.VMEM(padded, f32)] * 5,
            *[pltpu.VMEM((count, 1, *padded[2:]), f32) for count in (1, 2, 1)],
            *[pltpu.VMEM((count, TX, TY), f32) for count in (2, 3)] * 4,
            *[pltpu.VMEM((count, MOST, TY), f32) for count in (2, 3)],
            narrow, wide, narrow, narrow,
            narrow, wide, narrow, narrow,
            pltpu.SemaphoreType.DMA((5,)),
            pltpu.SemaphoreType.DMA((4,)),
            pltpu.SemaphoreType.DMA((4,)),
            pltpu.SemaphoreType.DMA((2 * PARTS,)),
            pltpu.SemaphoreType.DMA((2 * PARTS,)),
            pltpu.SemaphoreType.DMA((2,)),
            pltpu.SemaphoreType.DMA((2,)),
            pltpu.SemaphoreType.DMA((16,)),
            pltpu.SemaphoreType.DMA((16,)),
            pltpu.SemaphoreType.REGULAR((2,)),
        ],
        compiler_params=pltpu.CompilerParams(
            collective_id=0, has_side_effects=True, vmem_limit_bytes=20 * 2**20),
    )(*(pltpu.with_memory_space_constraint(array, pltpu.HBM) for array in (decay, coupling, seeds, material)))
    return done.reshape(seeds.shape)


def solution(mesh):
    placed = (P("tile", None, "sub", None, None), P("tile", "sub", None, None), P(), P())
    return jax.shard_map(
        functools.partial(on_device, mesh.shape["tile"], mesh.shape["sub"]),
        mesh=mesh,
        in_specs=placed,
        out_specs=P("tile", None, "sub", None, None),
        check_vma=False,
    )
```

```python
import functools
import math

import jax
import jax.numpy as jnp
from jax import lax
from jax.experimental import pallas as pl
from jax.experimental.pallas import tpu as pltpu
from jax.sharding import PartitionSpec as P

BAND = 32
MESH = pl.DeviceIdType.MESH
MAGNETIC = 0.5
TX = 256
TY = 128
PAD = 8
ROWS = 32
EX, EY, EZ, HX, HY, HZ = range(6)

EARLY = ((HX, 0), (HY, 0), (HZ, 0), (HZ, 1), (EZ, 0))
LATE = ((HX, 1), (HY, 1), (EX, 0), (EY, 0), (EX, 1), (EY, 1), (EZ, 1))
ORDER = EARLY + LATE
GROUPS = ((0, len(EARLY)), (len(EARLY), len(LATE)))
PLACE = tuple(2 * comp + plane for comp, plane in ORDER)

RUN = 8
PARTS = 3
LINE = 4
DIRECT = (104, 88)
PIECES = (((104, 40), (144, 40), (184, 72)), ((88, 64), (152, 56), (208, 48)))
MOST = 72


def row_tiles(body):
    def step(index, carry):
        body(pl.multiple_of(index * ROWS, ROWS))
        return carry

    lax.fori_loop(0, TX // ROWS, step, 0, unroll=8)


def planes_of(group, body):
    first, count = GROUPS[group]
    for index in range(first, first + count):
        body(index)


def kernel(
    tiles, subs, decay_in, coupling_in, seeds, material, w,
    decay, coupling, field, mat, ca, cb, s0, s1, h1, h2, e1, decayed, under, mixed,
    up_out0, up_out1, down_out0, down_out1, up_in0, up_in1, down_in0, down_in1, relay_in0, relay_in1,
    yc_out, yn_out, xn_out, xc_out, yc_in, yn_in, xn_in, xc_in,
    load_sem, depth_send, depth_recv, part_send, part_recv, relay_recv, relay_send, band_send, band_recv, word_sem,
):
    tile = lax.axis_index("tile")
    sub = lax.axis_index("sub")
    side = math.isqrt(tiles)
    has_below = sub > 0
    has_above = sub < subs - 1
    below = jnp.maximum(sub - 1, 0)
    above = jnp.minimum(sub + 1, subs - 1)
    x_prev = lax.rem(tile + tiles - 1, tiles)
    x_next = lax.rem(tile + 1, tiles)
    y_prev = lax.rem(tile + tiles - side, tiles)
    y_next = lax.rem(tile + side, tiles)

    loads = [
        pltpu.make_async_copy(material.at[0], mat, load_sem.at[0]),
        pltpu.make_async_copy(seeds.at[0, 0:3], field.at[0:3, :, PAD : PAD + TX], load_sem.at[1]),
        pltpu.make_async_copy(seeds.at[0, 3:6], field.at[3:6, :, PAD : PAD + TX], load_sem.at[2]),
        pltpu.make_async_copy(decay_in, decay, load_sem.at[3]),
        pltpu.make_async_copy(coupling_in, coupling, load_sem.at[4]),
    ]
    barrier = pltpu.get_barrier_semaphore()

    def greet(other_tile, other_sub):
        pl.semaphore_signal(barrier, inc=1, device_id=(other_tile, other_sub), device_id_type=MESH)

    pl.when(has_below)(lambda: greet(tile, below))
    pl.when(has_above)(lambda: greet(tile, above))
    for load in loads:
        load.start()
    in_line = lax.rem(tile, LINE)
    for other in (y_prev, y_next):
        greet(other, sub)
    pl.when(in_line > 0)(lambda: greet(x_prev, sub))
    pl.when(in_line < LINE - 1)(lambda: greet(x_next, sub))
    place_in_run = lax.rem(sub, RUN)
    start = sub - place_in_run
    run_above = start + RUN < subs
    run_below = start > 0
    crosses_up = jnp.logical_and(place_in_run == RUN - 1, run_above)
    crosses_down = jnp.logical_and(place_in_run == 0, run_below)

    def relays(upward, part):
        return jnp.logical_and(place_in_run == 2 * part + (1 if upward else 2), run_above if upward else run_below)

    last_here = start + RUN - 1
    first_above = jnp.minimum(start + RUN, subs - 1)
    last_below = jnp.maximum(start - 1, 0)

    def up_relay(part):
        return start + 2 * part + 1

    def down_relay(part):
        return start + 2 * part + 2

    for part in range(PARTS):
        pl.when(relays(True, part))(lambda: greet(tile, last_here))
        pl.when(relays(False, part))(lambda: greet(tile, start))

    lane = lax.broadcasted_iota(jnp.int32, (ROWS, TY), 1)
    not_last = lane < TY - 1
    not_first = lane > 0
    zeros_pad = jnp.zeros((PAD, TY), jnp.float32)
    for comp in range(3):
        for plane in range(2):
            for buf in (s0, s1):
                buf[comp, plane, PAD + TX : PAD + TX + PAD, :] = zeros_pad
            for buf in (h1, h2):
                buf[comp, plane, 0:PAD, :] = zeros_pad
    for buf in (decayed, mixed):
        buf[0, 0, PAD + TX : PAD + TX + PAD, :] = zeros_pad
    under[1, 0, 0:PAD, :] = zeros_pad
    up_out, down_out = (up_out0, up_out1), (down_out0, down_out1)
    up_in, down_in, relay_in = (up_in0, up_in1), (down_in0, down_in1), (relay_in0, relay_in1)

    def at(buf, comp, plane, row):
        return buf[comp, plane, pl.ds(PAD + row, ROWS), :]

    def put(buf, comp, plane, row, value):
        buf[comp, plane, pl.ds(PAD + row, ROWS), :] = value

    def plus_x(buf, comp, plane, row):
        return buf[comp, plane, pl.ds(PAD + row + 1, ROWS), :] - at(buf, comp, plane, row)

    def minus_x(buf, comp, plane, row):
        return at(buf, comp, plane, row) - buf[comp, plane, pl.ds(PAD + row - 1, ROWS), :]

    def plus_y(value):
        return jnp.where(not_last, pltpu.roll(value, TY - 1, 1), 0.0) - value

    def minus_y(value):
        return value - jnp.where(not_first, pltpu.roll(value, 1, 1), 0.0)

    def curl_z(buf, plane, row):
        return plus_x(buf, 1, plane, row) - plus_y(at(buf, 0, plane, row))

    ramp_lane = lane.astype(jnp.float32) + 0.5
    ramp_y = jnp.minimum(jnp.minimum(ramp_lane, TY - ramp_lane) * (1.0 / BAND), 1.0)
    row_iota = lax.broadcasted_iota(jnp.int32, (ROWS, TY), 0)

    def weight(row):
        position = (row_iota + row).astype(jnp.float32) + 0.5
        return jnp.minimum(jnp.minimum(position, TX - position) * (1.0 / BAND), 1.0) * ramp_y

    def rows_of(buf, index, row):
        return buf[index, pl.ds(row, ROWS), :]

    def depth_rows(turn, upward, first, count):
        return (up_out if upward else down_out)[turn].at[:, first : first + count]

    def depth_copy(turn, upward, count):
        slot = turn * 2 + int(upward)
        return pltpu.make_async_remote_copy(
            depth_rows(turn, upward, 0, count), (up_in if upward else down_in)[turn].at[:, 0:count],
            depth_send.at[slot], depth_recv.at[slot],
            device_id=(tile, above if upward else below), device_id_type=MESH)

    def part_copy(turn, upward, part):
        relay = up_relay(part) if upward else down_relay(part)
        first, count = PIECES[int(upward)][part]
        return pltpu.make_async_remote_copy(
            depth_rows(turn, upward, first, count), relay_in[turn].at[:, 0:count],
            part_send.at[turn * PARTS + part], relay_recv.at[turn],
            device_id=(tile, relay), device_id_type=MESH)

    def relay_copy(turn, upward, part):
        first, count = PIECES[int(upward)][part]
        return pltpu.make_async_remote_copy(
            relay_in[turn].at[:, 0:count], (up_in if upward else down_in)[turn].at[:, first : first + count],
            relay_send.at[turn], part_recv.at[turn * PARTS + part],
            device_id=(tile, first_above if upward else last_below), device_id_type=MESH)

    def send_depth(turn, upward):
        crosses = crosses_up if upward else crosses_down
        plain = jnp.logical_and(has_above if upward else has_below, jnp.logical_not(crosses))

        pl.when(plain)(lambda: depth_copy(turn, upward, TX).start())

        @pl.when(crosses)
        def _():
            for part in (1, 0, 2) if not upward else (1, 2, 0):
                part_copy(turn, upward, part).start()
            depth_copy(turn, upward, DIRECT[int(upward)]).start()

    late_up = start + 2 * RUN < subs

    def relay_depth(turn, late):
        for upward in (True, False):
            if late and not upward:
                continue
            for part in range(PARTS):
                now = relays(upward, part)
                if upward:
                    now = jnp.logical_and(now, late_up if late else jnp.logical_not(late_up))

                @pl.when(now)
                def _():
                    part_copy(turn, upward, part).wait_recv()
                    relay_copy(turn, upward, part).start()

    def wait_depth(turn):
        for upward, crosses in ((True, crosses_down), (False, crosses_up)):
            plain = jnp.logical_and(has_below if upward else has_above, jnp.logical_not(crosses))
            pl.when(plain)(lambda: depth_copy(turn, upward, TX).wait_recv())

            @pl.when(crosses)
            def _():
                depth_copy(turn, upward, DIRECT[int(upward)]).wait_recv()
                for part in range(PARTS):
                    relay_copy(turn, upward, part).wait_recv()

    def finish_depth(turn):
        for upward, crosses in ((True, crosses_up), (False, crosses_down)):
            plain = jnp.logical_and(has_above if upward else has_below, jnp.logical_not(crosses))
            pl.when(plain)(lambda: depth_copy(turn, upward, TX).wait_send())

            @pl.when(crosses)
            def _():
                for part in range(PARTS):
                    part_copy(turn, upward, part).wait_send()
                depth_copy(turn, upward, DIRECT[int(upward)]).wait_send()

            for part in range(PARTS):
                pl.when(relays(upward, part))(lambda: relay_copy(turn, upward, part).wait_send())

    def band_copy(kind, group, toward_next):
        first, count = GROUPS[group]
        source, target = ((yc_out, yc_in), (xn_out, xn_in), (yn_out, yn_in), (xc_out, xc_in))[kind]
        direction = int(toward_next)
        if kind in (0, 2):
            other = y_next if toward_next else y_prev
        else:
            other = x_next if toward_next else x_prev
        slot = (kind * 2 + group) * 2 + direction
        part = slice(first, first + count)
        return pltpu.make_async_remote_copy(
            source.at[direction, part], target.at[direction, part],
            band_send.at[slot], band_recv.at[slot],
            device_id=(other, sub), device_id_type=MESH)

    def send_band(kind, group):
        for toward_next in (False, True):
            band_copy(kind, group, toward_next).start()

    def wait_band(kind, group):
        for toward_next in (False, True):
            band_copy(kind, group, toward_next).wait_recv()

    for number in (3, 4, 0, 1):
        loads[number].wait()
    d0, d1, d2, d3 = (decay[i] for i in range(4))
    c0, c1, c2, c3 = (coupling[i] for i in range(4))

    def scale(row):
        for plane in range(2):
            label = mat[plane, pl.ds(row, ROWS), :]
            is0, is1, is2 = label == 0, label == 1, label == 2
            couple = jnp.where(is0, c0, jnp.where(is1, c1, jnp.where(is2, c2, c3)))
            decays = jnp.where(is0, d0, jnp.where(is1, d1, jnp.where(is2, d2, d3)))
            cb[plane, pl.ds(row, ROWS), :] = couple
            ca[plane, pl.ds(row, ROWS), :] = decays
            (down_out, up_out)[plane][1][2, pl.ds(row, ROWS), :] = couple
            scaled = [couple * at(field, comp, plane, row) for comp in range(3)]
            for comp in range(3):
                put(s0, comp, plane, row, scaled[comp])
            if plane == 0:
                for comp in range(2):
                    down_out[0][comp, pl.ds(row, ROWS), :] = scaled[comp]
            else:
                put(decayed, 0, 0, row, decays * scaled[2])

    row_tiles(scale)
    count = lambda flag, number: jnp.where(flag, number, 0)
    crosses_any = jnp.logical_or(crosses_up, crosses_down)
    pl.semaphore_wait(barrier, 3 + count(jnp.logical_and(in_line > 0, in_line < LINE - 1), 1) + count(has_below, 1) + count(has_above, 1) + count(crosses_any, PARTS))
    def pass_word(step):
        for onward in range(2):
            place = step if onward else LINE - 1 - step

            @pl.when(in_line == place)
            def _():
                if step > 0:
                    pl.semaphore_wait(word_sem.at[onward], 1)
                if step < LINE - 1:
                    pl.semaphore_signal(
                        word_sem.at[onward], inc=1, device_id=(x_next if onward else x_prev, sub), device_id_type=MESH)

    send_depth(0, False)
    pass_word(0)
    loads[2].wait()

    def without_above(hbuf, offset, sbuf, row):
        s_x, s_y, s_z = (at(sbuf, comp, 1, row) for comp in range(3))
        part_x = at(hbuf, offset, 1, row) + plus_y(s_z) + s_y
        part_y = at(hbuf, offset + 1, 1, row) - s_x - plus_x(sbuf, 2, 1, row)
        return part_x, part_y

    def first_partial(row):
        up_out[0][0, pl.ds(row, ROWS), :], up_out[0][1, pl.ds(row, ROWS), :] = without_above(field, HX, s0, row)

    row_tiles(first_partial)
    send_depth(0, True)

    def magnetic_local(hbuf, offset, sbuf, row):
        s_x0, s_y0, s_z0 = (at(sbuf, comp, 0, row) for comp in range(3))
        new_x = at(hbuf, offset, 0, row) + plus_y(s_z0) - (at(sbuf, 1, 1, row) - s_y0)
        new_y = at(hbuf, offset + 1, 0, row) + (at(sbuf, 0, 1, row) - s_x0) - plus_x(sbuf, 2, 0, row)
        new_z = at(hbuf, offset + 2, 0, row) + curl_z(sbuf, 0, row)
        new_z1 = at(hbuf, offset + 2, 1, row) + curl_z(sbuf, 1, row)
        return new_x, new_y, new_z, new_z1

    def first_local(row):
        new_x, new_y, new_z, new_z1 = magnetic_local(field, HX, s0, row)
        put(h1, 0, 0, row, new_x)
        put(h1, 1, 0, row, new_y)
        put(h1, 2, 0, row, new_z)
        put(h1, 2, 1, row, new_z1)

    row_tiles(first_local)

    def second_terms(row):
        h_x, h_y = at(h1, 0, 0, row), at(h1, 1, 0, row)
        decays, couple = rows_of(ca, 1, row), rows_of(cb, 1, row)
        part_x = decays * at(field, EX, 1, row) - MAGNETIC * (minus_y(at(h1, 2, 1, row)) + h_y)
        part_y = decays * at(field, EY, 1, row) + MAGNETIC * (h_x + minus_x(h1, 2, 1, row))
        up_out[1][0, pl.ds(row, ROWS), :] = plus_y(at(decayed, 0, 0, row)) + couple * part_y
        up_out[1][1, pl.ds(row, ROWS), :] = -couple * part_x - plus_x(decayed, 0, 0, row)
        decays, couple = rows_of(ca, 0, row), rows_of(cb, 0, row)
        down_out[1][0, pl.ds(row, ROWS), :] = couple * (
            decays * at(field, EX, 0, row) - MAGNETIC * (minus_y(at(h1, 2, 0, row)) - h_y))
        down_out[1][1, pl.ds(row, ROWS), :] = couple * (
            decays * at(field, EY, 0, row) - MAGNETIC * (h_x - minus_x(h1, 2, 0, row)))

    row_tiles(second_terms)
    send_depth(1, False)
    send_depth(1, True)

    @pl.when(jnp.logical_not(has_above))
    def _():
        def clear(row):
            for buf in down_in:
                for comp in range(buf.shape[0]):
                    buf[comp, pl.ds(row, ROWS), :] = jnp.zeros((ROWS, TY), jnp.float32)

        row_tiles(clear)

    @pl.when(jnp.logical_not(has_below))
    def _():
        def cancel(row):
            up_in[0][0, pl.ds(row, ROWS), :] = at(s0, 1, 0, row)
            up_in[0][1, pl.ds(row, ROWS), :] = -at(s0, 0, 0, row)
            for comp in range(3):
                up_in[1][comp, pl.ds(row, ROWS), :] = jnp.zeros((ROWS, TY), jnp.float32)

        row_tiles(cancel)

    def electric_xy(ebuf, hbuf, plane, row, h_x, h_y, under_x, under_y):
        h_z = at(hbuf, 2, plane, row)
        decays = rows_of(ca, plane, row)
        new_x = decays * at(ebuf, 0, plane, row) - MAGNETIC * (minus_y(h_z) - (h_y - under_y))
        new_y = decays * at(ebuf, 1, plane, row) - MAGNETIC * ((h_x - under_x) - minus_x(hbuf, 2, plane, row))
        return new_x, new_y

    def electric_z(ebuf, hbuf, plane, row, h_x):
        decays = rows_of(ca, plane, row)
        return decays * at(ebuf, 2, plane, row) - MAGNETIC * (minus_x(hbuf, 1, plane, row) - minus_y(h_x))

    for step in range(1, LINE - 1):
        pass_word(step)
    relay_depth(0, False)
    wait_depth(0)
    relay_depth(1, False)

    def first_rest(row):
        x1 = rows_of(up_out[0], 0, row) - rows_of(down_in[0], 1, row)
        y1 = rows_of(up_out[0], 1, row) + rows_of(down_in[0], 0, row)
        under_x = rows_of(up_in[0], 0, row) - at(s0, 1, 0, row)
        under_y = rows_of(up_in[0], 1, row) + at(s0, 0, 0, row)
        put(h1, 0, 1, row, x1)
        put(h1, 1, 1, row, y1)
        put(under, 0, 0, row, under_x)
        put(under, 1, 0, row, under_y)
        x0, y0 = at(h1, 0, 0, row), at(h1, 1, 0, row)
        for plane, (h_x, h_y, b_x, b_y) in enumerate(((x0, y0, under_x, under_y), (x1, y1, x0, y0))):
            new = (*electric_xy(field, h1, plane, row, h_x, h_y, b_x, b_y), electric_z(field, h1, plane, row, h_x))
            couple = rows_of(cb, plane, row)
            for comp in range(3):
                put(e1, comp, plane, row, new[comp])
                put(s1, comp, plane, row, couple * new[comp])

    row_tiles(first_rest)

    def keep(name, row, value, weights):
        w[2 * name[0] + name[1], pl.ds(row, ROWS), :] = value * weights

    def second_local(row):
        new_x, new_y, new_z, new_z1 = magnetic_local(h1, 0, s1, row)
        put(h2, 0, 0, row, new_x)
        put(h2, 1, 0, row, new_y)
        put(h2, 2, 0, row, new_z)
        put(h2, 2, 1, row, new_z1)
        weights = weight(row)
        keep((HX, 0), row, new_x, weights)
        keep((HY, 0), row, new_y, weights)
        keep((HZ, 0), row, new_z, weights)
        keep((HZ, 1), row, new_z1, weights)
        keep((EZ, 0), row, electric_z(e1, h2, 0, row, new_x), weights)

    row_tiles(second_local)

    def slot_of(rows):
        return lax.broadcasted_iota(jnp.int32, (rows, TY), 1) // BAND

    def pack_lanes(values):
        slot = slot_of(values[0].shape[0])
        turned = [values[0]] + [pltpu.roll(values[k], BAND * k, 1) for k in (1, 2, 3)]
        low, high = turned[3], turned[0]
        for k in (2, 1, 0):
            low = jnp.where(slot == k, turned[k], low)
            high = jnp.where(slot == k, turned[k + 1], high)
        return low, high

    def unpack_lanes(low_side, high_side):
        slot = slot_of(low_side.shape[0])
        turned = []
        for k in range(4):
            mixed = jnp.where(slot == (k + 3) % 4, low_side, high_side)
            shift = (TY - BAND * (k - 1)) % TY
            turned.append(pltpu.roll(mixed, shift, 1) if shift else mixed)
        return [jnp.where(slot == 0, turned[k], jnp.where(slot == 3, turned[(k + 2) % 4], 0.0)) for k in range(4)]

    corner_rows = (0, 16, TX - 32, TX - 16)
    middle_rows = (32, 80, 128, 176)

    def middle_lanes():
        slot = slot_of(16)
        return jnp.logical_or(slot == 1, slot == 2)

    def pack_corners(index):
        values = [w[PLACE[index], first : first + 16, :] for first in corner_rows]
        low, high = pack_lanes(values)
        yc_out[0, index], yc_out[1, index] = low, high
        middle = middle_lanes()
        for direction in range(2):
            xn_out[direction, index] = jnp.where(
                middle, values[2 * direction], pltpu.roll(values[2 * direction + 1], TY // 2, 1))

    def pack_middle(index):
        low, high = pack_lanes([w[PLACE[index], first : first + 48, :] for first in middle_rows])
        yn_out[0, index], yn_out[1, index] = low, high

    def add_corners(index):
        added = unpack_lanes(yc_in[1, index], yc_in[0, index])
        values = []
        for first, more in zip(corner_rows, added):
            total = w[PLACE[index], first : first + 16, :] + more
            w[PLACE[index], first : first + 16, :] = total
            values.append(total)
        middle = middle_lanes()
        for direction in range(2):
            xc_out[direction, index] = jnp.where(
                middle, pltpu.roll(values[2 * direction + 1], TY // 2, 1), values[2 * direction])

    def add_middle(index):
        added = unpack_lanes(yn_in[1, index], yn_in[0, index])
        for first, more in zip(middle_rows, added):
            w[PLACE[index], first : first + 48, :] += more

    def add_x_bands(index):
        middle = middle_lanes()
        for side_of, first in ((1, 0), (0, TX - 32)):
            plain, summed = xn_in[side_of, index], xc_in[side_of, index]
            w[PLACE[index], first : first + 16, :] += jnp.where(middle, plain, summed)
            w[PLACE[index], first + 16 : first + 32, :] += pltpu.roll(jnp.where(middle, summed, plain), TY // 2, 1)

    def send_group(group):
        planes_of(group, pack_corners)
        send_band(0, group)
        send_band(1, group)
        planes_of(group, pack_middle)
        send_band(2, group)

    pass_word(LINE - 1)
    send_group(0)
    relay_depth(0, True)
    relay_depth(1, True)
    wait_depth(1)

    def mix(row):
        turn_z = minus_x(under, 1, 0, row) - minus_y(at(under, 0, 0, row))
        put(mixed, 0, 0, row, MAGNETIC * rows_of(up_in[1], 2, row) * turn_z)

    row_tiles(mix)

    def second_rest(row):
        x1, y1 = without_above(h1, 0, s1, row)
        couple = MAGNETIC * rows_of(down_in[1], 2, row)
        x1 -= rows_of(down_in[1], 1, row) + couple * at(h1, 0, 1, row)
        y1 += rows_of(down_in[1], 0, row) - couple * at(h1, 1, 1, row)
        couple = MAGNETIC * rows_of(up_in[1], 2, row)
        under_x, under_y = at(under, 0, 0, row), at(under, 1, 0, row)
        under_x += rows_of(up_in[1], 0, row) - couple * under_x - plus_y(at(mixed, 0, 0, row)) - at(s1, 1, 0, row)
        under_y += rows_of(up_in[1], 1, row) - couple * under_y + plus_x(mixed, 0, 0, row) + at(s1, 0, 0, row)
        under_x = jnp.where(has_below, under_x, 0.0)
        under_y = jnp.where(has_below, under_y, 0.0)
        put(h2, 0, 1, row, x1)
        put(h2, 1, 1, row, y1)
        x0, y0 = at(h2, 0, 0, row), at(h2, 1, 0, row)
        weights = weight(row)
        keep((HX, 1), row, x1, weights)
        keep((HY, 1), row, y1, weights)
        for plane, (h_x, h_y, b_x, b_y) in enumerate(((x0, y0, under_x, under_y), (x1, y1, x0, y0))):
            new_x, new_y = electric_xy(e1, h2, plane, row, h_x, h_y, b_x, b_y)
            keep((EX, plane), row, new_x, weights)
            keep((EY, plane), row, new_y, weights)
        keep((EZ, 1), row, electric_z(e1, h2, 1, row, x1), weights)

    row_tiles(second_rest)
    send_group(1)

    for group in range(2):
        wait_band(0, group)
        planes_of(group, add_corners)
        send_band(3, group)

    for group in range(2):
        wait_band(2, group)
        planes_of(group, add_middle)
        wait_band(1, group)
        wait_band(3, group)
        planes_of(group, add_x_bands)

    for turn in range(2):
        finish_depth(turn)
    for group in range(2):
        for kind in range(4):
            for toward_next in (False, True):
                band_copy(kind, group, toward_next).wait_send()


def on_device(tiles, subs, seeds, material, decay, coupling):
    f32 = jnp.float32
    padded = (3, 2, PAD + TX + PAD, TY)
    planes = len(ORDER)
    narrow, wide = pltpu.VMEM((2, planes, 16, TY), f32), pltpu.VMEM((2, planes, 48, TY), f32)
    hbm = pl.BlockSpec(memory_space=pltpu.HBM)
    done = pl.pallas_call(
        functools.partial(kernel, tiles, subs),
        out_shape=jax.ShapeDtypeStruct((planes, TX, TY), f32),
        in_specs=[hbm] * 4,
        out_specs=pl.BlockSpec(memory_space=pltpu.VMEM),
        scratch_shapes=[
            pltpu.SMEM(decay.shape, f32),
            pltpu.SMEM(coupling.shape, f32),
            pltpu.VMEM((6, *padded[1:]), f32),
            pltpu.VMEM((2, TX, TY), jnp.int32),
            pltpu.VMEM((2, TX, TY), f32),
            pltpu.VMEM((2, TX, TY), f32),
            *[pltpu.VMEM(padded, f32)] * 5,
            *[pltpu.VMEM((count, 1, *padded[2:]), f32) for count in (1, 2, 1)],
            *[pltpu.VMEM((count, TX, TY), f32) for count in (2, 3)] * 4,
            *[pltpu.VMEM((count, MOST, TY), f32) for count in (2, 3)],
            narrow, wide, narrow, narrow,
            narrow, wide, narrow, narrow,
            pltpu.SemaphoreType.DMA((5,)),
            pltpu.SemaphoreType.DMA((4,)),
            pltpu.SemaphoreType.DMA((4,)),
            pltpu.SemaphoreType.DMA((2 * PARTS,)),
            pltpu.SemaphoreType.DMA((2 * PARTS,)),
            pltpu.SemaphoreType.DMA((2,)),
            pltpu.SemaphoreType.DMA((2,)),
            pltpu.SemaphoreType.DMA((16,)),
            pltpu.SemaphoreType.DMA((16,)),
            pltpu.SemaphoreType.REGULAR((2,)),
        ],
        compiler_params=pltpu.CompilerParams(
            collective_id=0, has_side_effects=True, vmem_limit_bytes=20 * 2**20),
    )(*(pltpu.with_memory_space_constraint(array, pltpu.HBM) for array in (decay, coupling, seeds, material)))
    return done.reshape(seeds.shape)


def solution(mesh):
    placed = (P("tile", None, "sub", None, None), P("tile", "sub", None, None), P(), P())
    return jax.shard_map(
        functools.partial(on_device, mesh.shape["tile"], mesh.shape["sub"]),
        mesh=mesh,
        in_specs=placed,
        out_specs=P("tile", None, "sub", None, None),
        check_vma=False,
    )
```
